256 devices in a mesh: scan: 8 (over x, core), obj: 32 (over y, z).
Axes of the slice: x: 4, y: 4, z: 8, core: 2. Of those that a mesh axis runs over, the one named last changes fastest.
Arguments:
- object_slices: float32 [2, 2, 8192, 2048], P(None, None, 'obj'), may hold values from -4 to 4
- probe: float32 [2, 2, 256, 256], replicated, may hold values from -6 to 6
- measured: bfloat16 [8, 32, 2, 256, 256], P('scan', 'obj'), may hold values from 0 to 4
- positions: int32 [8, 32, 2, 2], P('scan', 'obj'), may hold values from 0 to 1792, as said below
- counts: int32 [8, 32], P('scan', 'obj'), may hold values from 0 to 2, as said below
Outputs:
- object_grad: float32 [2, 2, 8192, 2048], P(None, None, 'obj', 'scan')
- probe_grad: float32 [2, 2, 256, 256], P(None, None, 'obj', 'scan')
The draws below stay inside these ranges and needn't reach their ends.
Inputs may be any that keep to these rules, and one draw needn't show every extreme that they name: In every tile o the counts over the 8 batches sum to exactly 8, and some batch of every tile has 2 live patterns. `positions`: the row offset is below 256, the column at most 1792.
All inputs are finite; a program needn't handle non-finite values.
Results may differ from the reference program's by a relative error of at most 0.013.
Values may be sent and summed in bfloat16 or wider, within the bound.
A program may use at most 128 MiB of HBM per device.

```python
import math
import jax
import jax.numpy as jnp
from jax import lax

N = 256
M = 2
L = 2
R = 256
W = 2048
P_DEV = 2
H = 8192
LIVE = 256
N_SCAN = 8
N_OBJ = 32


def draw_positions(key, part):
    key_rows, key_cols = jax.random.split(jax.random.fold_in(key, 11))
    grid_shape = (N_SCAN, N_OBJ, P_DEV)
    row_vals = jax.random.randint(key_rows, grid_shape, 0, R)
    col_vals = jax.random.randint(key_cols, grid_shape, 0, W - N + 1)
    row_vals = row_vals.at[0, 0, 0].set(R - 1).at[0, 0, 1].set(0)
    col_vals = col_vals.at[0, 0, 0].set(W - N).at[0, 0, 1].set(0)
    return jnp.stack([row_vals, col_vals], axis=-1).astype(jnp.int32)


def draw_counts(key, part):
    key_pairs, key_perm = jax.random.split(jax.random.fold_in(key, 23))
    pair_count = N_SCAN // 2
    lower = jax.random.randint(key_pairs, (pair_count, N_OBJ), 0, P_DEV + 1)
    lower = lower.at[0].set(0)
    paired = jnp.stack([lower, P_DEV - lower], axis=1).reshape(N_SCAN, N_OBJ)
    perm_keys = jax.random.split(key_perm, N_OBJ)
    orders = jax.vmap(lambda one_key: jax.random.permutation(one_key, N_SCAN))(perm_keys)
    shuffled = jnp.take_along_axis(paired, orders.T.astype(jnp.int32), axis=0)
    return shuffled.astype(jnp.int32)


def shard_levels(rng, extent, pieces, smallest, largest):
    loudness, own = 1.0, jax.random.fold_in(rng, 6)
    for dim, blocks in pieces:
        steps = jnp.exp(jax.random.uniform(jax.random.fold_in(own, dim), (blocks,), jnp.float32, smallest / len(pieces), largest / len(pieces)))
        loudness = loudness * jnp.repeat(steps, extent[dim] // blocks).reshape([-1 if axis == dim else 1 for axis in range(len(extent))])
    return loudness


def bell_draw(key, shape, scale, most, cuts=(), kind=jnp.bfloat16):
    level = shard_levels(key, shape, cuts, -0.22, 0.18) if cuts else 1.0
    drawn = jax.random.normal(key, shape, jnp.float32) * scale * level
    return jnp.minimum(jnp.maximum(drawn, -most), most).astype(kind)


def setup_inputs(seed: int = 0) -> dict:
    key_list = jax.random.split(jax.random.key(seed), 6)
    object_slices = bell_draw(key_list[0], (L, 2, H, W), 0.7, 4.0, ((2, 32),), jnp.float32)
    probe = bell_draw(key_list[1], (M, 2, N, N), 1.0, 6.0, (), jnp.float32)
    measured = jnp.clip(4.0 * jax.random.uniform(key_list[2], (N_SCAN, N_OBJ, P_DEV, N, N), jnp.float32) ** shard_levels(key_list[2], (N_SCAN, N_OBJ, P_DEV, N, N), ((0, 8), (1, 32)), -0.2, 0.2), 0.0, 4.0).astype(jnp.bfloat16)
    positions = draw_positions(jax.random.fold_in(key_list[5], 71), 0)
    counts = draw_counts(jax.random.fold_in(key_list[5], 71), 0)
    return {"object_slices": object_slices, "probe": probe, "measured": measured, "positions": positions, "counts": counts}


HIGHEST_MODE = lax.Precision.HIGHEST

def dft_matrix(length, sign):
    index_row = jnp.arange(length, dtype=jnp.int32)
    product = index_row[:, None] * index_row[None, :] % length
    angles = product.astype(jnp.float32) * (2.0 * math.pi / length)
    factor = 1.0 / math.sqrt(length)
    real_part = jnp.cos(angles) * factor
    imag_part = sign * jnp.sin(angles) * factor
    stacked = jnp.stack([jnp.stack([real_part, -imag_part]), jnp.stack([imag_part, real_part])])
    return stacked.astype(jnp.bfloat16)

def fresnel_kernel(length):
    index_row = jnp.arange(length, dtype=jnp.int32)
    freqs = jnp.where(index_row < length // 2, index_row, index_row - length)
    squares = freqs * freqs
    summed = (squares[:, None] + squares[None, :]) % (4 * length)
    phases = summed.astype(jnp.float32) * (2.0 * math.pi / (4 * length))
    return jnp.stack([jnp.cos(phases), -jnp.sin(phases)])

def rounded(values):
    return lax.optimization_barrier(values.astype(jnp.bfloat16)).astype(jnp.float32)

def transform(field_in, matrix):
    weights = matrix.astype(jnp.float32)
    partial_out = jnp.einsum('pqab,qbc->pac', weights, rounded(field_in), precision=HIGHEST_MODE)
    return jnp.einsum('qab,pqbc->pac', rounded(partial_out), weights, precision=HIGHEST_MODE)

def complex_mul(first_op, second_op):
    return jnp.stack([first_op[0] * second_op[0] - first_op[1] * second_op[1], first_op[0] * second_op[1] + first_op[1] * second_op[0]])

def conj_mul(first_op, second_op):
    return jnp.stack([first_op[0] * second_op[0] + first_op[1] * second_op[1], first_op[0] * second_op[1] - first_op[1] * second_op[0]])

def pattern_terms(patches, probe, pattern_data, weight, forward, inverse, kernel):
    layers = patches.shape[0]

    def forward_mode(mode_probe):
        arrivals = [mode_probe]
        field_now = complex_mul(mode_probe, patches[0])
        for layer_idx in range(1, layers):
            spectrum = transform(field_now, forward)
            field_now = transform(complex_mul(kernel, spectrum), inverse)
            arrivals.append(field_now)
            field_now = complex_mul(field_now, patches[layer_idx])
        return (transform(field_now, forward), jnp.stack(arrivals))
    far_field, arrivals = jax.vmap(forward_mode)(probe)
    intensity = lax.optimization_barrier(jnp.sum(far_field[:, 0] ** 2 + far_field[:, 1] ** 2, axis=0))
    misfit = (intensity - pattern_data.astype(jnp.float32)) * weight

    def back_mode(mode_far, mode_arrivals):
        adjoint = transform(misfit[None] * mode_far, inverse)
        layer_grads = [None] * layers
        for layer_idx in reversed(range(layers)):
            layer_grads[layer_idx] = conj_mul(mode_arrivals[layer_idx], adjoint)
            adjoint = conj_mul(patches[layer_idx], adjoint)
            if layer_idx > 0:
                spectrum = transform(adjoint, forward)
                adjoint = transform(conj_mul(kernel, spectrum), inverse)
        return (jnp.stack(layer_grads), adjoint)
    patch_grads, probe_grads = jax.vmap(back_mode)(far_field, arrivals)
    return (lax.optimization_barrier(jnp.sum(patch_grads, axis=0)), probe_grads)

def reference(object_slices, probe, measured, positions, counts):
    forward = dft_matrix(N, -1.0)
    inverse = dft_matrix(N, 1.0)
    kernel = fresnel_kernel(N)
    extended = jnp.concatenate([object_slices, object_slices[:, :, :N]], axis=2)
    count_all = N_SCAN * N_OBJ * P_DEV
    flat_measured = measured.reshape(count_all, N, N)
    flat_positions = positions.reshape(count_all, 2)
    flat_counts = counts.reshape(N_SCAN * N_OBJ)
    zero_index = jnp.zeros((), jnp.int32)

    def step_fn(state_in, inputs):
        grad_ext, probe_sum = state_in
        pattern_id, pattern_data, pattern_pos = inputs
        group_id = pattern_id // P_DEV
        tile_id = group_id % N_OBJ
        slot_id = pattern_id % P_DEV
        weight = (slot_id < flat_counts[group_id]).astype(jnp.float32)
        row_start = (tile_id * R + pattern_pos[0]).astype(jnp.int32)
        col_start = pattern_pos[1].astype(jnp.int32)
        corner = (zero_index, zero_index, row_start, col_start)
        patches = lax.dynamic_slice(extended, corner, (L, 2, N, N))
        patch_grad, probe_grad = pattern_terms(patches, probe, pattern_data, weight, forward, inverse, kernel)
        current = lax.dynamic_slice(grad_ext, corner, (L, 2, N, N))
        grad_ext = lax.dynamic_update_slice(grad_ext, current + patch_grad, corner)
        return ((grad_ext, probe_sum + probe_grad), None)
    initial = (jnp.zeros((L, 2, H + N, W), jnp.float32), jnp.zeros(probe.shape, jnp.float32))
    pattern_ids = jnp.arange(count_all, dtype=jnp.int32)
    (grad_ext, probe_sum), leftover = lax.scan(step_fn, initial, (pattern_ids, flat_measured, flat_positions))
    object_grad = grad_ext[:, :, :H].at[:, :, :N].add(grad_ext[:, :, H:])
    return (object_grad, probe_sum * (1.0 / math.sqrt(LIVE)))
```

```python
import functools
import math

import jax
import jax.numpy as jnp
import numpy as np
from jax import lax
from jax.experimental import pallas as pl
from jax.experimental.pallas import tpu as pltpu
from jax.sharding import PartitionSpec as P

MESH = pl.DeviceIdType.MESH
BF = jnp.bfloat16
F32 = jnp.float32
N = 256
NS, NX, NO, NY, NZ = 8, 4, 32, 4, 8


def rem(a, b):
    return lax.rem(a, jnp.int32(b))


def tables():
    index = np.arange(N)
    angle = (np.outer(index, index) % N) * (2.0 * np.pi / N)
    rounded = lambda a: a.astype(np.float32).astype(BF)
    f_re, f_im = rounded(np.cos(angle) / 16.0), rounded(-np.sin(angle) / 16.0)
    fwd = f_re.astype(np.float64) + 1j * f_im.astype(np.float64)
    freq = np.where(index < N // 2, index, index - N)
    phase = np.exp(-2j * np.pi * ((freq * freq) % (4 * N)) / (4 * N))
    prop = np.conj(fwd) @ (phase[:, None] * fwd)
    return np.stack([f_re, f_im, rounded(prop.real), rounded(prop.imag)])


def remote(src, dst, send, recv, device):
    return pltpu.make_async_remote_copy(
        src_ref=src, dst_ref=dst, send_sem=send, recv_sem=recv, device_id=device, device_id_type=MESH
    )


def table_kernel(pos_ref, count_ref, out_ref, row_ref, tab_ref, send, recv):
    s, o = lax.axis_index("scan"), lax.axis_index("obj")
    up, down = rem(o + 1, NO), rem(o + NO - 1, NO)
    barrier = pltpu.get_barrier_semaphore()
    for k in range(NS):
        if k:
            pl.semaphore_signal(barrier, inc=1, device_id=(rem(s + k, NS), o), device_id_type=MESH)
        pl.semaphore_signal(barrier, inc=1, device_id=(rem(s + k, NS), down), device_id_type=MESH)
    lane = lax.broadcasted_iota(jnp.int32, (1, 128), 1)
    row = jnp.zeros((1, 128), jnp.int32)
    for j, value in enumerate((pos_ref[0, 0], pos_ref[0, 1], pos_ref[1, 0], pos_ref[1, 1], count_ref[0, 0])):
        row = jnp.where(lane == j, value, row)
    row_ref[...] = row
    tab_ref[s] = row
    pl.semaphore_wait(barrier, 2 * NS - 1)
    copies = []
    for k in range(NS):
        peer = rem(s + k, NS)
        source = rem(s + NS - k, NS)
        if k:
            copy = remote(row_ref, tab_ref.at[s], send.at[k], recv.at[k], (peer, o))
            copy.start()
            copies.append((copy, remote(row_ref, tab_ref.at[source], send.at[k], recv.at[k], (peer, o))))
        copy = remote(row_ref, tab_ref.at[NS + s], send.at[NS + k], recv.at[NS + k], (peer, up))
        copy.start()
        copies.append((copy, remote(row_ref, tab_ref.at[NS + source], send.at[NS + k], recv.at[NS + k], (peer, up))))
    for sent, landed in copies:
        sent.wait_send()
        landed.wait_recv()
    out_ref[...] = tab_ref[...]


def main_kernel(
    tab, tile_hbm, probe_hbm, meas_hbm, table_hbm, out_ref, pout_ref,
    tile_0, tile_1, probe, meas, tabs, e_f, e_i, e_h, e_c, hsend, hrecv, local, pattern, win, v, u, arr, far, cur,
    gsend, wins, acc, tsend, trecv, bsend, brecv, esend, erecv, ysend, yrecv, zsend, zrecv, xsend, xrecv,
    dma, send, recv,
):
    s, o = lax.axis_index("scan"), lax.axis_index("obj")
    x, core = lax.div(s, jnp.int32(2)), rem(s, 2)
    y, z = lax.div(o, jnp.int32(NZ)), rem(o, NZ)
    other = 1 - core
    partner = 2 * x + other
    right = [2 * rem(x + 1, NX) + c for c in range(2)]
    left = [2 * rem(x + 3, NX) + c for c in range(2)]
    right_me, left_me = 2 * rem(x + 1, NX) + core, 2 * rem(x + 3, NX) + core
    far_me, left_ot, right_ot, far_ot = (
        2 * rem(x + 2, NX) + core, 2 * rem(x + 3, NX) + other, 2 * rem(x + 1, NX) + other, 2 * rem(x + 2, NX) + other
    )
    far_at = [2 * rem(x + 2, NX) + c for c in range(2)]
    up, down = rem(o + 1, NO), rem(o + NO - 1, NO)
    tile = (tile_0, tile_1)
    sends = []

    loads = [
        pltpu.make_async_copy(table_hbm, tabs, dma.at[0]),
        pltpu.make_async_copy(probe_hbm, probe, dma.at[1]),
        pltpu.make_async_copy(meas_hbm, meas.at[pl.ds(2 * s, 2)], dma.at[2]),
    ]
    for layer in range(2):
        for b in range(NS):
            block = tile_hbm.at[layer, :, :, pl.ds(b * N, N)]
            loads.append(pltpu.make_async_copy(block, tile[layer].at[b], dma.at[3 + NS * layer + b]))
    for load in loads:
        load.start()

    barrier = pltpu.get_barrier_semaphore()
    peers = [(rem(s + k, NS), o) for k in range(1, NS)]
    peers += [(s, up), (s, down), (partner, down)]
    peers += [(s, rem(y + k, NY) * NZ + z) for k in range(1, NY)]
    peers += [(s, y * NZ + rem(z + k, NZ)) for k in range(1, NZ)]
    for peer in peers:
        pl.semaphore_signal(barrier, inc=1, device_id=peer, device_id_type=MESH)

    def assigned(base, n):
        start, found = jnp.int32(0), [jnp.int32(0)] * 3
        for t in range(NS):
            count = tab[base + t, 0, 4]
            for k in range(2):
                hit = (k < count) & (start + k == n)
                for j, value in enumerate((jnp.int32(2 * t + k), tab[base + t, 0, 2 * k], tab[base + t, 0, 2 * k + 1])):
                    found[j] = jnp.where(hit, value, found[j])
            start = start + count
        return found

    places = [assigned(0, n) for n in range(NS)]
    source, row0, col0 = places[0]
    for n in range(1, NS):
        source, row0, col0 = (jnp.where(s == n, a, b) for a, b in zip(places[n], (source, row0, col0)))
    _, _, col_prev = assigned(NS, s)

    loads[0].wait()
    for e_ref, re, im, sign in ((e_f, 0, 1, 1), (e_i, 0, 1, -1), (e_h, 2, 3, 1), (e_c, 2, 3, -1)):
        e_ref[0:N, 0:N] = tabs[re]
        e_ref[N:, N:] = tabs[re]
        e_ref[0:N, N:] = -tabs[im] if sign > 0 else tabs[im]
        e_ref[N:, 0:N] = tabs[im] if sign > 0 else -tabs[im]

    def one_hot(shape, rule):
        a, b = lax.broadcasted_iota(jnp.int32, shape, 0), lax.broadcasted_iota(jnp.int32, shape, 1)
        return jnp.where(rule(a, b), 1.0, 0.0).astype(BF)

    def dot(a, b):
        return jnp.dot(a, b, preferred_element_type=F32)

    def col_block(col):
        k = jnp.int32(0)
        for edge in range(1, NS - 1):
            k = k + jnp.where(col >= edge * N, 1, 0)
        return k

    def picks(offset):
        return [one_hot((N, N), lambda a, b: a + h * N == b + offset) for h in range(2)]

    def columns(layer, part, k, pick):
        first, second = tile[layer][k, part].astype(BF), tile[layer][k + 1, part].astype(BF)
        return (dot(first, pick[0]) + dot(second, pick[1])).astype(BF)

    k_prev, k_own = col_block(col_prev), col_block(col0)
    pick_prev = picks(col_prev - k_prev * N)

    pl.semaphore_wait(barrier, len(peers))

    def start(copy):
        copy.start()
        sends.append(copy)

    def meas_copy(q, slot, n, peer):
        ref = meas.at[pl.ds(slot, n)]
        return remote(ref, ref, send.at[q], recv.at[q], (peer, o))

    for q, peer in ((0, partner), (1, right_me), (2, left_me)):
        start(remote(meas_hbm, meas.at[pl.ds(2 * s, 2)], send.at[q], recv.at[q], (peer, o)))

    def halo_copy(layer):
        return remote(hsend.at[layer], hrecv.at[layer], send.at[9 + layer], recv.at[9 + layer], (s, down))

    for layer in range(2):
        for b in range(NS):
            loads[3 + NS * layer + b].wait()
        for part in range(2):
            hsend[layer, part] = columns(layer, part, k_prev, pick_prev)
        start(halo_copy(layer))
    pick_own = picks(col0 - k_own * N)
    for layer in range(2):
        for part in range(2):
            local[layer, part] = columns(layer, part, k_own, pick_own)
    rows_here = one_hot((N, N), lambda a, b: b == a + row0)
    rows_next = one_hot((N, N), lambda a, b: b + N == a + row0)
    turn = jnp.where(col0 == 7 * N, 0, col0 - k_own * N)
    turn_rows = one_hot((N, N), lambda a, b: (b + row0 == a) | (b + row0 == a + N))
    turn_cols = one_hot((N, N), lambda a, b: (a + turn == b) | (a + turn == b + N))
    loads[1].wait()

    def window(layer):
        halo_copy(layer).wait_recv()
        for part in range(2):
            win[layer, part] = dot(rows_here, local[layer, part]) + dot(rows_next, hrecv[layer, part])

    step = 32

    def by_rows(body):
        def run(i, carry):
            body(pl.ds(pl.multiple_of(i * step, step), step), i)
            return carry

        lax.fori_loop(0, N // step, run, 0)

    def put(m, rows, i, re, im):
        v[pl.ds(pl.multiple_of(i * step, step), step), m * N : (m + 1) * N] = re.astype(BF)
        v[pl.ds(pl.multiple_of(N + i * step, step), step), m * N : (m + 1) * N] = im.astype(BF)

    def left_mul(matrix):
        for m in range(2):
            product = dot(matrix[...], v[:, m * N : (m + 1) * N])
            u[m * N : (m + 1) * N, 0:N] = product[0:N].astype(BF)
            u[m * N : (m + 1) * N, N:] = product[N:].astype(BF)

    def right_mul(matrix, result):
        for part in range(2):
            product = dot(u[...], matrix[:, part * N : (part + 1) * N])
            result[0, part] = product[0:N]
            result[1, part] = product[N:]

    window(0)

    def enter(rows, i):
        re, im = win[0, 0, rows, :], win[0, 1, rows, :]
        for m in range(2):
            pr, pi = probe[m, 0, rows, :], probe[m, 1, rows, :]
            put(m, rows, i, pr * re - pi * im, pr * im + pi * re)

    by_rows(enter)
    left_mul(e_h)
    meas_copy(1, 2 * left_me, 2, right_me).wait_recv()
    start(meas_copy(3, 2 * left_me, 1, right_me))
    start(meas_copy(4, 2 * left_me, 2, partner))
    meas_copy(2, 2 * right_me, 2, left_me).wait_recv()
    start(meas_copy(5, 2 * right_me + 1, 1, left_me))
    start(meas_copy(6, 2 * right_me, 2, partner))
    right_mul(e_c, arr)
    window(1)

    def second(rows, i):
        re, im = win[1, 0, rows, :], win[1, 1, rows, :]
        for m in range(2):
            pr, pi = arr[m, 0, rows, :], arr[m, 1, rows, :]
            put(m, rows, i, pr * re - pi * im, pr * im + pi * re)

    by_rows(second)
    meas_copy(3, 2 * far_me, 1, right_me).wait_recv()
    start(meas_copy(7, 2 * far_me, 1, partner))
    meas_copy(5, 2 * far_me + 1, 1, left_me).wait_recv()
    start(meas_copy(8, 2 * far_me + 1, 1, partner))
    left_mul(e_f)
    right_mul(e_i, far)
    loads[2].wait()
    meas_copy(0, 2 * partner, 2, partner).wait_recv()
    meas_copy(4, 2 * left_ot, 2, partner).wait_recv()
    meas_copy(6, 2 * right_ot, 2, partner).wait_recv()
    meas_copy(7, 2 * far_ot, 1, partner).wait_recv()
    meas_copy(8, 2 * far_ot + 1, 1, partner).wait_recv()

    pattern[...] = meas[source]

    def misfit(rows, i):
        parts = [(far[m, 0, rows, :], far[m, 1, rows, :]) for m in range(2)]
        total = parts[0][0] ** 2 + parts[0][1] ** 2 + (parts[1][0] ** 2 + parts[1][1] ** 2)
        gap = total - pattern[rows, :].astype(F32)
        for m in range(2):
            put(m, rows, i, gap * parts[m][0], gap * parts[m][1])

    by_rows(misfit)
    left_mul(e_i)
    right_mul(e_f, cur)

    def near(layer, c, side):
        q = 11 + 18 * layer + (2 if side else 4)
        peer = (right if side else left)[c]
        return remote(
            gsend.at[layer, c], wins.at[layer, s], send.at[q + c], recv.at[q + core], (peer, o)
        )

    def near_in(layer, c, side):
        q = 11 + 18 * layer + (2 if side else 4)
        slot = wins.at[layer, (left if side else right)[c]]
        return remote(slot, slot, send.at[q + c], recv.at[q + c], (partner, o))

    def relay(layer, c, side, incoming=False):
        q = 11 + 18 * layer + (6 if side else 8) + c
        owner = far_at[c] if incoming else (left if side else right)[c]
        half = wins.at[layer, owner, pl.ds(0 if side else N // 2, N // 2)]
        return remote(half, half, send.at[q], recv.at[q], (right_me if side else left_me, o))

    def pair(layer, incoming=False):
        q = 11 + 18 * layer
        slot = wins.at[layer, partner if incoming else s]
        return remote(gsend.at[layer, other], slot, send.at[q], recv.at[q], (partner, o))

    def share(layer, first, adjoint):
        for part in range(2):
            if part == 0:
                term = lambda m: first[m, 0] * adjoint[m, 0] + first[m, 1] * adjoint[m, 1]
            else:
                term = lambda m: first[m, 0] * adjoint[m, 1] - first[m, 1] * adjoint[m, 0]
            grad = (term(0) + term(1)).astype(BF)
            gsend[layer, part] = dot(dot(turn_rows, grad).astype(BF), turn_cols).astype(BF)
        start(pair(layer))
        for c in range(2):
            start(near(layer, c, 1))
            start(near(layer, c, 0))
        wins[layer, s] = gsend[layer, core]

    def pass_on(layer):
        for side in (1, 0):
            for c in range(2):
                near_in(layer, c, side).wait_recv()
                start(relay(layer, c, side))

    share(1, arr, cur)

    def behind(rows, i):
        re, im = win[1, 0, rows, :], win[1, 1, rows, :]
        for m in range(2):
            cr, ci = cur[m, 0, rows, :], cur[m, 1, rows, :]
            put(m, rows, i, re * cr + im * ci, re * ci - im * cr)

    by_rows(behind)
    left_mul(e_c)
    right_mul(e_h, cur)
    share(0, probe, cur)

    def leave(rows, i):
        re, im = win[0, 0, rows, :], win[0, 1, rows, :]
        for m in range(2):
            cr, ci = cur[m, 0, rows, :], cur[m, 1, rows, :]
            esend[m, 0, rows, :] = (re * cr + im * ci).astype(BF)
            esend[m, 1, rows, :] = (re * ci - im * cr).astype(BF)

    by_rows(leave)
    q_pair, q_y, q_z, q_x = 53, 54, 57, 64
    e_copy = remote(esend.at[other], erecv, send.at[q_pair], recv.at[q_pair], (partner, o))
    start(e_copy)
    pass_on(1)
    e_copy.wait_recv()

    def add_pair(rows, i):
        for part in range(2):
            ysend[part, rows, :] = (esend[core, part, rows, :].astype(F32) + erecv[part, rows, :].astype(F32)).astype(BF)

    by_rows(add_pair)
    deep = N // NY
    y_copies = []
    for k in range(1, NY):
        y_to = rem(y + k, NY)
        rows_to = pl.ds(pl.multiple_of(y_to * deep, deep), deep)
        copy = remote(
            ysend.at[:, rows_to, :], yrecv.at[k - 1], send.at[q_y + k - 1], recv.at[q_y + k - 1], (s, y_to * NZ + z)
        )
        start(copy)
        y_copies.append(copy)

    lane = lax.broadcasted_iota(jnp.int32, (1, N), 1)

    def gather(layer):
        chunk = 16
        cols = [[(lane + (2 * x + b) * N >= c0) & (lane + (2 * x + b) * N < c0 + N) for b in range(2)] for _, _, c0 in places]
        cols = [[jnp.where(mask, 1.0, 0.0).astype(F32) for mask in pair_masks] for pair_masks in cols]

        def run(i, carry):
            rows = pl.ds(pl.multiple_of(i * chunk, chunk), chunk)
            line = lax.broadcasted_iota(jnp.int32, (chunk, N), 0) + i * chunk
            sums = [[jnp.zeros((chunk, N), F32) for _ in range(2)] for _ in range(2)]
            for n in range(NS):
                term = wins[layer, n, rows, :].astype(F32)
                above = line >= places[n][1]
                for b in range(2):
                    masked = term * cols[n][b]
                    sums[b][0] = sums[b][0] + jnp.where(above, masked, 0.0)
                    sums[b][1] = sums[b][1] + jnp.where(above, 0.0, masked)
            mine = core == 0
            acc[layer, rows, :] = jnp.where(mine, sums[0][0], sums[1][0])
            tsend[layer, rows, :] = jnp.where(mine, sums[1][0], sums[0][0]).astype(BF)
            for b in range(2):
                bsend[layer, b, rows, :] = sums[b][1].astype(BF)
            return carry

        lax.fori_loop(0, N // chunk, run, 0)

    def top_copy(layer):
        q = 71 + layer
        return remote(tsend.at[layer], trecv.at[layer], send.at[q], recv.at[q], (partner, o))

    def bottom_copy(layer, b):
        q = 73 + 2 * layer
        return remote(bsend.at[layer, b], brecv.at[layer, core], send.at[q + b], recv.at[q + core], (2 * x + b, up))

    def bottom_in(layer, c):
        q = 73 + 2 * layer
        return remote(bsend.at[layer, c], brecv.at[layer, c], send.at[q + c], recv.at[q + c], (s, up))

    def collect(layer):
        pair(layer, True).wait_recv()
        for side in (1, 0):
            for c in range(2):
                relay(layer, c, side, True).wait_recv()
        gather(layer)
        for b in range(2):
            start(bottom_copy(layer, b))
        start(top_copy(layer))

    def finish(layer):
        top_copy(layer).wait_recv()
        for c in range(2):
            bottom_in(layer, c).wait_recv()
        for i in range(N // 64):
            rows = pl.ds(i * 64, 64)
            out_ref[layer, core, rows, :] = acc[layer, rows, :] + brecv[layer, core, rows, :].astype(F32)
            out_ref[layer, other, rows, :] = (
                trecv[layer, rows, :].astype(F32) + brecv[layer, other, rows, :].astype(F32)
            )

    collect(1)
    for copy in y_copies:
        copy.wait_recv()
    rows_me = pl.ds(pl.multiple_of(y * deep, deep), deep)
    for part in range(2):
        total = ysend[part, rows_me, :].astype(F32)
        for k in range(NY - 1):
            total = total + yrecv[k, part].astype(F32)
        zsend[part] = total
    z_copies = []
    for k in range(1, NZ):
        z_to = rem(z + k, NZ)
        copy = remote(
            zsend.at[:, pl.ds(pl.multiple_of(z_to * 8, 8), 8), :], zrecv.at[k - 1],
            send.at[q_z + k - 1], recv.at[q_z + k - 1], (s, y * NZ + z_to),
        )
        start(copy)
        z_copies.append(copy)
    pass_on(0)
    for copy in z_copies:
        copy.wait_recv()
    for part in range(2):
        total = zsend[part, pl.ds(pl.multiple_of(z * 8, 8), 8), :]
        for k in range(NZ - 1):
            total = total + zrecv[k, part]
        xsend[part] = total
    x_copies = []
    for k in range(1, NS):
        copy = remote(xsend, xrecv.at[k - 1], send.at[q_x + k - 1], recv.at[q_x + k - 1], (rem(s + k, NS), o))
        start(copy)
        x_copies.append(copy)
    collect(0)
    for copy in x_copies:
        copy.wait_recv()
    factor = 1.0 / math.sqrt(256.0)
    mine, theirs = xsend[...], xrecv[0]
    for k in range(2, NS):
        if k % 2:
            theirs = theirs + xrecv[k - 1]
        else:
            mine = mine + xrecv[k - 1]
    pout_ref[core] = mine * factor
    pout_ref[other] = theirs * factor
    finish(1)
    finish(0)
    for copy in sends:
        copy.wait_send()


def body(object_slices, probe, measured, positions, counts):
    table = pl.pallas_call(
        table_kernel,
        out_shape=jax.ShapeDtypeStruct((2 * NS, 1, 128), jnp.int32),
        in_specs=[pl.BlockSpec(memory_space=pltpu.SMEM)] * 2,
        out_specs=pl.BlockSpec(memory_space=pltpu.VMEM),
        scratch_shapes=[
            pltpu.VMEM((1, 128), jnp.int32),
            pltpu.VMEM((2 * NS, 1, 128), jnp.int32),
            pltpu.SemaphoreType.DMA((2 * NS,)),
            pltpu.SemaphoreType.DMA((2 * NS,)),
        ],
        compiler_params=pltpu.CompilerParams(collective_id=0, has_side_effects=True),
        name="places",
    )(positions[0, 0], counts)

    vmem = pltpu.VMEM
    square = lambda *lead: (*lead, N, N)
    any_spec = pl.BlockSpec(memory_space=pl.ANY)
    object_grad, probe_rows = pl.pallas_call(
        main_kernel,
        out_shape=(
            jax.ShapeDtypeStruct(square(2, 2), F32),
            jax.ShapeDtypeStruct((2, 2, 8, N), F32),
        ),
        in_specs=[pl.BlockSpec(memory_space=pltpu.SMEM), any_spec, any_spec, any_spec, any_spec],
        out_specs=(pl.BlockSpec(memory_space=vmem), pl.BlockSpec(memory_space=vmem)),
        scratch_shapes=[
            *[vmem(square(NS, 2), F32)] * 2,
            vmem(square(2, 2), F32),
            vmem(square(16), BF),
            vmem(square(4), BF),
            *[vmem((2 * N, 2 * N), BF)] * 4,
            vmem(square(2, 2), BF),
            vmem(square(2, 2), BF),
            vmem(square(2, 2), BF),
            vmem(square(), BF),
            vmem(square(2, 2), F32),
            vmem((2 * N, 2 * N), BF),
            vmem((2 * N, 2 * N), BF),
            vmem(square(2, 2), F32),
            vmem(square(2, 2), F32),
            vmem(square(2, 2), F32),
            vmem(square(2, 2), BF),
            vmem(square(2, NS), BF),
            vmem(square(2), F32),
            vmem(square(2), BF),
            vmem(square(2), BF),
            vmem(square(2, 2), BF),
            vmem(square(2, 2), BF),
            vmem(square(2, 2), BF),
            vmem(square(2), BF),
            vmem(square(2), BF),
            vmem((NY - 1, 2, N // NY, N), BF),
            vmem((2, N // NY, N), F32),
            vmem((NZ - 1, 2, 8, N), F32),
            vmem((2, 8, N), F32),
            vmem((NS - 1, 2, 8, N), F32),
            pltpu.SemaphoreType.DMA((3 + 2 * NS,)),
            pltpu.SemaphoreType.DMA((77,)),
            pltpu.SemaphoreType.DMA((77,)),
        ],
        compiler_params=pltpu.CompilerParams(
            collective_id=1, has_side_effects=True, vmem_limit_bytes=60 * 1024 * 1024
        ),
        name="gradient",
    )(table, object_slices, probe, measured[0, 0], tables())
    cols = lax.axis_index("scan") * 32
    return object_grad, lax.dynamic_slice_in_dim(probe_rows, cols, 32, axis=3)


def solution(mesh):
    return jax.shard_map(
        body,
        mesh=mesh,
        in_specs=(
            P(None, None, "obj", None),
            P(),
            P("scan", "obj", None, None, None),
            P("scan", "obj", None, None),
            P("scan", "obj"),
        ),
        out_specs=(P(None, None, "obj", "scan"), P(None, None, "obj", "scan")),
        check_vma=False,
    )
```

```python
import functools
import math

import jax
import jax.numpy as jnp
import numpy as np
from jax import lax
from jax.experimental import pallas as pl
from jax.experimental.pallas import tpu as pltpu
from jax.sharding import PartitionSpec as P

MESH = pl.DeviceIdType.MESH
BF = jnp.bfloat16
F32 = jnp.float32
N = 256
NS, NX, NO, NY, NZ = 8, 4, 32, 4, 8


def rem(a, b):
    return lax.rem(a, jnp.int32(b))


def tables():
    index = np.arange(N)
    angle = (np.outer(index, index) % N) * (2.0 * np.pi / N)
    rounded = lambda a: a.astype(np.float32).astype(BF)
    f_re, f_im = rounded(np.cos(angle) / 16.0), rounded(-np.sin(angle) / 16.0)
    fwd = f_re.astype(np.float64) + 1j * f_im.astype(np.float64)
    freq = np.where(index < N // 2, index, index - N)
    phase = np.exp(-2j * np.pi * ((freq * freq) % (4 * N)) / (4 * N))
    prop = np.conj(fwd) @ (phase[:, None] * fwd)
    return np.stack([f_re, f_im, rounded(prop.real), rounded(prop.imag)])


def remote(src, dst, send, recv, device):
    return pltpu.make_async_remote_copy(
        src_ref=src, dst_ref=dst, send_sem=send, recv_sem=recv, device_id=device, device_id_type=MESH
    )


def main_kernel(
    pos_ref, count_ref, tile_hbm, probe_hbm, meas_hbm, table_hbm, out_ref, pout_ref,
    row, rows_in, tab, tile_0, tile_1, probe, meas, tabs, e_f, e_i, e_h, e_c, hsend, hrecv, local, pattern, win, v, u, arr, far, cur,
    gsend, wins, acc, tsend, trecv, bsend, brecv, esend, erecv, ysend, yrecv, zsend, zrecv, xsend, xrecv,
    dma, send, recv,
):
    s, o = lax.axis_index("scan"), lax.axis_index("obj")
    x, core = lax.div(s, jnp.int32(2)), rem(s, 2)
    y, z = lax.div(o, jnp.int32(NZ)), rem(o, NZ)
    other = 1 - core
    partner = 2 * x + other
    right = [2 * rem(x + 1, NX) + c for c in range(2)]
    left = [2 * rem(x + 3, NX) + c for c in range(2)]
    right_me, left_me = 2 * rem(x + 1, NX) + core, 2 * rem(x + 3, NX) + core
    far_me, left_ot, right_ot, far_ot = (
        2 * rem(x + 2, NX) + core, 2 * rem(x + 3, NX) + other, 2 * rem(x + 1, NX) + other, 2 * rem(x + 2, NX) + other
    )
    far_at = [2 * rem(x + 2, NX) + c for c in range(2)]
    up, down = rem(o + 1, NO), rem(o + NO - 1, NO)
    tile = (tile_0, tile_1)
    sends = []

    loads = [
        pltpu.make_async_copy(table_hbm, tabs, dma.at[0]),
        pltpu.make_async_copy(probe_hbm, probe, dma.at[1]),
        pltpu.make_async_copy(meas_hbm, meas.at[pl.ds(2 * s, 2)], dma.at[2]),
    ]
    for layer in range(2):
        for b in range(NS):
            block = tile_hbm.at[layer, :, :, pl.ds(b * N, N)]
            loads.append(pltpu.make_async_copy(block, tile[layer].at[b], dma.at[3 + NS * layer + b]))
    for load in loads:
        load.start()

    barrier = pltpu.get_barrier_semaphore()
    peers = [(rem(s + k, NS), o) for k in range(1, NS)]
    peers += [(s, up)] + [(rem(s + k, NS), down) for k in range(NS)]
    peers += [(s, rem(y + k, NY) * NZ + z) for k in range(1, NY)]
    peers += [(s, y * NZ + rem(z + k, NZ)) for k in range(1, NZ)]
    for peer in peers:
        pl.semaphore_signal(barrier, inc=1, device_id=peer, device_id_type=MESH)

    lane = lax.broadcasted_iota(jnp.int32, (1, 128), 1)
    line = jnp.zeros((1, 128), jnp.int32)
    for j, value in enumerate((pos_ref[0, 0], pos_ref[0, 1], pos_ref[1, 0], pos_ref[1, 1], count_ref[0, 0])):
        line = jnp.where(lane == j, value, line)
    row[...] = line
    rows_in[s] = line

    loads[0].wait()
    for e_ref, re, im, sign in ((e_f, 0, 1, 1), (e_i, 0, 1, -1), (e_h, 2, 3, 1), (e_c, 2, 3, -1)):
        e_ref[0:N, 0:N] = tabs[re]
        e_ref[N:, N:] = tabs[re]
        e_ref[0:N, N:] = -tabs[im] if sign > 0 else tabs[im]
        e_ref[N:, 0:N] = tabs[im] if sign > 0 else -tabs[im]

    def one_hot(shape, rule):
        a, b = lax.broadcasted_iota(jnp.int32, shape, 0), lax.broadcasted_iota(jnp.int32, shape, 1)
        return jnp.where(rule(a, b), 1.0, 0.0).astype(BF)

    def dot(a, b):
        return jnp.dot(a, b, preferred_element_type=F32)

    def col_block(col):
        k = jnp.int32(0)
        for edge in range(1, NS - 1):
            k = k + jnp.where(col >= edge * N, 1, 0)
        return k

    def picks(offset):
        return [one_hot((N, N), lambda a, b: a + h * N == b + offset) for h in range(2)]

    def columns(layer, part, k, pick):
        first, second = tile[layer][k, part].astype(BF), tile[layer][k + 1, part].astype(BF)
        return (dot(first, pick[0]) + dot(second, pick[1])).astype(BF)


    pl.semaphore_wait(barrier, len(peers))

    def start(copy):
        copy.start()
        sends.append(copy)

    def meas_copy(q, slot, n, peer):
        ref = meas.at[pl.ds(slot, n)]
        return remote(ref, ref, send.at[q], recv.at[q], (peer, o))

    def place_copy(k, base, owner):
        peer = (rem(s + k, NS), up if base else o)
        return remote(row, rows_in.at[base + owner], send.at[77 + base + k], recv.at[77 + base + k], peer)

    every = [(k, base) for base in (0, NS) for k in range(NS) if base or k]
    for k, base in every:
        start(place_copy(k, base, s))
    for q, peer in ((0, partner), (1, right_me), (2, left_me)):
        start(remote(meas_hbm, meas.at[pl.ds(2 * s, 2)], send.at[q], recv.at[q], (peer, o)))

    for k, base in every:
        place_copy(k, base, rem(s + NS - k, NS)).wait_recv()
    fetch = pltpu.make_async_copy(rows_in, tab, dma.at[3 + 2 * NS])
    fetch.start()
    fetch.wait()

    def assigned(base, n):
        start, found = jnp.int32(0), [jnp.int32(0)] * 3
        for t in range(NS):
            count = tab[base + t, 0, 4]
            for k in range(2):
                hit = (k < count) & (start + k == n)
                for j, value in enumerate((jnp.int32(2 * t + k), tab[base + t, 0, 2 * k], tab[base + t, 0, 2 * k + 1])):
                    found[j] = jnp.where(hit, value, found[j])
            start = start + count
        return found

    places = [assigned(0, n) for n in range(NS)]
    source, row0, col0 = places[0]
    for n in range(1, NS):
        source, row0, col0 = (jnp.where(s == n, a, b) for a, b in zip(places[n], (source, row0, col0)))
    _, _, col_prev = assigned(NS, s)

    k_prev, k_own = col_block(col_prev), col_block(col0)
    pick_prev = picks(col_prev - k_prev * N)

    def halo_copy(layer):
        return remote(hsend.at[layer], hrecv.at[layer], send.at[9 + layer], recv.at[9 + layer], (s, down))

    for layer in range(2):
        for b in range(NS):
            loads[3 + NS * layer + b].wait()
        for part in range(2):
            hsend[layer, part] = columns(layer, part, k_prev, pick_prev)
        start(halo_copy(layer))
    pick_own = picks(col0 - k_own * N)
    for layer in range(2):
        for part in range(2):
            local[layer, part] = columns(layer, part, k_own, pick_own)
    rows_here = one_hot((N, N), lambda a, b: b == a + row0)
    rows_next = one_hot((N, N), lambda a, b: b + N == a + row0)
    turn = jnp.where(col0 == 7 * N, 0, col0 - k_own * N)
    turn_rows = one_hot((N, N), lambda a, b: (b + row0 == a) | (b + row0 == a + N))
    turn_cols = one_hot((N, N), lambda a, b: (a + turn == b) | (a + turn == b + N))
    loads[1].wait()

    def window(layer):
        halo_copy(layer).wait_recv()
        for part in range(2):
            win[layer, part] = dot(rows_here, local[layer, part]) + dot(rows_next, hrecv[layer, part])

    step = 32

    def by_rows(body):
        def run(i, carry):
            body(pl.ds(pl.multiple_of(i * step, step), step), i)
            return carry

        lax.fori_loop(0, N // step, run, 0)

    def put(m, rows, i, re, im):
        v[pl.ds(pl.multiple_of(i * step, step), step), m * N : (m + 1) * N] = re.astype(BF)
        v[pl.ds(pl.multiple_of(N + i * step, step), step), m * N : (m + 1) * N] = im.astype(BF)

    def left_mul(matrix):
        for m in range(2):
            product = dot(matrix[...], v[:, m * N : (m + 1) * N])
            u[m * N : (m + 1) * N, 0:N] = product[0:N].astype(BF)
            u[m * N : (m + 1) * N, N:] = product[N:].astype(BF)

    def right_mul(matrix, result):
        for part in range(2):
            product = dot(u[...], matrix[:, part * N : (part + 1) * N])
            result[0, part] = product[0:N]
            result[1, part] = product[N:]

    window(0)

    def enter(rows, i):
        re, im = win[0, 0, rows, :], win[0, 1, rows, :]
        for m in range(2):
            pr, pi = probe[m, 0, rows, :], probe[m, 1, rows, :]
            put(m, rows, i, pr * re - pi * im, pr * im + pi * re)

    by_rows(enter)
    left_mul(e_h)
    meas_copy(1, 2 * left_me, 2, right_me).wait_recv()
    start(meas_copy(3, 2 * left_me, 1, right_me))
    start(meas_copy(4, 2 * left_me, 2, partner))
    meas_copy(2, 2 * right_me, 2, left_me).wait_recv()
    start(meas_copy(5, 2 * right_me + 1, 1, left_me))
    start(meas_copy(6, 2 * right_me, 2, partner))
    right_mul(e_c, arr)
    window(1)

    def second(rows, i):
        re, im = win[1, 0, rows, :], win[1, 1, rows, :]
        for m in range(2):
            pr, pi = arr[m, 0, rows, :], arr[m, 1, rows, :]
            put(m, rows, i, pr * re - pi * im, pr * im + pi * re)

    by_rows(second)
    meas_copy(3, 2 * far_me, 1, right_me).wait_recv()
    start(meas_copy(7, 2 * far_me, 1, partner))
    meas_copy(5, 2 * far_me + 1, 1, left_me).wait_recv()
    start(meas_copy(8, 2 * far_me + 1, 1, partner))
    left_mul(e_f)
    right_mul(e_i, far)
    loads[2].wait()
    meas_copy(0, 2 * partner, 2, partner).wait_recv()
    meas_copy(4, 2 * left_ot, 2, partner).wait_recv()
    meas_copy(6, 2 * right_ot, 2, partner).wait_recv()
    meas_copy(7, 2 * far_ot, 1, partner).wait_recv()
    meas_copy(8, 2 * far_ot + 1, 1, partner).wait_recv()

    pattern[...] = meas[source]

    def misfit(rows, i):
        parts = [(far[m, 0, rows, :], far[m, 1, rows, :]) for m in range(2)]
        total = parts[0][0] ** 2 + parts[0][1] ** 2 + (parts[1][0] ** 2 + parts[1][1] ** 2)
        gap = total - pattern[rows, :].astype(F32)
        for m in range(2):
            put(m, rows, i, gap * parts[m][0], gap * parts[m][1])

    by_rows(misfit)
    left_mul(e_i)
    right_mul(e_f, cur)

    def near(layer, c, side):
        q = 11 + 18 * layer + (2 if side else 4)
        peer = (right if side else left)[c]
        return remote(
            gsend.at[layer, c], wins.at[layer, s], send.at[q + c], recv.at[q + core], (peer, o)
        )

    def near_in(layer, c, side):
        q = 11 + 18 * layer + (2 if side else 4)
        slot = wins.at[layer, (left if side else right)[c]]
        return remote(slot, slot, send.at[q + c], recv.at[q + c], (partner, o))

    def relay(layer, c, side, incoming=False):
        q = 11 + 18 * layer + (6 if side else 8) + c
        owner = far_at[c] if incoming else (left if side else right)[c]
        half = wins.at[layer, owner, pl.ds(0 if side else N // 2, N // 2)]
        return remote(half, half, send.at[q], recv.at[q], (right_me if side else left_me, o))

    def pair(layer, incoming=False):
        q = 11 + 18 * layer
        slot = wins.at[layer, partner if incoming else s]
        return remote(gsend.at[layer, other], slot, send.at[q], recv.at[q], (partner, o))

    def share(layer, first, adjoint):
        for part in range(2):
            if part == 0:
                term = lambda m: first[m, 0] * adjoint[m, 0] + first[m, 1] * adjoint[m, 1]
            else:
                term = lambda m: first[m, 0] * adjoint[m, 1] - first[m, 1] * adjoint[m, 0]
            grad = (term(0) + term(1)).astype(BF)
            gsend[layer, part] = dot(dot(turn_rows, grad).astype(BF), turn_cols).astype(BF)
        start(pair(layer))
        for c in range(2):
            start(near(layer, c, 1))
            start(near(layer, c, 0))
        wins[layer, s] = gsend[layer, core]

    def pass_on(layer):
        for side in (1, 0):
            for c in range(2):
                near_in(layer, c, side).wait_recv()
                start(relay(layer, c, side))

    share(1, arr, cur)

    def behind(rows, i):
        re, im = win[1, 0, rows, :], win[1, 1, rows, :]
        for m in range(2):
            cr, ci = cur[m, 0, rows, :], cur[m, 1, rows, :]
            put(m, rows, i, re * cr + im * ci, re * ci - im * cr)

    by_rows(behind)
    left_mul(e_c)
    right_mul(e_h, cur)
    share(0, probe, cur)

    def leave(rows, i):
        re, im = win[0, 0, rows, :], win[0, 1, rows, :]
        for m in range(2):
            cr, ci = cur[m, 0, rows, :], cur[m, 1, rows, :]
            esend[m, 0, rows, :] = (re * cr + im * ci).astype(BF)
            esend[m, 1, rows, :] = (re * ci - im * cr).astype(BF)

    by_rows(leave)
    q_pair, q_y, q_z, q_x = 53, 54, 57, 64
    e_copy = remote(esend.at[other], erecv, send.at[q_pair], recv.at[q_pair], (partner, o))
    start(e_copy)
    pass_on(1)
    e_copy.wait_recv()

    def add_pair(rows, i):
        for part in range(2):
            ysend[part, rows, :] = (esend[core, part, rows, :].astype(F32) + erecv[part, rows, :].astype(F32)).astype(BF)

    by_rows(add_pair)
    deep = N // NY
    y_copies = []
    for k in range(1, NY):
        y_to = rem(y + k, NY)
        rows_to = pl.ds(pl.multiple_of(y_to * deep, deep), deep)
        copy = remote(
            ysend.at[:, rows_to, :], yrecv.at[k - 1], send.at[q_y + k - 1], recv.at[q_y + k - 1], (s, y_to * NZ + z)
        )
        start(copy)
        y_copies.append(copy)

    lane = lax.broadcasted_iota(jnp.int32, (1, N), 1)

    def gather(layer):
        chunk = 16
        cols = [[(lane + (2 * x + b) * N >= c0) & (lane + (2 * x + b) * N < c0 + N) for b in range(2)] for _, _, c0 in places]
        cols = [[jnp.where(mask, 1.0, 0.0).astype(F32) for mask in pair_masks] for pair_masks in cols]

        def run(i, carry):
            rows = pl.ds(pl.multiple_of(i * chunk, chunk), chunk)
            line = lax.broadcasted_iota(jnp.int32, (chunk, N), 0) + i * chunk
            sums = [[jnp.zeros((chunk, N), F32) for _ in range(2)] for _ in range(2)]
            for n in range(NS):
                term = wins[layer, n, rows, :].astype(F32)
                above = line >= places[n][1]
                for b in range(2):
                    masked = term * cols[n][b]
                    sums[b][0] = sums[b][0] + jnp.where(above, masked, 0.0)
                    sums[b][1] = sums[b][1] + jnp.where(above, 0.0, masked)
            mine = core == 0
            acc[layer, rows, :] = jnp.where(mine, sums[0][0], sums[1][0])
            tsend[layer, rows, :] = jnp.where(mine, sums[1][0], sums[0][0]).astype(BF)
            for b in range(2):
                bsend[layer, b, rows, :] = sums[b][1].astype(BF)
            return carry

        lax.fori_loop(0, N // chunk, run, 0)

    def top_copy(layer):
        q = 71 + layer
        return remote(tsend.at[layer], trecv.at[layer], send.at[q], recv.at[q], (partner, o))

    def bottom_copy(layer, b):
        q = 73 + 2 * layer
        return remote(bsend.at[layer, b], brecv.at[layer, core], send.at[q + b], recv.at[q + core], (2 * x + b, up))

    def bottom_in(layer, c):
        q = 73 + 2 * layer
        return remote(bsend.at[layer, c], brecv.at[layer, c], send.at[q + c], recv.at[q + c], (s, up))

    def collect(layer):
        pair(layer, True).wait_recv()
        for side in (1, 0):
            for c in range(2):
                relay(layer, c, side, True).wait_recv()
        gather(layer)
        for b in range(2):
            start(bottom_copy(layer, b))
        start(top_copy(layer))

    def finish(layer):
        top_copy(layer).wait_recv()
        for c in range(2):
            bottom_in(layer, c).wait_recv()
        for i in range(N // 64):
            rows = pl.ds(i * 64, 64)
            out_ref[layer, core, rows, :] = acc[layer, rows, :] + brecv[layer, core, rows, :].astype(F32)
            out_ref[layer, other, rows, :] = (
                trecv[layer, rows, :].astype(F32) + brecv[layer, other, rows, :].astype(F32)
            )

    collect(1)
    for copy in y_copies:
        copy.wait_recv()
    rows_me = pl.ds(pl.multiple_of(y * deep, deep), deep)
    for part in range(2):
        total = ysend[part, rows_me, :].astype(F32)
        for k in range(NY - 1):
            total = total + yrecv[k, part].astype(F32)
        zsend[part] = total
    z_copies = []
    for k in range(1, NZ):
        z_to = rem(z + k, NZ)
        copy = remote(
            zsend.at[:, pl.ds(pl.multiple_of(z_to * 8, 8), 8), :], zrecv.at[k - 1],
            send.at[q_z + k - 1], recv.at[q_z + k - 1], (s, y * NZ + z_to),
        )
        start(copy)
        z_copies.append(copy)
    pass_on(0)
    for copy in z_copies:
        copy.wait_recv()
    for part in range(2):
        total = zsend[part, pl.ds(pl.multiple_of(z * 8, 8), 8), :]
        for k in range(NZ - 1):
            total = total + zrecv[k, part]
        xsend[part] = total
    x_copies = []
    for k in range(1, NS):
        copy = remote(xsend, xrecv.at[k - 1], send.at[q_x + k - 1], recv.at[q_x + k - 1], (rem(s + k, NS), o))
        start(copy)
        x_copies.append(copy)
    collect(0)
    for copy in x_copies:
        copy.wait_recv()
    factor = 1.0 / math.sqrt(256.0)
    mine, theirs = xsend[...], xrecv[0]
    for k in range(2, NS):
        if k % 2:
            theirs = theirs + xrecv[k - 1]
        else:
            mine = mine + xrecv[k - 1]
    pout_ref[core] = mine * factor
    pout_ref[other] = theirs * factor
    finish(1)
    finish(0)
    for copy in sends:
        copy.wait_send()


def body(object_slices, probe, measured, positions, counts):
    vmem = pltpu.VMEM
    square = lambda *lead: (*lead, N, N)
    any_spec = pl.BlockSpec(memory_space=pl.ANY)
    object_grad, probe_rows = pl.pallas_call(
        main_kernel,
        out_shape=(
            jax.ShapeDtypeStruct(square(2, 2), F32),
            jax.ShapeDtypeStruct((2, 2, 8, N), F32),
        ),
        in_specs=[pl.BlockSpec(memory_space=pltpu.SMEM)] * 2 + [any_spec] * 4,
        out_specs=(pl.BlockSpec(memory_space=vmem), pl.BlockSpec(memory_space=vmem)),
        scratch_shapes=[
            vmem((1, 128), jnp.int32),
            vmem((2 * NS, 1, 128), jnp.int32),
            pltpu.SMEM((2 * NS, 1, 128), jnp.int32),
            *[vmem(square(NS, 2), F32)] * 2,
            vmem(square(2, 2), F32),
            vmem(square(16), BF),
            vmem(square(4), BF),
            *[vmem((2 * N, 2 * N), BF)] * 4,
            vmem(square(2, 2), BF),
            vmem(square(2, 2), BF),
            vmem(square(2, 2), BF),
            vmem(square(), BF),
            vmem(square(2, 2), F32),
            vmem((2 * N, 2 * N), BF),
            vmem((2 * N, 2 * N), BF),
            vmem(square(2, 2), F32),
            vmem(square(2, 2), F32),
            vmem(square(2, 2), F32),
            vmem(square(2, 2), BF),
            vmem(square(2, NS), BF),
            vmem(square(2), F32),
            vmem(square(2), BF),
            vmem(square(2), BF),
            vmem(square(2, 2), BF),
            vmem(square(2, 2), BF),
            vmem(square(2, 2), BF),
            vmem(square(2), BF),
            vmem(square(2), BF),
            vmem((NY - 1, 2, N // NY, N), BF),
            vmem((2, N // NY, N), F32),
            vmem((NZ - 1, 2, 8, N), F32),
            vmem((2, 8, N), F32),
            vmem((NS - 1, 2, 8, N), F32),
            pltpu.SemaphoreType.DMA((4 + 2 * NS,)),
            pltpu.SemaphoreType.DMA((93,)),
            pltpu.SemaphoreType.DMA((93,)),
        ],
        compiler_params=pltpu.CompilerParams(
            collective_id=0, has_side_effects=True, vmem_limit_bytes=60 * 1024 * 1024
        ),
        name="gradient",
    )(positions[0, 0], counts, object_slices, probe, measured[0, 0], tables())
    cols = lax.axis_index("scan") * 32
    return object_grad, lax.dynamic_slice_in_dim(probe_rows, cols, 32, axis=3)


def solution(mesh):
    return jax.shard_map(
        body,
        mesh=mesh,
        in_specs=(
            P(None, None, "obj", None),
            P(),
            P("scan", "obj", None, None, None),
            P("scan", "obj", None, None),
            P("scan", "obj"),
        ),
        out_specs=(P(None, None, "obj", "scan"), P(None, None, "obj", "scan")),
        check_vma=False,
    )
```

```python
import functools
import math

import jax
import jax.numpy as jnp
import numpy as np
from jax import lax
from jax.experimental import pallas as pl
from jax.experimental.pallas import tpu as pltpu
from jax.sharding import PartitionSpec as P

MESH = pl.DeviceIdType.MESH
BF = jnp.bfloat16
F32 = jnp.float32
N = 256
NS, NX, NO, NY, NZ = 8, 4, 32, 4, 8


def rem(a, b):
    return lax.rem(a, jnp.int32(b))


def tables():
    index = np.arange(N)
    angle = (np.outer(index, index) % N) * (2.0 * np.pi / N)
    rounded = lambda a: a.astype(np.float32).astype(BF)
    f_re, f_im = rounded(np.cos(angle) / 16.0), rounded(-np.sin(angle) / 16.0)
    fwd = f_re.astype(np.float64) + 1j * f_im.astype(np.float64)
    freq = np.where(index < N // 2, index, index - N)
    phase = np.exp(-2j * np.pi * ((freq * freq) % (4 * N)) / (4 * N))
    prop = np.conj(fwd) @ (phase[:, None] * fwd)
    return np.stack([f_re, f_im, rounded(prop.real), rounded(prop.imag)])


def remote(src, dst, send, recv, device):
    return pltpu.make_async_remote_copy(
        src_ref=src, dst_ref=dst, send_sem=send, recv_sem=recv, device_id=device, device_id_type=MESH
    )


def main_kernel(
    pos_ref, count_ref, tile_hbm, probe_hbm, meas_hbm, table_hbm, out_ref, pout_ref,
    row, rows_in, tab, tile_0, tile_1, probe, meas, tabs, e_f, e_i, e_h, e_c, hsend, hrecv, local, pattern, win, v, u, arr, far, cur,
    gsend, wins, acc, tsend, trecv, bsend, brecv, esend, erecv, ysend, yrecv, zsend, zrecv, xall,
    dma, send, recv,
):
    s, o = lax.axis_index("scan"), lax.axis_index("obj")
    x, core = lax.div(s, jnp.int32(2)), rem(s, 2)
    y, z = lax.div(o, jnp.int32(NZ)), rem(o, NZ)
    other = 1 - core
    partner = 2 * x + other
    right = [2 * rem(x + 1, NX) + c for c in range(2)]
    left = [2 * rem(x + 3, NX) + c for c in range(2)]
    right_me, left_me = 2 * rem(x + 1, NX) + core, 2 * rem(x + 3, NX) + core
    far_me, left_ot, right_ot, far_ot = (
        2 * rem(x + 2, NX) + core, 2 * rem(x + 3, NX) + other, 2 * rem(x + 1, NX) + other, 2 * rem(x + 2, NX) + other
    )
    far_at = [2 * rem(x + 2, NX) + c for c in range(2)]
    up, down = rem(o + 1, NO), rem(o + NO - 1, NO)
    tile = (tile_0, tile_1)
    sends = []

    barrier = pltpu.get_barrier_semaphore()
    peers = [(rem(s + k, NS), o) for k in range(1, NS)]
    peers += [(s, up)] + [(rem(s + k, NS), down) for k in range(NS)]
    peers += [(s, rem(y + k, NY) * NZ + z) for k in range(1, NY)]
    peers += [(s, y * NZ + rem(z + k, NZ)) for k in range(1, NZ)]
    for peer in peers:
        pl.semaphore_signal(barrier, inc=1, device_id=peer, device_id_type=MESH)

    loads = [
        pltpu.make_async_copy(table_hbm, tabs, dma.at[0]),
        pltpu.make_async_copy(probe_hbm, probe, dma.at[1]),
        pltpu.make_async_copy(meas_hbm, meas.at[pl.ds(2 * s, 2)], dma.at[2]),
    ]
    for layer in range(2):
        for b in range(NS):
            block = tile_hbm.at[layer, :, :, pl.ds(b * N, N)]
            loads.append(pltpu.make_async_copy(block, tile[layer].at[b], dma.at[3 + NS * layer + b]))
    for load in loads:
        load.start()

    lane = lax.broadcasted_iota(jnp.int32, (1, 128), 1)
    line = jnp.zeros((1, 128), jnp.int32)
    for j, value in enumerate((pos_ref[0, 0], pos_ref[0, 1], pos_ref[1, 0], pos_ref[1, 1], count_ref[0, 0])):
        line = jnp.where(lane == j, value, line)
    row[...] = line
    rows_in[s] = line

    loads[0].wait()
    for e_ref, re, im, sign in ((e_f, 0, 1, 1), (e_i, 0, 1, -1), (e_h, 2, 3, 1), (e_c, 2, 3, -1)):
        e_ref[0:N, 0:N] = tabs[re]
        e_ref[N:, N:] = tabs[re]
        e_ref[0:N, N:] = -tabs[im] if sign > 0 else tabs[im]
        e_ref[N:, 0:N] = tabs[im] if sign > 0 else -tabs[im]

    def one_hot(shape, rule):
        a, b = lax.broadcasted_iota(jnp.int32, shape, 0), lax.broadcasted_iota(jnp.int32, shape, 1)
        return jnp.where(rule(a, b), 1.0, 0.0).astype(BF)

    def dot(a, b):
        return jnp.dot(a, b, preferred_element_type=F32)

    def col_block(col):
        k = jnp.int32(0)
        for edge in range(1, NS - 1):
            k = k + jnp.where(col >= edge * N, 1, 0)
        return k

    def picks(offset):
        return [one_hot((N, N), lambda a, b: a + h * N == b + offset) for h in range(2)]

    def columns(layer, part, k, pick):
        first, second = tile[layer][k, part].astype(BF), tile[layer][k + 1, part].astype(BF)
        return (dot(first, pick[0]) + dot(second, pick[1])).astype(BF)


    pl.semaphore_wait(barrier, len(peers))

    def start(copy):
        copy.start()
        sends.append(copy)

    def meas_copy(q, slot, n, peer):
        ref = meas.at[pl.ds(slot, n)]
        return remote(ref, ref, send.at[q], recv.at[q], (peer, o))

    def place_copy(k, base, owner):
        peer = (rem(s + k, NS), up if base else o)
        return remote(row, rows_in.at[base + owner], send.at[85 + base + k], recv.at[85 + base + k], peer)

    every = [(k, base) for base in (0, NS) for k in range(NS) if base or k]
    for k, base in every:
        start(place_copy(k, base, s))
    for k, base in every:
        place_copy(k, base, rem(s + NS - k, NS)).wait_recv()
    fetch = pltpu.make_async_copy(rows_in, tab, dma.at[3 + 2 * NS])
    fetch.start()
    for q, peer in ((0, partner), (1, right_me), (2, left_me)):
        start(remote(meas_hbm, meas.at[pl.ds(2 * s, 2)], send.at[q], recv.at[q], (peer, o)))
    fetch.wait()

    def assigned(base, n):
        start, found = jnp.int32(0), [jnp.int32(0)] * 3
        for t in range(NS):
            count = tab[base + t, 0, 4]
            for k in range(2):
                hit = (k < count) & (start + k == n)
                for j, value in enumerate((jnp.int32(2 * t + k), tab[base + t, 0, 2 * k], tab[base + t, 0, 2 * k + 1])):
                    found[j] = jnp.where(hit, value, found[j])
            start = start + count
        return found

    places = [assigned(0, n) for n in range(NS)]
    source, row0, col0 = places[0]
    for n in range(1, NS):
        source, row0, col0 = (jnp.where(s == n, a, b) for a, b in zip(places[n], (source, row0, col0)))
    _, _, col_prev = assigned(NS, s)

    k_prev, k_own = col_block(col_prev), col_block(col0)
    pick_prev = picks(col_prev - k_prev * N)

    def halo_copy(layer):
        return remote(hsend.at[layer], hrecv.at[layer], send.at[9 + layer], recv.at[9 + layer], (s, down))

    for layer in range(2):
        for b in range(NS):
            loads[3 + NS * layer + b].wait()
        for part in range(2):
            hsend[layer, part] = columns(layer, part, k_prev, pick_prev)
        start(halo_copy(layer))
    pick_own = picks(col0 - k_own * N)
    for layer in range(2):
        for part in range(2):
            local[layer, part] = columns(layer, part, k_own, pick_own)
    rows_here = one_hot((N, N), lambda a, b: b == a + row0)
    rows_next = one_hot((N, N), lambda a, b: b + N == a + row0)
    turn = jnp.where(col0 == 7 * N, 0, col0 - k_own * N)
    turn_rows = one_hot((N, N), lambda a, b: (b + row0 == a) | (b + row0 == a + N))
    turn_cols = one_hot((N, N), lambda a, b: (a + turn == b) | (a + turn == b + N))
    loads[1].wait()

    def window(layer):
        halo_copy(layer).wait_recv()
        for part in range(2):
            win[layer, part] = dot(rows_here, local[layer, part]) + dot(rows_next, hrecv[layer, part])

    step = 32

    def by_rows(body):
        def run(i, carry):
            body(pl.ds(pl.multiple_of(i * step, step), step), i)
            return carry

        lax.fori_loop(0, N // step, run, 0)

    def put(m, rows, i, re, im):
        v[pl.ds(pl.multiple_of(i * step, step), step), m * N : (m + 1) * N] = re.astype(BF)
        v[pl.ds(pl.multiple_of(N + i * step, step), step), m * N : (m + 1) * N] = im.astype(BF)

    def left_mul(matrix):
        for m in range(2):
            product = dot(matrix[...], v[:, m * N : (m + 1) * N])
            u[m * N : (m + 1) * N, 0:N] = product[0:N].astype(BF)
            u[m * N : (m + 1) * N, N:] = product[N:].astype(BF)

    def right_mul(matrix, result):
        for part in range(2):
            product = dot(u[...], matrix[:, part * N : (part + 1) * N])
            result[0, part] = product[0:N]
            result[1, part] = product[N:]

    window(0)

    def enter(rows, i):
        re, im = win[0, 0, rows, :], win[0, 1, rows, :]
        for m in range(2):
            pr, pi = probe[m, 0, rows, :], probe[m, 1, rows, :]
            put(m, rows, i, pr * re - pi * im, pr * im + pi * re)

    by_rows(enter)
    left_mul(e_h)
    meas_copy(1, 2 * left_me, 2, right_me).wait_recv()
    start(meas_copy(3, 2 * left_me, 1, right_me))
    start(meas_copy(4, 2 * left_me, 2, partner))
    meas_copy(2, 2 * right_me, 2, left_me).wait_recv()
    start(meas_copy(5, 2 * right_me + 1, 1, left_me))
    start(meas_copy(6, 2 * right_me, 2, partner))
    right_mul(e_c, arr)
    window(1)

    def second(rows, i):
        re, im = win[1, 0, rows, :], win[1, 1, rows, :]
        for m in range(2):
            pr, pi = arr[m, 0, rows, :], arr[m, 1, rows, :]
            put(m, rows, i, pr * re - pi * im, pr * im + pi * re)

    by_rows(second)
    meas_copy(3, 2 * far_me, 1, right_me).wait_recv()
    start(meas_copy(7, 2 * far_me, 1, partner))
    meas_copy(5, 2 * far_me + 1, 1, left_me).wait_recv()
    start(meas_copy(8, 2 * far_me + 1, 1, partner))
    left_mul(e_f)
    right_mul(e_i, far)
    loads[2].wait()
    meas_copy(0, 2 * partner, 2, partner).wait_recv()
    meas_copy(4, 2 * left_ot, 2, partner).wait_recv()
    meas_copy(6, 2 * right_ot, 2, partner).wait_recv()
    meas_copy(7, 2 * far_ot, 1, partner).wait_recv()
    meas_copy(8, 2 * far_ot + 1, 1, partner).wait_recv()

    pattern[...] = meas[source]

    def misfit(rows, i):
        parts = [(far[m, 0, rows, :], far[m, 1, rows, :]) for m in range(2)]
        total = parts[0][0] ** 2 + parts[0][1] ** 2 + (parts[1][0] ** 2 + parts[1][1] ** 2)
        gap = total - pattern[rows, :].astype(F32)
        for m in range(2):
            put(m, rows, i, gap * parts[m][0], gap * parts[m][1])

    by_rows(misfit)
    left_mul(e_i)
    right_mul(e_f, cur)

    half = N // 2
    chunks = [(1, 0), (1, 1), (0, 0), (0, 1)]

    def span(j, part=None):
        first = chunks[j][1] * half
        return pl.ds(first, half) if part is None else pl.ds(first + part * half // 2, half // 2)

    def near(j, c, side):
        layer, q = chunks[j][0], 11 + 14 * j + (2 if side else 4)
        peer = (right if side else left)[c]
        return remote(
            gsend.at[layer, c, span(j)], wins.at[layer, s, span(j)], send.at[q + c], recv.at[q + core], (peer, o)
        )

    def near_in(j, c, side):
        layer, q = chunks[j][0], 11 + 14 * j + (2 if side else 4)
        slot = wins.at[layer, (left if side else right)[c], span(j)]
        return remote(slot, slot, send.at[q + c], recv.at[q + c], (partner, o))

    def relay(j, c, side, incoming=False):
        q = 11 + 14 * j + (6 if side else 8) + c
        owner = far_at[c] if incoming else (left if side else right)[c]
        piece = wins.at[chunks[j][0], owner, span(j, 0 if side else 1)]
        return remote(piece, piece, send.at[q], recv.at[q], (right_me if side else left_me, o))

    def pair(j, incoming=False):
        layer, q = chunks[j][0], 11 + 14 * j
        slot = wins.at[layer, partner if incoming else s, span(j)]
        return remote(gsend.at[layer, other, span(j)], slot, send.at[q], recv.at[q], (partner, o))

    def share(layer, first, adjoint):
        for part in range(2):
            if part == 0:
                term = lambda m: first[m, 0] * adjoint[m, 0] + first[m, 1] * adjoint[m, 1]
            else:
                term = lambda m: first[m, 0] * adjoint[m, 1] - first[m, 1] * adjoint[m, 0]
            grad = (term(0) + term(1)).astype(BF)
            gsend[layer, part] = dot(dot(turn_rows, grad).astype(BF), turn_cols).astype(BF)
        wins[layer, s] = gsend[layer, core]

    def launch(j):
        for c in range(2):
            start(near(j, c, 1))
            start(near(j, c, 0))
        start(pair(j))

    def pass_on(j):
        for c in range(2):
            for side in (1, 0):
                near_in(j, c, side).wait_recv()
                start(relay(j, c, side))

    lane = lax.broadcasted_iota(jnp.int32, (1, N), 1)
    cols = [
        [jnp.where((lane + (2 * x + b) * N >= c0) & (lane + (2 * x + b) * N < c0 + N), 1.0, 0.0) for b in range(2)]
        for _, _, c0 in places
    ]

    def gather(j):
        layer, first = chunks[j][0], chunks[j][1] * half
        chunk = 16

        def run(i, carry):
            at = pl.multiple_of(first + i * chunk, chunk)
            rows = pl.ds(at, chunk)
            line = lax.broadcasted_iota(jnp.int32, (chunk, N), 0) + at
            sums = [[jnp.zeros((chunk, N), F32) for _ in range(2)] for _ in range(2)]
            for n in range(NS):
                term = wins[layer, n, rows, :].astype(F32)
                above = line >= places[n][1]
                for b in range(2):
                    masked = term * cols[n][b]
                    sums[b][0] = sums[b][0] + jnp.where(above, masked, 0.0)
                    sums[b][1] = sums[b][1] + jnp.where(above, 0.0, masked)
            mine = core == 0
            acc[layer, rows, :] = jnp.where(mine, sums[0][0], sums[1][0])
            tsend[layer, rows, :] = jnp.where(mine, sums[1][0], sums[0][0]).astype(BF)
            for b in range(2):
                bsend[layer, b, rows, :] = sums[b][1].astype(BF)
            return carry

        lax.fori_loop(0, half // chunk, run, 0)

    def top_copy(j):
        layer, q = chunks[j][0], 21 + 14 * j
        return remote(tsend.at[layer, span(j)], trecv.at[layer, span(j)], send.at[q], recv.at[q], (partner, o))

    def bottom_copy(j, b):
        layer, q = chunks[j][0], 22 + 14 * j
        return remote(
            bsend.at[layer, b, span(j)], brecv.at[layer, core, span(j)], send.at[q + b], recv.at[q + core], (2 * x + b, up)
        )

    def bottom_in(j, c):
        layer, q = chunks[j][0], 22 + 14 * j
        return remote(bsend.at[layer, c, span(j)], brecv.at[layer, c, span(j)], send.at[q + c], recv.at[q + c], (s, up))

    def collect(j):
        pair(j, True).wait_recv()
        for c in range(2):
            for side in (1, 0):
                relay(j, c, side, True).wait_recv()
        gather(j)
        for b in range(2):
            start(bottom_copy(j, b))
        start(top_copy(j))

    def finish(j):
        layer = chunks[j][0]
        top_copy(j).wait_recv()
        for c in range(2):
            bottom_in(j, c).wait_recv()
        for i in range(2):
            rows = span(j, i)
            out_ref[layer, core, rows, :] = acc[layer, rows, :] + brecv[layer, core, rows, :].astype(F32)
            out_ref[layer, other, rows, :] = (
                trecv[layer, rows, :].astype(F32) + brecv[layer, other, rows, :].astype(F32)
            )

    share(1, arr, cur)
    launch(0)
    launch(1)

    def behind(rows, i):
        re, im = win[1, 0, rows, :], win[1, 1, rows, :]
        for m in range(2):
            cr, ci = cur[m, 0, rows, :], cur[m, 1, rows, :]
            put(m, rows, i, re * cr + im * ci, re * ci - im * cr)

    by_rows(behind)
    left_mul(e_c)
    right_mul(e_h, cur)

    def leave(rows, i):
        re, im = win[0, 0, rows, :], win[0, 1, rows, :]
        for m in range(2):
            cr, ci = cur[m, 0, rows, :], cur[m, 1, rows, :]
            esend[m, 0, rows, :] = (re * cr + im * ci).astype(BF)
            esend[m, 1, rows, :] = (re * ci - im * cr).astype(BF)

    by_rows(leave)
    q_pair, q_y, q_z, q_x = 67, 68, 71, 78
    e_copy = remote(esend.at[other], erecv, send.at[q_pair], recv.at[q_pair], (partner, o))
    start(e_copy)
    share(0, probe, cur)
    e_copy.wait_recv()

    def add_pair(rows, i):
        for part in range(2):
            ysend[part, rows, :] = (esend[core, part, rows, :].astype(F32) + erecv[part, rows, :].astype(F32)).astype(BF)

    by_rows(add_pair)
    deep = N // NY
    y_copies = []
    for k in range(1, NY):
        y_to = rem(y + k, NY)
        rows_to = pl.ds(pl.multiple_of(y_to * deep, deep), deep)
        copy = remote(
            ysend.at[:, rows_to, :], yrecv.at[k - 1], send.at[q_y + k - 1], recv.at[q_y + k - 1], (s, y_to * NZ + z)
        )
        start(copy)
        y_copies.append(copy)
    pass_on(0)
    launch(2)
    for copy in y_copies:
        copy.wait_recv()
    rows_me = pl.ds(pl.multiple_of(y * deep, deep), deep)
    totals = []
    for part in range(2):
        total = ysend[part, rows_me, :].astype(F32)
        for k in range(NY - 1):
            total = total + yrecv[k, part].astype(F32)
        totals.append(total)
    for k in range(NZ):
        zsend[k] = jnp.concatenate([total[8 * k : 8 * k + 8] for total in totals], axis=0).astype(BF)
    z_copies = []
    for k in range(1, NZ):
        z_to = rem(z + k, NZ)
        copy = remote(
            zsend.at[z_to], zrecv.at[k - 1], send.at[q_z + k - 1], recv.at[q_z + k - 1], (s, y * NZ + z_to)
        )
        start(copy)
        z_copies.append(copy)
    pass_on(1)
    launch(3)
    collect(0)
    for copy in z_copies:
        copy.wait_recv()
    total = zsend[z].astype(F32)
    for k in range(NZ - 1):
        total = total + zrecv[k].astype(F32)
    xall[0] = total.astype(BF)
    x_copies = []
    for k in range(1, NS):
        copy = remote(xall.at[0], xall.at[k], send.at[q_x + k - 1], recv.at[q_x + k - 1], (rem(s + k, NS), o))
        start(copy)
        x_copies.append(copy)
    pass_on(2)
    collect(1)
    pass_on(3)
    finish(0)
    collect(2)
    for copy in x_copies:
        copy.wait_recv()
    pick = one_hot((N, 128), lambda a, b: a == b + 32 * s)
    factor = 1.0 / math.sqrt(256.0)
    shares = [dot(xall[k], pick) for k in range(NS)]
    mine = (shares[0] + shares[2] + (shares[4] + shares[6])) * factor
    theirs = (shares[1] + shares[3] + (shares[5] + shares[7])) * factor
    for part in range(2):
        pout_ref[core, part] = mine[8 * part : 8 * part + 8, :32]
        pout_ref[other, part] = theirs[8 * part : 8 * part + 8, :32]
    finish(1)
    collect(3)
    finish(2)
    finish(3)
    for copy in sends:
        copy.wait_send()


def body(object_slices, probe, measured, positions, counts):
    vmem = pltpu.VMEM
    square = lambda *lead: (*lead, N, N)
    any_spec = pl.BlockSpec(memory_space=pl.ANY)
    return pl.pallas_call(
        main_kernel,
        out_shape=(
            jax.ShapeDtypeStruct(square(2, 2), F32),
            jax.ShapeDtypeStruct((2, 2, 8, 32), F32),
        ),
        in_specs=[pl.BlockSpec(memory_space=pltpu.SMEM)] * 2 + [any_spec] * 4,
        out_specs=(pl.BlockSpec(memory_space=vmem), pl.BlockSpec(memory_space=vmem)),
        scratch_shapes=[
            vmem((1, 128), jnp.int32),
            vmem((2 * NS, 1, 128), jnp.int32),
            pltpu.SMEM((2 * NS, 1, 128), jnp.int32),
            *[vmem(square(NS, 2), F32)] * 2,
            vmem(square(2, 2), F32),
            vmem(square(16), BF),
            vmem(square(4), BF),
            *[vmem((2 * N, 2 * N), BF)] * 4,
            vmem(square(2, 2), BF),
            vmem(square(2, 2), BF),
            vmem(square(2, 2), BF),
            vmem(square(), BF),
            vmem(square(2, 2), F32),
            vmem((2 * N, 2 * N), BF),
            vmem((2 * N, 2 * N), BF),
            vmem(square(2, 2), F32),
            vmem(square(2, 2), F32),
            vmem(square(2, 2), F32),
            vmem(square(2, 2), BF),
            vmem(square(2, NS), BF),
            vmem(square(2), F32),
            vmem(square(2), BF),
            vmem(square(2), BF),
            vmem(square(2, 2), BF),
            vmem(square(2, 2), BF),
            vmem(square(2, 2), BF),
            vmem(square(2), BF),
            vmem(square(2), BF),
            vmem((NY - 1, 2, N // NY, N), BF),
            vmem((NZ, 16, N), BF),
            vmem((NZ - 1, 16, N), BF),
            vmem((NS, 16, N), BF),
            pltpu.SemaphoreType.DMA((4 + 2 * NS,)),
            pltpu.SemaphoreType.DMA((101,)),
            pltpu.SemaphoreType.DMA((101,)),
        ],
        compiler_params=pltpu.CompilerParams(
            collective_id=0, has_side_effects=True, vmem_limit_bytes=60 * 1024 * 1024
        ),
        name="gradient",
    )(positions[0, 0], counts, object_slices, probe, measured[0, 0], tables())


def solution(mesh):
    return jax.shard_map(
        body,
        mesh=mesh,
        in_specs=(
            P(None, None, "obj", None),
            P(),
            P("scan", "obj", None, None, None),
            P("scan", "obj", None, None),
            P("scan", "obj"),
        ),
        out_specs=(P(None, None, "obj", "scan"), P(None, None, "obj", "scan")),
        check_vma=False,
    )
```

```python
import functools
import math

import jax
import jax.numpy as jnp
import numpy as np
from jax import lax
from jax.experimental import pallas as pl
from jax.experimental.pallas import tpu as pltpu
from jax.sharding import PartitionSpec as P

MESH = pl.DeviceIdType.MESH
BF = jnp.bfloat16
F32 = jnp.float32
N = 256
NS, NX, NO, NY, NZ = 8, 4, 32, 4, 8


def rem(a, b):
    return lax.rem(a, jnp.int32(b))


def tables():
    index = np.arange(N)
    angle = (np.outer(index, index) % N) * (2.0 * np.pi / N)
    rounded = lambda a: a.astype(np.float32).astype(BF)
    f_re, f_im = rounded(np.cos(angle) / 16.0), rounded(-np.sin(angle) / 16.0)
    fwd = f_re.astype(np.float64) + 1j * f_im.astype(np.float64)
    freq = np.where(index < N // 2, index, index - N)
    phase = np.exp(-2j * np.pi * ((freq * freq) % (4 * N)) / (4 * N))
    prop = np.conj(fwd) @ (phase[:, None] * fwd)
    return np.stack([f_re, f_im, rounded(prop.real), rounded(prop.imag)])


def remote(src, dst, send, recv, device):
    return pltpu.make_async_remote_copy(
        src_ref=src, dst_ref=dst, send_sem=send, recv_sem=recv, device_id=device, device_id_type=MESH
    )


def main_kernel(
    count_ref, pos_hbm, tile_hbm, probe_hbm, meas_hbm, table_hbm, out_hbm, pout_ref,
    pos_ref, row, rows_in, tab, tile_0, tile_1, probe, meas, tabs, e_f, e_i, e_h, e_c, hsend, hrecv, local, pattern, win, v, u, arr, far, cur,
    gsend, wins, acc, done, tsend, trecv, bsend, brecv, esend, erecv, ysend, yrecv, zsend, zrecv, xall,
    dma, send, recv,
):
    s, o = lax.axis_index("scan"), lax.axis_index("obj")
    x, core = lax.div(s, jnp.int32(2)), rem(s, 2)
    y, z = lax.div(o, jnp.int32(NZ)), rem(o, NZ)
    other = 1 - core
    partner = 2 * x + other
    right = [2 * rem(x + 1, NX) + c for c in range(2)]
    left = [2 * rem(x + 3, NX) + c for c in range(2)]
    right_me, left_me = 2 * rem(x + 1, NX) + core, 2 * rem(x + 3, NX) + core
    far_me, left_ot, right_ot, far_ot = (
        2 * rem(x + 2, NX) + core, 2 * rem(x + 3, NX) + other, 2 * rem(x + 1, NX) + other, 2 * rem(x + 2, NX) + other
    )
    far_at = [2 * rem(x + 2, NX) + c for c in range(2)]
    up, down = rem(o + 1, NO), rem(o + NO - 1, NO)
    tile = (tile_0, tile_1)
    sends, gone = [], []

    barrier = pltpu.get_barrier_semaphore()
    peers = [(rem(s + k, NS), o) for k in range(1, NS)]
    peers += [(s, up)] + [(rem(s + k, NS), down) for k in range(NS)]
    peers += [(s, rem(y + k, NY) * NZ + z) for k in range(1, NY)]
    peers += [(s, y * NZ + rem(z + k, NZ)) for k in range(1, NZ)]
    for peer in peers:
        pl.semaphore_signal(barrier, inc=1, device_id=peer, device_id_type=MESH)

    given = pltpu.make_async_copy(pos_hbm, pos_ref, dma.at[4 + 2 * NS])
    given.start()
    loads = [
        pltpu.make_async_copy(table_hbm, tabs, dma.at[0]),
        pltpu.make_async_copy(probe_hbm, probe, dma.at[1]),
        pltpu.make_async_copy(meas_hbm, meas.at[pl.ds(2 * s, 2)], dma.at[2]),
    ]
    for layer in range(2):
        for b in range(NS):
            block = tile_hbm.at[layer, :, :, pl.ds(b * N, N)]
            loads.append(pltpu.make_async_copy(block, tile[layer].at[b], dma.at[3 + NS * layer + b]))
    for load in loads:
        load.start()

    lane = lax.broadcasted_iota(jnp.int32, (1, 128), 1)
    given.wait()
    line = jnp.zeros((1, 128), jnp.int32)
    for j, value in enumerate((pos_ref[0, 0], pos_ref[0, 1], pos_ref[1, 0], pos_ref[1, 1], count_ref[0, 0])):
        line = jnp.where(lane == j, value, line)
    row[...] = line
    rows_in[s] = line

    def one_hot(shape, rule):
        a, b = lax.broadcasted_iota(jnp.int32, shape, 0), lax.broadcasted_iota(jnp.int32, shape, 1)
        return jnp.where(rule(a, b), 1.0, 0.0).astype(BF)

    def dot(a, b):
        return jnp.dot(a, b, preferred_element_type=F32)

    def col_block(col):
        k = jnp.int32(0)
        for edge in range(1, NS - 1):
            k = k + jnp.where(col >= edge * N, 1, 0)
        return k

    def picks(offset):
        return [one_hot((N, N), lambda a, b: a + h * N == b + offset) for h in range(2)]

    def columns(layer, part, k, pick):
        first, second = tile[layer][k, part].astype(BF), tile[layer][k + 1, part].astype(BF)
        return (dot(first, pick[0]) + dot(second, pick[1])).astype(BF)


    pl.semaphore_wait(barrier, len(peers))

    def start(copy):
        copy.start()
        sends.append(copy)

    def meas_copy(q, slot, n, peer):
        ref = meas.at[pl.ds(slot, n)]
        return remote(ref, ref, send.at[q], recv.at[q], (peer, o))

    def place_copy(k, base, owner):
        peer = (rem(s + k, NS), up if base else o)
        return remote(row, rows_in.at[base + owner], send.at[85 + base + k], recv.at[85 + base + k], peer)

    every = [(k, base) for base in (0, NS) for k in range(NS) if base or k]
    for k, base in every:
        start(place_copy(k, base, s))
    for q, peer in ((0, partner), (1, right_me), (2, left_me)):
        start(remote(meas_hbm, meas.at[pl.ds(2 * s, 2)], send.at[q], recv.at[q], (peer, o)))
    loads[0].wait()
    for e_ref, re, im, sign in ((e_f, 0, 1, 1), (e_i, 0, 1, -1), (e_h, 2, 3, 1), (e_c, 2, 3, -1)):
        e_ref[0:N, 0:N] = tabs[re]
        e_ref[N:, N:] = tabs[re]
        e_ref[0:N, N:] = -tabs[im] if sign > 0 else tabs[im]
        e_ref[N:, 0:N] = tabs[im] if sign > 0 else -tabs[im]

    for k, base in every:
        place_copy(k, base, rem(s + NS - k, NS)).wait_recv()
    fetch = pltpu.make_async_copy(rows_in, tab, dma.at[3 + 2 * NS])
    fetch.start()
    fetch.wait()

    def assigned(base, n):
        start, found = jnp.int32(0), [jnp.int32(0)] * 3
        for t in range(NS):
            count = tab[base + t, 0, 4]
            for k in range(2):
                hit = (k < count) & (start + k == n)
                for j, value in enumerate((jnp.int32(2 * t + k), tab[base + t, 0, 2 * k], tab[base + t, 0, 2 * k + 1])):
                    found[j] = jnp.where(hit, value, found[j])
            start = start + count
        return found

    places = [assigned(0, n) for n in range(NS)]
    source, row0, col0 = places[0]
    for n in range(1, NS):
        source, row0, col0 = (jnp.where(s == n, a, b) for a, b in zip(places[n], (source, row0, col0)))
    _, _, col_prev = assigned(NS, s)

    k_prev, k_own = col_block(col_prev), col_block(col0)
    pick_prev = picks(col_prev - k_prev * N)

    def halo_copy(layer):
        return remote(hsend.at[layer], hrecv.at[layer], send.at[9 + layer], recv.at[9 + layer], (s, down))

    for layer in range(2):
        for b in range(NS):
            loads[3 + NS * layer + b].wait()
        for part in range(2):
            hsend[layer, part] = columns(layer, part, k_prev, pick_prev)
        start(halo_copy(layer))
    pick_own = picks(col0 - k_own * N)
    for layer in range(2):
        for part in range(2):
            local[layer, part] = columns(layer, part, k_own, pick_own)
    rows_here = one_hot((N, N), lambda a, b: b == a + row0)
    rows_next = one_hot((N, N), lambda a, b: b + N == a + row0)
    turn = jnp.where(col0 == 7 * N, 0, col0 - k_own * N)
    turn_rows = one_hot((N, N), lambda a, b: (b + row0 == a) | (b + row0 == a + N))
    turn_cols = one_hot((N, N), lambda a, b: (a + turn == b) | (a + turn == b + N))
    loads[1].wait()

    def window(layer):
        halo_copy(layer).wait_recv()
        for part in range(2):
            win[layer, part] = dot(rows_here, local[layer, part]) + dot(rows_next, hrecv[layer, part])

    step = 32

    def by_rows(body):
        def run(i, carry):
            body(pl.ds(pl.multiple_of(i * step, step), step), i)
            return carry

        lax.fori_loop(0, N // step, run, 0)

    def put(m, rows, i, re, im):
        v[pl.ds(pl.multiple_of(i * step, step), step), m * N : (m + 1) * N] = re.astype(BF)
        v[pl.ds(pl.multiple_of(N + i * step, step), step), m * N : (m + 1) * N] = im.astype(BF)

    def left_mul(matrix):
        for m in range(2):
            product = dot(matrix[...], v[:, m * N : (m + 1) * N])
            u[m * N : (m + 1) * N, 0:N] = product[0:N].astype(BF)
            u[m * N : (m + 1) * N, N:] = product[N:].astype(BF)

    def right_mul(matrix, result):
        for part in range(2):
            product = dot(u[...], matrix[:, part * N : (part + 1) * N])
            result[0, part] = product[0:N]
            result[1, part] = product[N:]

    window(0)

    def enter(rows, i):
        re, im = win[0, 0, rows, :], win[0, 1, rows, :]
        for m in range(2):
            pr, pi = probe[m, 0, rows, :], probe[m, 1, rows, :]
            put(m, rows, i, pr * re - pi * im, pr * im + pi * re)

    by_rows(enter)
    left_mul(e_h)
    meas_copy(1, 2 * left_me, 2, right_me).wait_recv()
    start(meas_copy(3, 2 * left_me, 1, right_me))
    start(meas_copy(4, 2 * left_me, 2, partner))
    meas_copy(2, 2 * right_me, 2, left_me).wait_recv()
    start(meas_copy(5, 2 * right_me + 1, 1, left_me))
    start(meas_copy(6, 2 * right_me, 2, partner))
    right_mul(e_c, arr)
    window(1)

    def second(rows, i):
        re, im = win[1, 0, rows, :], win[1, 1, rows, :]
        for m in range(2):
            pr, pi = arr[m, 0, rows, :], arr[m, 1, rows, :]
            put(m, rows, i, pr * re - pi * im, pr * im + pi * re)

    by_rows(second)
    meas_copy(3, 2 * far_me, 1, right_me).wait_recv()
    start(meas_copy(7, 2 * far_me, 1, partner))
    meas_copy(5, 2 * far_me + 1, 1, left_me).wait_recv()
    start(meas_copy(8, 2 * far_me + 1, 1, partner))
    left_mul(e_f)
    right_mul(e_i, far)
    loads[2].wait()
    meas_copy(0, 2 * partner, 2, partner).wait_recv()
    meas_copy(4, 2 * left_ot, 2, partner).wait_recv()
    meas_copy(6, 2 * right_ot, 2, partner).wait_recv()
    meas_copy(7, 2 * far_ot, 1, partner).wait_recv()
    meas_copy(8, 2 * far_ot + 1, 1, partner).wait_recv()

    pattern[...] = meas[source]

    def misfit(rows, i):
        parts = [(far[m, 0, rows, :], far[m, 1, rows, :]) for m in range(2)]
        total = parts[0][0] ** 2 + parts[0][1] ** 2 + (parts[1][0] ** 2 + parts[1][1] ** 2)
        gap = total - pattern[rows, :].astype(F32)
        for m in range(2):
            put(m, rows, i, gap * parts[m][0], gap * parts[m][1])

    by_rows(misfit)
    left_mul(e_i)
    right_mul(e_f, cur)

    half = N // 2
    chunks = [(1, 0), (1, 1), (0, 0), (0, 1)]

    def span(j, part=None):
        first = chunks[j][1] * half
        return pl.ds(first, half) if part is None else pl.ds(first + part * half // 2, half // 2)

    def near(j, c, side):
        layer, q = chunks[j][0], 11 + 14 * j + (2 if side else 4)
        peer = (right if side else left)[c]
        return remote(
            gsend.at[layer, c, span(j)], wins.at[layer, s, span(j)], send.at[q + c], recv.at[q + core], (peer, o)
        )

    def near_in(j, c, side):
        layer, q = chunks[j][0], 11 + 14 * j + (2 if side else 4)
        slot = wins.at[layer, (left if side else right)[c], span(j)]
        return remote(slot, slot, send.at[q + c], recv.at[q + c], (partner, o))

    def relay(j, c, side, incoming=False):
        q = 11 + 14 * j + (6 if side else 8) + c
        owner = far_at[c] if incoming else (left if side else right)[c]
        piece = wins.at[chunks[j][0], owner, span(j, 0 if side else 1)]
        return remote(piece, piece, send.at[q], recv.at[q], (right_me if side else left_me, o))

    def pair(j, incoming=False):
        layer, q = chunks[j][0], 11 + 14 * j
        slot = wins.at[layer, partner if incoming else s, span(j)]
        return remote(gsend.at[layer, other, span(j)], slot, send.at[q], recv.at[q], (partner, o))

    def share(layer, first, adjoint):
        for part in range(2):
            if part == 0:
                term = lambda m: first[m, 0] * adjoint[m, 0] + first[m, 1] * adjoint[m, 1]
            else:
                term = lambda m: first[m, 0] * adjoint[m, 1] - first[m, 1] * adjoint[m, 0]
            grad = (term(0) + term(1)).astype(BF)
            gsend[layer, part] = dot(dot(turn_rows, grad).astype(BF), turn_cols).astype(BF)
        wins[layer, s] = gsend[layer, core]

    def launch(j):
        for c in range(2):
            start(near(j, c, 1))
            start(near(j, c, 0))
        start(pair(j))

    def pass_on(j):
        for c in range(2):
            for side in (1, 0):
                near_in(j, c, side).wait_recv()
                start(relay(j, c, side))

    lane = lax.broadcasted_iota(jnp.int32, (1, N), 1)
    cols = [
        [jnp.where((lane + (2 * x + b) * N >= c0) & (lane + (2 * x + b) * N < c0 + N), 1.0, 0.0) for b in range(2)]
        for _, _, c0 in places
    ]

    def gather(j):
        layer, first = chunks[j][0], chunks[j][1] * half
        chunk = 16

        def run(i, carry):
            at = pl.multiple_of(first + i * chunk, chunk)
            rows = pl.ds(at, chunk)
            line = lax.broadcasted_iota(jnp.int32, (chunk, N), 0) + at
            sums = [[jnp.zeros((chunk, N), F32) for _ in range(2)] for _ in range(2)]
            for n in range(NS):
                term = wins[layer, n, rows, :].astype(F32)
                above = line >= places[n][1]
                for b in range(2):
                    masked = term * cols[n][b]
                    sums[b][0] = sums[b][0] + jnp.where(above, masked, 0.0)
                    sums[b][1] = sums[b][1] + jnp.where(above, 0.0, masked)
            mine = core == 0
            acc[layer, rows, :] = jnp.where(mine, sums[0][0], sums[1][0])
            tsend[layer, rows, :] = jnp.where(mine, sums[1][0], sums[0][0]).astype(BF)
            for b in range(2):
                bsend[layer, b, rows, :] = sums[b][1].astype(BF)
            return carry

        lax.fori_loop(0, half // chunk, run, 0)

    def top_copy(j):
        layer, q = chunks[j][0], 21 + 14 * j
        return remote(tsend.at[layer, span(j)], trecv.at[layer, span(j)], send.at[q], recv.at[q], (partner, o))

    def bottom_copy(j, b):
        layer, q = chunks[j][0], 22 + 14 * j
        return remote(
            bsend.at[layer, b, span(j)], brecv.at[layer, core, span(j)], send.at[q + b], recv.at[q + core], (2 * x + b, up)
        )

    def bottom_in(j, c):
        layer, q = chunks[j][0], 22 + 14 * j
        return remote(bsend.at[layer, c, span(j)], brecv.at[layer, c, span(j)], send.at[q + c], recv.at[q + c], (s, up))

    def collect(j):
        pair(j, True).wait_recv()
        for c in range(2):
            for side in (1, 0):
                relay(j, c, side, True).wait_recv()
        gather(j)
        for b in range(2):
            start(bottom_copy(j, b))
        start(top_copy(j))

    def finish(j):
        layer = chunks[j][0]
        top_copy(j).wait_recv()
        for c in range(2):
            bottom_in(j, c).wait_recv()
        for i in range(2):
            rows = span(j, i)
            done[layer, core, rows, :] = acc[layer, rows, :] + brecv[layer, core, rows, :].astype(F32)
            done[layer, other, rows, :] = (
                trecv[layer, rows, :].astype(F32) + brecv[layer, other, rows, :].astype(F32)
            )
        leaving = pltpu.make_async_copy(
            done.at[layer, :, span(j)], out_hbm.at[layer, :, span(j)], dma.at[6 + 2 * NS + j]
        )
        leaving.start()
        gone.append(leaving)

    share(1, arr, cur)
    launch(0)
    launch(1)

    def behind(rows, i):
        re, im = win[1, 0, rows, :], win[1, 1, rows, :]
        for m in range(2):
            cr, ci = cur[m, 0, rows, :], cur[m, 1, rows, :]
            put(m, rows, i, re * cr + im * ci, re * ci - im * cr)

    by_rows(behind)
    left_mul(e_c)
    right_mul(e_h, cur)

    def leave(rows, i):
        re, im = win[0, 0, rows, :], win[0, 1, rows, :]
        for m in range(2):
            cr, ci = cur[m, 0, rows, :], cur[m, 1, rows, :]
            esend[m, 0, rows, :] = (re * cr + im * ci).astype(BF)
            esend[m, 1, rows, :] = (re * ci - im * cr).astype(BF)

    by_rows(leave)
    q_pair, q_y, q_z, q_x = 67, 68, 71, 78
    e_copy = remote(esend.at[other], erecv, send.at[q_pair], recv.at[q_pair], (partner, o))
    start(e_copy)
    share(0, probe, cur)
    e_copy.wait_recv()

    def add_pair(rows, i):
        for part in range(2):
            ysend[part, rows, :] = (esend[core, part, rows, :].astype(F32) + erecv[part, rows, :].astype(F32)).astype(BF)

    by_rows(add_pair)
    deep = N // NY
    y_copies = []
    for k in range(1, NY):
        y_to = rem(y + k, NY)
        rows_to = pl.ds(pl.multiple_of(y_to * deep, deep), deep)
        copy = remote(
            ysend.at[:, rows_to, :], yrecv.at[k - 1], send.at[q_y + k - 1], recv.at[q_y + k - 1], (s, y_to * NZ + z)
        )
        start(copy)
        y_copies.append(copy)
    pass_on(0)
    launch(2)
    pass_on(1)
    launch(3)
    for copy in y_copies:
        copy.wait_recv()
    rows_me = pl.ds(pl.multiple_of(y * deep, deep), deep)
    totals = []
    for part in range(2):
        total = ysend[part, rows_me, :].astype(F32)
        for k in range(NY - 1):
            total = total + yrecv[k, part].astype(F32)
        totals.append(total)
    for k in range(NZ):
        zsend[k] = jnp.concatenate([total[8 * k : 8 * k + 8] for total in totals], axis=0).astype(BF)
    z_copies = []
    for k in range(1, NZ):
        z_to = rem(z + k, NZ)
        copy = remote(
            zsend.at[z_to], zrecv.at[k - 1], send.at[q_z + k - 1], recv.at[q_z + k - 1], (s, y * NZ + z_to)
        )
        start(copy)
        z_copies.append(copy)
    collect(0)
    pass_on(2)
    collect(1)
    for copy in z_copies:
        copy.wait_recv()
    total = zsend[z].astype(F32)
    for k in range(NZ - 1):
        total = total + zrecv[k].astype(F32)
    xall[0] = total.astype(BF)
    x_copies = []
    for k in range(1, NS):
        copy = remote(xall.at[0], xall.at[k], send.at[q_x + k - 1], recv.at[q_x + k - 1], (rem(s + k, NS), o))
        start(copy)
        x_copies.append(copy)
    pass_on(3)
    finish(0)
    collect(2)
    for copy in x_copies:
        copy.wait_recv()
    pick = one_hot((N, 128), lambda a, b: a == b + 32 * s)
    factor = 1.0 / math.sqrt(256.0)
    shares = [dot(xall[k], pick) for k in range(NS)]
    mine = (shares[0] + shares[2] + (shares[4] + shares[6])) * factor
    theirs = (shares[1] + shares[3] + (shares[5] + shares[7])) * factor
    for part in range(2):
        pout_ref[core, part] = mine[8 * part : 8 * part + 8, :32]
        pout_ref[other, part] = theirs[8 * part : 8 * part + 8, :32]
    finish(1)
    collect(3)
    finish(2)
    finish(3)
    for copy in gone:
        copy.wait()
    for copy in sends:
        copy.wait_send()


def hand_on(grad_ref, probe_ref, grad_out, probe_out):
    grad_out[...] = grad_ref[...]
    probe_out[...] = probe_ref[...]


def body(object_slices, probe, measured, positions, counts):
    vmem = pltpu.VMEM
    square = lambda *lead: (*lead, N, N)
    any_spec = pl.BlockSpec(memory_space=pl.ANY)
    results = pl.pallas_call(
        main_kernel,
        out_shape=(
            jax.ShapeDtypeStruct(square(2, 2), F32),
            jax.ShapeDtypeStruct((2, 2, 8, 32), F32),
        ),
        in_specs=[pl.BlockSpec(memory_space=pltpu.SMEM)] + [any_spec] * 5,
        out_specs=(any_spec, pl.BlockSpec(memory_space=vmem)),
        scratch_shapes=[
            pltpu.SMEM((2, 2), jnp.int32),
            vmem((1, 128), jnp.int32),
            vmem((2 * NS, 1, 128), jnp.int32),
            pltpu.SMEM((2 * NS, 1, 128), jnp.int32),
            *[vmem(square(NS, 2), F32)] * 2,
            vmem(square(2, 2), F32),
            vmem(square(16), BF),
            vmem(square(4), BF),
            *[vmem((2 * N, 2 * N), BF)] * 4,
            vmem(square(2, 2), BF),
            vmem(square(2, 2), BF),
            vmem(square(2, 2), BF),
            vmem(square(), BF),
            vmem(square(2, 2), F32),
            vmem((2 * N, 2 * N), BF),
            vmem((2 * N, 2 * N), BF),
            vmem(square(2, 2), F32),
            vmem(square(2, 2), F32),
            vmem(square(2, 2), F32),
            vmem(square(2, 2), BF),
            vmem(square(2, NS), BF),
            vmem(square(2), F32),
            vmem(square(2, 2), F32),
            vmem(square(2), BF),
            vmem(square(2), BF),
            vmem(square(2, 2), BF),
            vmem(square(2, 2), BF),
            vmem(square(2, 2), BF),
            vmem(square(2), BF),
            vmem(square(2), BF),
            vmem((NY - 1, 2, N // NY, N), BF),
            vmem((NZ, 16, N), BF),
            vmem((NZ - 1, 16, N), BF),
            vmem((NS, 16, N), BF),
            pltpu.SemaphoreType.DMA((10 + 2 * NS,)),
            pltpu.SemaphoreType.DMA((101,)),
            pltpu.SemaphoreType.DMA((101,)),
        ],
        compiler_params=pltpu.CompilerParams(
            collective_id=0, has_side_effects=True, vmem_limit_bytes=60 * 1024 * 1024
        ),
        name="gradient",
    )(counts, positions[0, 0], object_slices, probe, measured[0, 0], tables())
    plane = pl.BlockSpec((1, 1, N, N), lambda a, b: (a, b, 0, 0))
    whole = pl.BlockSpec((2, 2, 8, 32), lambda a, b: (0, 0, 0, 0))
    return pl.pallas_call(
        hand_on,
        out_shape=tuple(jax.ShapeDtypeStruct(r.shape, F32) for r in results),
        grid=(2, 2),
        in_specs=[plane, whole],
        out_specs=(plane, whole),
        name="results",
    )(*results)


def solution(mesh):
    return jax.shard_map(
        body,
        mesh=mesh,
        in_specs=(
            P(None, None, "obj", None),
            P(),
            P("scan", "obj", None, None, None),
            P("scan", "obj", None, None),
            P("scan", "obj"),
        ),
        out_specs=(P(None, None, "obj", "scan"), P(None, None, "obj", "scan")),
        check_vma=False,
    )
```

```python
import functools
import math

import jax
import jax.numpy as jnp
import numpy as np
from jax import lax
from jax.experimental import pallas as pl
from jax.experimental.pallas import tpu as pltpu
from jax.sharding import PartitionSpec as P

MESH = pl.DeviceIdType.MESH
BF = jnp.bfloat16
F32 = jnp.float32
N = 256
NS, NX, NO, NY, NZ = 8, 4, 32, 4, 8


def rem(a, b):
    return lax.rem(a, jnp.int32(b))


def tables():
    index = np.arange(N)
    angle = (np.outer(index, index) % N) * (2.0 * np.pi / N)
    rounded = lambda a: a.astype(np.float32).astype(BF)
    f_re, f_im = rounded(np.cos(angle) / 16.0), rounded(-np.sin(angle) / 16.0)
    fwd = f_re.astype(np.float64) + 1j * f_im.astype(np.float64)
    freq = np.where(index < N // 2, index, index - N)
    phase = np.exp(-2j * np.pi * ((freq * freq) % (4 * N)) / (4 * N))
    prop = np.conj(fwd) @ (phase[:, None] * fwd)
    return np.stack([f_re, f_im, rounded(prop.real), rounded(prop.imag)])


def remote(src, dst, send, recv, device):
    return pltpu.make_async_remote_copy(
        src_ref=src, dst_ref=dst, send_sem=send, recv_sem=recv, device_id=device, device_id_type=MESH
    )


def main_kernel(
    count_ref, pos_hbm, tile_hbm, probe_hbm, meas_hbm, table_hbm, out_hbm, pout_ref,
    pos_ref, row, rows_in, tab, tile_0, tile_1, probe, meas, tabs, e_f, e_i, e_h, e_c, hsend, hrecv, local, offer, offered, chosen, pattern, win, v, u, arr, far, cur,
    gsend, wins, acc, done, tsend, trecv, bsend, brecv, csend, crecv, esend, erecv, ysend, yrecv, zsend, zrecv, xall,
    dma, send, recv,
):
    s, o = lax.axis_index("scan"), lax.axis_index("obj")
    x, core = lax.div(s, jnp.int32(2)), rem(s, 2)
    y, z = lax.div(o, jnp.int32(NZ)), rem(o, NZ)
    other = 1 - core
    partner = 2 * x + other
    right = [2 * rem(x + 1, NX) + c for c in range(2)]
    left = [2 * rem(x + 3, NX) + c for c in range(2)]
    right_me, left_me = 2 * rem(x + 1, NX) + core, 2 * rem(x + 3, NX) + core
    x_left, x_right, x_far = rem(x + 3, NX), rem(x + 1, NX), rem(x + 2, NX)
    far_at = [2 * rem(x + 2, NX) + c for c in range(2)]
    up, down = rem(o + 1, NO), rem(o + NO - 1, NO)
    tile = (tile_0, tile_1)
    sends, gone = [], []

    barrier = pltpu.get_barrier_semaphore()
    peers = [(rem(s + k, NS), o) for k in range(1, NS)]
    peers += [(s, up), (partner, up)] + [(rem(s + k, NS), down) for k in range(NS)]
    peers += [(s, rem(y + k, NY) * NZ + z) for k in range(1, NY)]
    peers += [(s, y * NZ + rem(z + k, NZ)) for k in range(1, NZ)]
    for peer in peers:
        pl.semaphore_signal(barrier, inc=1, device_id=peer, device_id_type=MESH)

    given = pltpu.make_async_copy(pos_hbm, pos_ref, dma.at[4 + 2 * NS])
    given.start()
    loads = [
        pltpu.make_async_copy(table_hbm, tabs, dma.at[0]),
        pltpu.make_async_copy(probe_hbm, probe, dma.at[1]),
        pltpu.make_async_copy(meas_hbm, meas.at[pl.ds(2 * x, 2)], dma.at[2]),
    ]
    for layer in range(2):
        for b in range(NS):
            block = tile_hbm.at[layer, :, :, pl.ds(b * N, N)]
            loads.append(pltpu.make_async_copy(block, tile[layer].at[b], dma.at[3 + NS * layer + b]))
    for load in loads:
        load.start()

    lane = lax.broadcasted_iota(jnp.int32, (1, 128), 1)
    given.wait()
    line = jnp.zeros((1, 128), jnp.int32)
    for j, value in enumerate((pos_ref[0, 0], pos_ref[0, 1], pos_ref[1, 0], pos_ref[1, 1], count_ref[0, 0])):
        line = jnp.where(lane == j, value, line)
    row[...] = line
    rows_in[s] = line

    def one_hot(shape, rule):
        a, b = lax.broadcasted_iota(jnp.int32, shape, 0), lax.broadcasted_iota(jnp.int32, shape, 1)
        return jnp.where(rule(a, b), 1.0, 0.0).astype(BF)

    def dot(a, b):
        return jnp.dot(a, b, preferred_element_type=F32)

    def col_block(col):
        k = jnp.int32(0)
        for edge in range(1, NS - 1):
            k = k + jnp.where(col >= edge * N, 1, 0)
        return k

    def picks(offset):
        return [one_hot((N, N), lambda a, b: a + h * N == b + offset) for h in range(2)]

    def columns(layer, part, k, pick):
        first, second = tile[layer][k, part].astype(BF), tile[layer][k + 1, part].astype(BF)
        return (dot(first, pick[0]) + dot(second, pick[1])).astype(BF)


    pl.semaphore_wait(barrier, len(peers))

    def start(copy):
        copy.start()
        sends.append(copy)

    def meas_copy(q, slot, n, peer):
        ref = meas.at[pl.ds(slot, n)]
        return remote(ref, ref, send.at[q], recv.at[q], (peer, o))

    def place_copy(k, base, owner):
        peer = (rem(s + k, NS), up if base else o)
        return remote(row, rows_in.at[base + owner], send.at[93 + base + k], recv.at[93 + base + k], peer)

    every = [(k, base) for base in (0, NS) for k in range(NS) if base or k]
    for k, base in every:
        start(place_copy(k, base, s))
    for q, peer in ((1, right_me), (2, left_me)):
        start(remote(meas_hbm, meas.at[pl.ds(2 * x, 2)], send.at[q], recv.at[q], (peer, o)))
    loads[0].wait()
    for e_ref, re, im, sign in ((e_f, 0, 1, 1), (e_i, 0, 1, -1), (e_h, 2, 3, 1), (e_c, 2, 3, -1)):
        e_ref[0:N, 0:N] = tabs[re]
        e_ref[N:, N:] = tabs[re]
        e_ref[0:N, N:] = -tabs[im] if sign > 0 else tabs[im]
        e_ref[N:, 0:N] = tabs[im] if sign > 0 else -tabs[im]

    for k, base in every:
        place_copy(k, base, rem(s + NS - k, NS)).wait_recv()
    fetch = pltpu.make_async_copy(rows_in, tab, dma.at[3 + 2 * NS])
    fetch.start()
    fetch.wait()

    def assigned(base, n):
        begin, found = jnp.int32(0), [jnp.int32(0)] * 4
        for t in range(NS):
            count = tab[base + t, 0, 4]
            for k in range(2):
                hit = (k < count) & (begin + k == n)
                values = (jnp.int32(t % 2), jnp.int32(2 * (t // 2) + k), tab[base + t, 0, 2 * k], tab[base + t, 0, 2 * k + 1])
                for j, value in enumerate(values):
                    found[j] = jnp.where(hit, value, found[j])
            begin = begin + count
        return found

    _, _, _, col_out = assigned(NS * other, x + NX * core)
    k_out = col_block(col_out)
    pick_out = picks(col_out - k_out * N)
    halo_to = jnp.where(core == 0, down, up)

    def halo_copy(layer):
        return remote(hsend.at[layer], hrecv.at[layer], send.at[9 + layer], recv.at[9 + layer], (s, halo_to))

    for layer in range(2):
        for b in range(NS):
            loads[3 + NS * layer + b].wait()
        for part in range(2):
            hsend[layer, part] = columns(layer, part, k_out, pick_out)
        start(halo_copy(layer))
    _, _, row0, col0 = assigned(NS * core, x + NX * core)
    k_own = col_block(col0)
    pick_own = picks(col0 - k_own * N)
    for layer in range(2):
        for part in range(2):
            local[layer, part] = columns(layer, part, k_own, pick_own)
    places = [assigned(NS * (d % 2), d // 2 + NX * (d % 2))[2:] for d in range(NS)]
    half_has, slot_has, _, _ = assigned(0, x + NX * core)
    _, slot_other, _, _ = assigned(0, x + NX * other)
    rows_own = one_hot((N, N), lambda a, b: b + N * core == a + row0)
    rows_halo = one_hot((N, N), lambda a, b: b + N * other == a + row0)
    turn = jnp.where(col0 == 7 * N, 0, col0 - k_own * N)
    turn_rows = one_hot((N, N), lambda a, b: (b + row0 == a) | (b + row0 == a + N))
    turn_cols = one_hot((N, N), lambda a, b: (a + turn == b) | (a + turn == b + N))
    loads[1].wait()

    def window(layer):
        halo_copy(layer).wait_recv()
        for part in range(2):
            win[layer, part] = dot(rows_own, local[layer, part]) + dot(rows_halo, hrecv[layer, part])

    step = 32

    def by_rows(body):
        def run(i, carry):
            body(pl.ds(pl.multiple_of(i * step, step), step), i)
            return carry

        lax.fori_loop(0, N // step, run, 0)

    def put(m, rows, i, re, im):
        v[pl.ds(pl.multiple_of(i * step, step), step), m * N : (m + 1) * N] = re.astype(BF)
        v[pl.ds(pl.multiple_of(N + i * step, step), step), m * N : (m + 1) * N] = im.astype(BF)

    def left_mul(matrix):
        for m in range(2):
            product = dot(matrix[...], v[:, m * N : (m + 1) * N])
            u[m * N : (m + 1) * N, 0:N] = product[0:N].astype(BF)
            u[m * N : (m + 1) * N, N:] = product[N:].astype(BF)

    def right_mul(matrix, result):
        for part in range(2):
            product = dot(u[...], matrix[:, part * N : (part + 1) * N])
            result[0, part] = product[0:N]
            result[1, part] = product[N:]

    meas_copy(1, 2 * x_left, 2, right_me).wait_recv()
    start(meas_copy(3, 2 * x_left, 1, right_me))
    meas_copy(2, 2 * x_right, 2, left_me).wait_recv()
    start(meas_copy(5, 2 * x_right + 1, 1, left_me))

    window(0)

    def enter(rows, i):
        re, im = win[0, 0, rows, :], win[0, 1, rows, :]
        for m in range(2):
            pr, pi = probe[m, 0, rows, :], probe[m, 1, rows, :]
            put(m, rows, i, pr * re - pi * im, pr * im + pi * re)

    by_rows(enter)
    meas_copy(3, 2 * x_far, 1, right_me).wait_recv()
    meas_copy(5, 2 * x_far + 1, 1, left_me).wait_recv()
    loads[2].wait()
    offer[...] = meas[slot_other]
    offer_copy = remote(offer, offered, send.at[0], recv.at[0], (partner, o))
    start(offer_copy)
    left_mul(e_h)
    right_mul(e_c, arr)
    offer_copy.wait_recv()
    chosen[...] = jnp.where(half_has == core, meas[slot_has], offered[...])
    rise = remote(chosen, pattern, send.at[4], recv.at[4], (s, up))

    @pl.when(core == 1)
    def _():
        rise.start()

    window(1)

    def second(rows, i):
        re, im = win[1, 0, rows, :], win[1, 1, rows, :]
        for m in range(2):
            pr, pi = arr[m, 0, rows, :], arr[m, 1, rows, :]
            put(m, rows, i, pr * re - pi * im, pr * im + pi * re)

    by_rows(second)
    left_mul(e_f)
    right_mul(e_i, far)

    @pl.when(core == 0)
    def _():
        pattern[...] = chosen[...]

    @pl.when(core == 1)
    def _():
        rise.wait_recv()

    def misfit(rows, i):
        parts = [(far[m, 0, rows, :], far[m, 1, rows, :]) for m in range(2)]
        total = parts[0][0] ** 2 + parts[0][1] ** 2 + (parts[1][0] ** 2 + parts[1][1] ** 2)
        gap = total - pattern[rows, :].astype(F32)
        for m in range(2):
            put(m, rows, i, gap * parts[m][0], gap * parts[m][1])

    by_rows(misfit)
    left_mul(e_i)
    right_mul(e_f, cur)

    half = N // 2
    chunks = [(1, 0), (1, 1), (0, 0), (0, 1)]

    def span(j, part=None):
        first = chunks[j][1] * half
        return pl.ds(first, half) if part is None else pl.ds(first + part * half // 2, half // 2)

    def near(j, c, side):
        layer, q = chunks[j][0], 11 + 16 * j + (2 if side else 4)
        peer = (right if side else left)[c]
        return remote(
            gsend.at[layer, c, span(j)], wins.at[layer, s, span(j)], send.at[q + c], recv.at[q + core], (peer, o)
        )

    def near_in(j, c, side):
        layer, q = chunks[j][0], 11 + 16 * j + (2 if side else 4)
        slot = wins.at[layer, (left if side else right)[c], span(j)]
        return remote(slot, slot, send.at[q + c], recv.at[q + c], (partner, o))

    def relay(j, c, side, incoming=False):
        q = 11 + 16 * j + (6 if side else 8) + c
        owner = far_at[c] if incoming else (left if side else right)[c]
        piece = wins.at[chunks[j][0], owner, span(j, 0 if side else 1)]
        return remote(piece, piece, send.at[q], recv.at[q], (right_me if side else left_me, o))

    def pair(j, incoming=False):
        layer, q = chunks[j][0], 11 + 16 * j
        slot = wins.at[layer, partner if incoming else s, span(j)]
        return remote(gsend.at[layer, other, span(j)], slot, send.at[q], recv.at[q], (partner, o))

    def share(layer, first, adjoint):
        for part in range(2):
            if part == 0:
                term = lambda m: first[m, 0] * adjoint[m, 0] + first[m, 1] * adjoint[m, 1]
            else:
                term = lambda m: first[m, 0] * adjoint[m, 1] - first[m, 1] * adjoint[m, 0]
            grad = (term(0) + term(1)).astype(BF)
            gsend[layer, part] = dot(dot(turn_rows, grad).astype(BF), turn_cols).astype(BF)
        wins[layer, s] = gsend[layer, core]

    def launch(j):
        for c in range(2):
            start(near(j, c, 1))
            start(near(j, c, 0))
        start(pair(j))

    def pass_on(j):
        for c in range(2):
            for side in (1, 0):
                near_in(j, c, side).wait_recv()
                start(relay(j, c, side))

    lane = lax.broadcasted_iota(jnp.int32, (1, N), 1)
    cols = [
        [jnp.where((lane + (2 * x + b) * N >= c0) & (lane + (2 * x + b) * N < c0 + N), 1.0, 0.0) for b in range(2)]
        for _, c0 in places
    ]

    def gather(j):
        layer, first = chunks[j][0], chunks[j][1] * half
        chunk = 16

        def run(i, carry):
            at = pl.multiple_of(first + i * chunk, chunk)
            rows = pl.ds(at, chunk)
            line = lax.broadcasted_iota(jnp.int32, (chunk, N), 0) + at
            sums = [[jnp.zeros((chunk, N), F32) for _ in range(3)] for _ in range(2)]
            for n in range(NS):
                term = wins[layer, n, rows, :].astype(F32)
                above = line >= places[n][0]
                for b in range(2):
                    masked = term * cols[n][b]
                    low, high = (2, 0) if n % 2 else (0, 1)
                    sums[b][low] = sums[b][low] + jnp.where(above, masked, 0.0)
                    sums[b][high] = sums[b][high] + jnp.where(above, 0.0, masked)
            mine = core == 0
            acc[layer, rows, :] = jnp.where(mine, sums[0][0], sums[1][0])
            tsend[layer, rows, :] = jnp.where(mine, sums[1][0], sums[0][0]).astype(BF)
            for b in range(2):
                bsend[layer, b, rows, :] = sums[b][1].astype(BF)
                csend[layer, b, rows, :] = sums[b][2].astype(BF)
            return carry

        lax.fori_loop(0, half // chunk, run, 0)

    def top_copy(j):
        layer, q = chunks[j][0], 21 + 16 * j
        return remote(tsend.at[layer, span(j)], trecv.at[layer, span(j)], send.at[q], recv.at[q], (partner, o))

    def edge(j, upward):
        q = 22 + 16 * j + (0 if upward else 2)
        return (bsend, brecv, q, up) if upward else (csend, crecv, q, down)

    def edge_copy(j, b, upward):
        layer, (source, target, q, to) = chunks[j][0], edge(j, upward)
        return remote(
            source.at[layer, b, span(j)], target.at[layer, core, span(j)], send.at[q + b], recv.at[q + core], (2 * x + b, to)
        )

    def edge_in(j, c, upward):
        layer, (source, target, q, to) = chunks[j][0], edge(j, upward)
        return remote(source.at[layer, c, span(j)], target.at[layer, c, span(j)], send.at[q + c], recv.at[q + c], (s, to))

    def collect(j):
        pair(j, True).wait_recv()
        for c in range(2):
            for side in (1, 0):
                relay(j, c, side, True).wait_recv()
        gather(j)
        for b in range(2):
            start(edge_copy(j, b, True))
            start(edge_copy(j, b, False))
        start(top_copy(j))

    def finish(j):
        layer = chunks[j][0]
        top_copy(j).wait_recv()
        for c in range(2):
            edge_in(j, c, True).wait_recv()
            edge_in(j, c, False).wait_recv()
        for i in range(2):
            rows = span(j, i)
            rims = [brecv[layer, c, rows, :].astype(F32) + crecv[layer, c, rows, :].astype(F32) for c in (core, other)]
            done[layer, core, rows, :] = acc[layer, rows, :] + rims[0]
            done[layer, other, rows, :] = trecv[layer, rows, :].astype(F32) + rims[1]
        leaving = pltpu.make_async_copy(
            done.at[layer, :, span(j)], out_hbm.at[layer, :, span(j)], dma.at[6 + 2 * NS + j]
        )
        leaving.start()
        gone.append(leaving)

    share(1, arr, cur)
    launch(0)
    launch(1)

    def behind(rows, i):
        re, im = win[1, 0, rows, :], win[1, 1, rows, :]
        for m in range(2):
            cr, ci = cur[m, 0, rows, :], cur[m, 1, rows, :]
            put(m, rows, i, re * cr + im * ci, re * ci - im * cr)

    by_rows(behind)
    left_mul(e_c)
    right_mul(e_h, cur)

    def leave(rows, i):
        re, im = win[0, 0, rows, :], win[0, 1, rows, :]
        for m in range(2):
            cr, ci = cur[m, 0, rows, :], cur[m, 1, rows, :]
            esend[m, 0, rows, :] = (re * cr + im * ci).astype(BF)
            esend[m, 1, rows, :] = (re * ci - im * cr).astype(BF)

    by_rows(leave)
    q_pair, q_y, q_z, q_x = 75, 76, 79, 86
    e_copy = remote(esend.at[other], erecv, send.at[q_pair], recv.at[q_pair], (partner, o))
    start(e_copy)
    share(0, probe, cur)
    e_copy.wait_recv()

    def add_pair(rows, i):
        for part in range(2):
            ysend[part, rows, :] = (esend[core, part, rows, :].astype(F32) + erecv[part, rows, :].astype(F32)).astype(BF)

    by_rows(add_pair)
    deep = N // NY
    y_copies = []
    for k in range(1, NY):
        y_to = rem(y + k, NY)
        rows_to = pl.ds(pl.multiple_of(y_to * deep, deep), deep)
        copy = remote(
            ysend.at[:, rows_to, :], yrecv.at[k - 1], send.at[q_y + k - 1], recv.at[q_y + k - 1], (s, y_to * NZ + z)
        )
        start(copy)
        y_copies.append(copy)
    pass_on(0)
    launch(2)
    pass_on(1)
    launch(3)
    for copy in y_copies:
        copy.wait_recv()
    rows_me = pl.ds(pl.multiple_of(y * deep, deep), deep)
    totals = []
    for part in range(2):
        total = ysend[part, rows_me, :].astype(F32)
        for k in range(NY - 1):
            total = total + yrecv[k, part].astype(F32)
        totals.append(total)
    for k in range(NZ):
        zsend[k] = jnp.concatenate([total[8 * k : 8 * k + 8] for total in totals], axis=0).astype(BF)
    z_copies = []
    for k in range(1, NZ):
        z_to = rem(z + k, NZ)
        copy = remote(
            zsend.at[z_to], zrecv.at[k - 1], send.at[q_z + k - 1], recv.at[q_z + k - 1], (s, y * NZ + z_to)
        )
        start(copy)
        z_copies.append(copy)
    collect(0)
    pass_on(2)
    collect(1)
    for copy in z_copies:
        copy.wait_recv()
    total = zsend[z].astype(F32)
    for k in range(NZ - 1):
        total = total + zrecv[k].astype(F32)
    xall[0] = total.astype(BF)
    x_copies = []
    for k in range(1, NS):
        copy = remote(xall.at[0], xall.at[k], send.at[q_x + k - 1], recv.at[q_x + k - 1], (rem(s + k, NS), o))
        start(copy)
        x_copies.append(copy)
    pass_on(3)
    finish(0)
    collect(2)
    for copy in x_copies:
        copy.wait_recv()
    pick = one_hot((N, 128), lambda a, b: a == b + 32 * s)
    factor = 1.0 / math.sqrt(256.0)
    shares = [dot(xall[k], pick) for k in range(NS)]
    mine = (shares[0] + shares[2] + (shares[4] + shares[6])) * factor
    theirs = (shares[1] + shares[3] + (shares[5] + shares[7])) * factor
    for part in range(2):
        pout_ref[core, part] = mine[8 * part : 8 * part + 8, :32]
        pout_ref[other, part] = theirs[8 * part : 8 * part + 8, :32]
    finish(1)
    collect(3)
    finish(2)
    finish(3)
    for copy in gone:
        copy.wait()
    for copy in sends:
        copy.wait_send()

    @pl.when(core == 1)
    def _():
        rise.wait_send()


def hand_on(grad_hbm, probe_hbm, grad_out, probe_out, held, probe_held, sem):
    moves = [(grad_hbm.at[a], held.at[a], grad_out.at[a]) for a in range(4)] + [(probe_hbm, probe_held, probe_out)]
    inward = [pltpu.make_async_copy(source, kept, sem.at[i]) for i, (source, kept, _) in enumerate(moves)]
    outward = [pltpu.make_async_copy(kept, target, sem.at[5 + i]) for i, (_, kept, target) in enumerate(moves)]
    for copy in inward:
        copy.start()
    for copy, after in zip(inward, outward):
        copy.wait()
        after.start()
    for copy in outward:
        copy.wait()


def body(object_slices, probe, measured, positions, counts):
    vmem = pltpu.VMEM
    square = lambda *lead: (*lead, N, N)
    any_spec = pl.BlockSpec(memory_space=pl.ANY)
    results = pl.pallas_call(
        main_kernel,
        out_shape=(
            jax.ShapeDtypeStruct(square(2, 2), F32),
            jax.ShapeDtypeStruct((2, 2, 8, 32), F32),
        ),
        in_specs=[pl.BlockSpec(memory_space=pltpu.SMEM)] + [any_spec] * 5,
        out_specs=(any_spec, pl.BlockSpec(memory_space=vmem)),
        scratch_shapes=[
            pltpu.SMEM((2, 2), jnp.int32),
            vmem((1, 128), jnp.int32),
            vmem((2 * NS, 1, 128), jnp.int32),
            pltpu.SMEM((2 * NS, 1, 128), jnp.int32),
            *[vmem(square(NS, 2), F32)] * 2,
            vmem(square(2, 2), F32),
            vmem(square(2 * NX), BF),
            vmem(square(4), BF),
            *[vmem((2 * N, 2 * N), BF)] * 4,
            vmem(square(2, 2), BF),
            vmem(square(2, 2), BF),
            vmem(square(2, 2), BF),
            *[vmem(square(), BF)] * 4,
            vmem(square(2, 2), F32),
            vmem((2 * N, 2 * N), BF),
            vmem((2 * N, 2 * N), BF),
            vmem(square(2, 2), F32),
            vmem(square(2, 2), F32),
            vmem(square(2, 2), F32),
            vmem(square(2, 2), BF),
            vmem(square(2, NS), BF),
            vmem(square(2), F32),
            vmem(square(2, 2), F32),
            vmem(square(2), BF),
            vmem(square(2), BF),
            *[vmem(square(2, 2), BF)] * 4,
            vmem(square(2, 2), BF),
            vmem(square(2), BF),
            vmem(square(2), BF),
            vmem((NY - 1, 2, N // NY, N), BF),
            vmem((NZ, 16, N), BF),
            vmem((NZ - 1, 16, N), BF),
            vmem((NS, 16, N), BF),
            pltpu.SemaphoreType.DMA((10 + 2 * NS,)),
            pltpu.SemaphoreType.DMA((109,)),
            pltpu.SemaphoreType.DMA((109,)),
        ],
        compiler_params=pltpu.CompilerParams(
            collective_id=0, has_side_effects=True, vmem_limit_bytes=60 * 1024 * 1024
        ),
        name="gradient",
    )(counts, positions[0, 0], object_slices, probe, measured[0, 0], tables())
    grad, probe_grad = pl.pallas_call(
        hand_on,
        out_shape=(jax.ShapeDtypeStruct(square(4), F32), jax.ShapeDtypeStruct((2, 2, 8, 32), F32)),
        in_specs=[any_spec] * 2,
        out_specs=(any_spec, any_spec),
        scratch_shapes=[vmem(square(4), F32), vmem((2, 2, 8, 32), F32), pltpu.SemaphoreType.DMA((10,))],
        name="results",
    )(results[0].reshape(square(4)), results[1])
    return grad.reshape(square(2, 2)), probe_grad


def solution(mesh):
    return jax.shard_map(
        body,
        mesh=mesh,
        in_specs=(
            P(None, None, "obj", None),
            P(),
            P("scan", "obj", None, None, None),
            P("scan", "obj", None, None),
            P("scan", "obj"),
        ),
        out_specs=(P(None, None, "obj", "scan"), P(None, None, "obj", "scan")),
        check_vma=False,
    )
```

```python
import functools
import math

import jax
import jax.numpy as jnp
import numpy as np
from jax import lax
from jax.experimental import pallas as pl
from jax.experimental.pallas import tpu as pltpu
from jax.sharding import PartitionSpec as P

MESH = pl.DeviceIdType.MESH
BF = jnp.bfloat16
F32 = jnp.float32
N = 256
NS, NX, NO, NY, NZ = 8, 4, 32, 4, 8


def rem(a, b):
    return lax.rem(a, jnp.int32(b))


def tables():
    index = np.arange(N)
    angle = (np.outer(index, index) % N) * (2.0 * np.pi / N)
    rounded = lambda a: a.astype(np.float32).astype(BF)
    f_re, f_im = rounded(np.cos(angle) / 16.0), rounded(-np.sin(angle) / 16.0)
    fwd = f_re.astype(np.float64) + 1j * f_im.astype(np.float64)
    freq = np.where(index < N // 2, index, index - N)
    phase = np.exp(-2j * np.pi * ((freq * freq) % (4 * N)) / (4 * N))
    prop = np.conj(fwd) @ (phase[:, None] * fwd)
    return np.stack([f_re, f_im, rounded(prop.real), rounded(prop.imag)])


def remote(src, dst, send, recv, device):
    return pltpu.make_async_remote_copy(
        src_ref=src, dst_ref=dst, send_sem=send, recv_sem=recv, device_id=device, device_id_type=MESH
    )


def main_kernel(
    count_ref, pos_hbm, tile_hbm, probe_hbm, meas_hbm, table_hbm, out_hbm, pout_ref,
    pos_ref, row, rows_in, tab, tile_0, tile_1, probe, meas, tabs, e_f, e_i, e_h, e_c, hsend, hrecv, local, offer, offered, rising, risen, pattern, win, v, u, arr, far, cur,
    gsend, wins, acc, done, tsend, trecv, bsend, brecv, csend, crecv, esend, erecv, ysend, yrecv, zsend, zrecv, xall,
    dma, send, recv,
):
    s, o = lax.axis_index("scan"), lax.axis_index("obj")
    x, core = lax.div(s, jnp.int32(2)), rem(s, 2)
    y, z = lax.div(o, jnp.int32(NZ)), rem(o, NZ)
    other = 1 - core
    partner = 2 * x + other
    right = [2 * rem(x + 1, NX) + c for c in range(2)]
    left = [2 * rem(x + 3, NX) + c for c in range(2)]
    right_me, left_me = 2 * rem(x + 1, NX) + core, 2 * rem(x + 3, NX) + core
    x_left, x_right, x_far = rem(x + 3, NX), rem(x + 1, NX), rem(x + 2, NX)
    far_at = [2 * rem(x + 2, NX) + c for c in range(2)]
    up, down = rem(o + 1, NO), rem(o + NO - 1, NO)
    tile = (tile_0, tile_1)
    sends, gone = [], []

    barrier = pltpu.get_barrier_semaphore()
    peers = [(rem(s + k, NS), o) for k in range(1, NS)]
    peers += [(s, up), (partner, up)] + [(rem(s + k, NS), down) for k in range(NS)]
    peers += [(s, rem(y + k, NY) * NZ + z) for k in range(1, NY)]
    peers += [(s, y * NZ + rem(z + k, NZ)) for k in range(1, NZ)]
    for peer in peers:
        pl.semaphore_signal(barrier, inc=1, device_id=peer, device_id_type=MESH)

    given = pltpu.make_async_copy(pos_hbm, pos_ref, dma.at[4 + 2 * NS])
    given.start()
    loads = [
        pltpu.make_async_copy(table_hbm, tabs, dma.at[0]),
        pltpu.make_async_copy(probe_hbm, probe, dma.at[1]),
        pltpu.make_async_copy(meas_hbm, meas.at[pl.ds(2 * x, 2)], dma.at[2]),
    ]
    for layer in range(2):
        for b in range(NS):
            block = tile_hbm.at[layer, :, :, pl.ds(b * N, N)]
            loads.append(pltpu.make_async_copy(block, tile[layer].at[b], dma.at[3 + NS * layer + b]))
    for load in loads:
        load.start()

    lane = lax.broadcasted_iota(jnp.int32, (1, 128), 1)
    given.wait()
    line = jnp.zeros((1, 128), jnp.int32)
    for j, value in enumerate((pos_ref[0, 0], pos_ref[0, 1], pos_ref[1, 0], pos_ref[1, 1], count_ref[0, 0])):
        line = jnp.where(lane == j, value, line)
    row[...] = line
    rows_in[s] = line

    def one_hot(shape, rule):
        a, b = lax.broadcasted_iota(jnp.int32, shape, 0), lax.broadcasted_iota(jnp.int32, shape, 1)
        return jnp.where(rule(a, b), 1.0, 0.0).astype(BF)

    def dot(a, b):
        return jnp.dot(a, b, preferred_element_type=F32)

    def col_block(col):
        k = jnp.int32(0)
        for edge in range(1, NS - 1):
            k = k + jnp.where(col >= edge * N, 1, 0)
        return k

    def picks(offset):
        return [one_hot((N, N), lambda a, b: a + h * N == b + offset) for h in range(2)]

    def columns(layer, part, k, pick):
        first, second = tile[layer][k, part].astype(BF), tile[layer][k + 1, part].astype(BF)
        return (dot(first, pick[0]) + dot(second, pick[1])).astype(BF)


    pl.semaphore_wait(barrier, len(peers))

    def start(copy):
        copy.start()
        sends.append(copy)

    def meas_copy(q, slot, n, peer):
        ref = meas.at[pl.ds(slot, n)]
        return remote(ref, ref, send.at[q], recv.at[q], (peer, o))

    def place_copy(k, base, owner):
        peer = (rem(s + k, NS), up if base else o)
        return remote(row, rows_in.at[base + owner], send.at[93 + base + k], recv.at[93 + base + k], peer)

    every = [(k, base) for base in (0, NS) for k in range(NS) if base or k]
    for k, base in every:
        start(place_copy(k, base, s))
    for q, k, peer in ((1, 0, right_me), (2, 1, left_me), (6, 1, right_me), (7, 0, left_me)):
        start(remote(meas_hbm.at[pl.ds(k, 1)], meas.at[pl.ds(2 * x + k, 1)], send.at[q], recv.at[q], (peer, o)))
    loads[0].wait()
    for e_ref, re, im, sign in ((e_f, 0, 1, 1), (e_i, 0, 1, -1), (e_h, 2, 3, 1), (e_c, 2, 3, -1)):
        e_ref[0:N, 0:N] = tabs[re]
        e_ref[N:, N:] = tabs[re]
        e_ref[0:N, N:] = -tabs[im] if sign > 0 else tabs[im]
        e_ref[N:, 0:N] = tabs[im] if sign > 0 else -tabs[im]

    for k, base in every:
        place_copy(k, base, rem(s + NS - k, NS)).wait_recv()
    fetch = pltpu.make_async_copy(rows_in, tab, dma.at[3 + 2 * NS])
    fetch.start()
    fetch.wait()

    def assigned(base, n):
        begin, found = jnp.int32(0), [jnp.int32(0)] * 4
        for t in range(NS):
            count = tab[base + t, 0, 4]
            for k in range(2):
                hit = (k < count) & (begin + k == n)
                values = (jnp.int32(t % 2), jnp.int32(2 * (t // 2) + k), tab[base + t, 0, 2 * k], tab[base + t, 0, 2 * k + 1])
                for j, value in enumerate(values):
                    found[j] = jnp.where(hit, value, found[j])
            begin = begin + count
        return found

    _, _, _, col_out = assigned(NS * other, x + NX * core)
    k_out = col_block(col_out)
    pick_out = picks(col_out - k_out * N)
    halo_to = jnp.where(core == 0, down, up)

    def halo_copy(layer, part):
        q = 111 + 2 * layer + part
        return remote(hsend.at[layer, part], hrecv.at[layer, part], send.at[q], recv.at[q], (s, halo_to))

    for layer in range(2):
        for b in range(NS):
            loads[3 + NS * layer + b].wait()
        for part in range(2):
            hsend[layer, part] = columns(layer, part, k_out, pick_out)
            start(halo_copy(layer, part))
    meas_copy(1, 2 * x_left, 1, right_me).wait_recv()
    start(meas_copy(3, 2 * x_left, 1, right_me))
    meas_copy(2, 2 * x_right + 1, 1, left_me).wait_recv()
    start(meas_copy(5, 2 * x_right + 1, 1, left_me))
    half_mine, slot_mine, row0, col0 = assigned(NS * core, x + NX * core)
    k_own = col_block(col0)
    pick_own = picks(col0 - k_own * N)
    for layer in range(2):
        for part in range(2):
            local[layer, part] = columns(layer, part, k_own, pick_own)
    places = [assigned(NS * (d % 2), d // 2 + NX * (d % 2))[2:] for d in range(NS)]
    _, slot_a, _, _ = assigned(0, x)
    _, slot_b, _, _ = assigned(0, x + NX)
    rows_own = one_hot((N, N), lambda a, b: b + N * core == a + row0)
    rows_halo = one_hot((N, N), lambda a, b: b + N * other == a + row0)
    turn = jnp.where(col0 == 7 * N, 0, col0 - k_own * N)
    turn_rows = one_hot((N, N), lambda a, b: (b + row0 == a) | (b + row0 == a + N))
    turn_cols = one_hot((N, N), lambda a, b: (a + turn == b) | (a + turn == b + N))
    loads[1].wait()

    def window(layer):
        for part in range(2):
            halo_copy(layer, part).wait_recv()
            win[layer, part] = dot(rows_own, local[layer, part]) + dot(rows_halo, hrecv[layer, part])

    step = 32

    def by_rows(body):
        def run(i, carry):
            body(pl.ds(pl.multiple_of(i * step, step), step), i)
            return carry

        lax.fori_loop(0, N // step, run, 0)

    def put(m, rows, i, re, im):
        v[pl.ds(pl.multiple_of(i * step, step), step), m * N : (m + 1) * N] = re.astype(BF)
        v[pl.ds(pl.multiple_of(N + i * step, step), step), m * N : (m + 1) * N] = im.astype(BF)

    def left_mul(matrix):
        for m in range(2):
            product = dot(matrix[...], v[:, m * N : (m + 1) * N])
            u[m * N : (m + 1) * N, 0:N] = product[0:N].astype(BF)
            u[m * N : (m + 1) * N, N:] = product[N:].astype(BF)

    def right_mul(matrix, result):
        for part in range(2):
            product = dot(u[...], matrix[:, part * N : (part + 1) * N])
            result[0, part] = product[0:N]
            result[1, part] = product[N:]

    window(0)

    def enter(rows, i):
        re, im = win[0, 0, rows, :], win[0, 1, rows, :]
        for m in range(2):
            pr, pi = probe[m, 0, rows, :], probe[m, 1, rows, :]
            put(m, rows, i, pr * re - pi * im, pr * im + pi * re)

    by_rows(enter)
    for q, slot, peer in ((3, 2 * x_far, right_me), (5, 2 * x_far + 1, left_me), (6, 2 * x_left + 1, right_me), (7, 2 * x_right, left_me)):
        meas_copy(q, slot, 1, peer).wait_recv()
    loads[2].wait()
    rising[...] = meas[slot_b]
    start(remote(rising, risen.at[core], send.at[109], recv.at[109 + core], (2 * x + 1, up)))
    offer[...] = meas[slot_a]
    offer_copy = remote(offer, offered, send.at[0], recv.at[0], (2 * x, o))

    @pl.when(core == 1)
    def _():
        offer_copy.start()

    left_mul(e_h)
    right_mul(e_c, arr)
    window(1)

    def second(rows, i):
        re, im = win[1, 0, rows, :], win[1, 1, rows, :]
        for m in range(2):
            pr, pi = arr[m, 0, rows, :], arr[m, 1, rows, :]
            put(m, rows, i, pr * re - pi * im, pr * im + pi * re)

    by_rows(second)
    left_mul(e_f)
    right_mul(e_i, far)

    @pl.when(core == 0)
    def _():
        offer_copy.wait_recv()
        pattern[...] = jnp.where(half_mine == 0, offer[...], offered[...])

    @pl.when(core == 1)
    def _():
        for c in range(2):
            remote(rising, risen.at[c], send.at[109], recv.at[109 + c], (s, up)).wait_recv()
        pattern[...] = jnp.where(half_mine == 0, risen[0], risen[1])

    def misfit(rows, i):
        parts = [(far[m, 0, rows, :], far[m, 1, rows, :]) for m in range(2)]
        total = parts[0][0] ** 2 + parts[0][1] ** 2 + (parts[1][0] ** 2 + parts[1][1] ** 2)
        gap = total - pattern[rows, :].astype(F32)
        for m in range(2):
            put(m, rows, i, gap * parts[m][0], gap * parts[m][1])

    by_rows(misfit)
    left_mul(e_i)
    right_mul(e_f, cur)

    chunks = [(1, 0, 128), (1, 128, 128), (0, 0, 160), (0, 160, 96)]

    def span(j, part=None):
        _, first, size = chunks[j]
        return pl.ds(first, size) if part is None else pl.ds(first + part * size // 2, size // 2)

    def near(j, c, side):
        layer, q = chunks[j][0], 11 + 16 * j + (2 if side else 4)
        peer = (right if side else left)[c]
        return remote(
            gsend.at[layer, c, span(j)], wins.at[layer, s, span(j)], send.at[q + c], recv.at[q + core], (peer, o)
        )

    def near_in(j, c, side):
        layer, q = chunks[j][0], 11 + 16 * j + (2 if side else 4)
        slot = wins.at[layer, (left if side else right)[c], span(j)]
        return remote(slot, slot, send.at[q + c], recv.at[q + c], (partner, o))

    def relay(j, c, side, incoming=False):
        q = 11 + 16 * j + (6 if side else 8) + c
        owner = far_at[c] if incoming else (left if side else right)[c]
        piece = wins.at[chunks[j][0], owner, span(j, 0 if side else 1)]
        return remote(piece, piece, send.at[q], recv.at[q], (right_me if side else left_me, o))

    def pair(j, incoming=False):
        layer, q = chunks[j][0], 11 + 16 * j
        slot = wins.at[layer, partner if incoming else s, span(j)]
        return remote(gsend.at[layer, other, span(j)], slot, send.at[q], recv.at[q], (partner, o))

    def share(layer, first, adjoint):
        for part in range(2):
            if part == 0:
                term = lambda m: first[m, 0] * adjoint[m, 0] + first[m, 1] * adjoint[m, 1]
            else:
                term = lambda m: first[m, 0] * adjoint[m, 1] - first[m, 1] * adjoint[m, 0]
            grad = (term(0) + term(1)).astype(BF)
            gsend[layer, part] = dot(dot(turn_rows, grad).astype(BF), turn_cols).astype(BF)
        wins[layer, s] = gsend[layer, core]

    def launch(j):
        for c in range(2):
            start(near(j, c, 1))
            start(near(j, c, 0))
        start(pair(j))

    def pass_on(j):
        for c in range(2):
            for side in (1, 0):
                near_in(j, c, side).wait_recv()
                start(relay(j, c, side))

    lane = lax.broadcasted_iota(jnp.int32, (1, N), 1)
    cols = [
        [jnp.where((lane + (2 * x + b) * N >= c0) & (lane + (2 * x + b) * N < c0 + N), 1.0, 0.0) for b in range(2)]
        for _, c0 in places
    ]

    def gather(j):
        layer, first, size = chunks[j]
        chunk = 16

        def run(i, carry):
            at = pl.multiple_of(first + i * chunk, chunk)
            rows = pl.ds(at, chunk)
            line = lax.broadcasted_iota(jnp.int32, (chunk, N), 0) + at
            sums = [[jnp.zeros((chunk, N), F32) for _ in range(3)] for _ in range(2)]
            for n in range(NS):
                term = wins[layer, n, rows, :].astype(F32)
                above = line >= places[n][0]
                for b in range(2):
                    masked = term * cols[n][b]
                    low, high = (2, 0) if n % 2 else (0, 1)
                    sums[b][low] = sums[b][low] + jnp.where(above, masked, 0.0)
                    sums[b][high] = sums[b][high] + jnp.where(above, 0.0, masked)
            mine = core == 0
            acc[layer, rows, :] = jnp.where(mine, sums[0][0], sums[1][0])
            tsend[layer, rows, :] = jnp.where(mine, sums[1][0], sums[0][0]).astype(BF)
            for b in range(2):
                bsend[layer, b, rows, :] = sums[b][1].astype(BF)
                csend[layer, b, rows, :] = sums[b][2].astype(BF)
            return carry

        lax.fori_loop(0, size // chunk, run, 0)

    def top_copy(j):
        layer, q = chunks[j][0], 21 + 16 * j
        return remote(tsend.at[layer, span(j)], trecv.at[layer, span(j)], send.at[q], recv.at[q], (partner, o))

    def edge(j, upward):
        q = 22 + 16 * j + (0 if upward else 2)
        return (bsend, brecv, q, up) if upward else (csend, crecv, q, down)

    def edge_copy(j, b, upward):
        layer, (source, target, q, to) = chunks[j][0], edge(j, upward)
        return remote(
            source.at[layer, b, span(j)], target.at[layer, core, span(j)], send.at[q + b], recv.at[q + core], (2 * x + b, to)
        )

    def edge_in(j, c, upward):
        layer, (source, target, q, to) = chunks[j][0], edge(j, upward)
        return remote(source.at[layer, c, span(j)], target.at[layer, c, span(j)], send.at[q + c], recv.at[q + c], (s, to))

    def collect(j):
        pair(j, True).wait_recv()
        for c in range(2):
            for side in (1, 0):
                relay(j, c, side, True).wait_recv()
        gather(j)
        for b in range(2):
            start(edge_copy(j, b, True))
            start(edge_copy(j, b, False))
        start(top_copy(j))

    def finish(j):
        layer = chunks[j][0]
        top_copy(j).wait_recv()
        for c in range(2):
            edge_in(j, c, True).wait_recv()
            edge_in(j, c, False).wait_recv()
        for i in range(2):
            rows = span(j, i)
            rims = [brecv[layer, c, rows, :].astype(F32) + crecv[layer, c, rows, :].astype(F32) for c in (core, other)]
            done[layer, core, rows, :] = acc[layer, rows, :] + rims[0]
            done[layer, other, rows, :] = trecv[layer, rows, :].astype(F32) + rims[1]
        leaving = pltpu.make_async_copy(
            done.at[layer, :, span(j)], out_hbm.at[layer, :, span(j)], dma.at[6 + 2 * NS + j]
        )
        leaving.start()
        gone.append(leaving)

    share(1, arr, cur)
    launch(0)
    launch(1)

    def behind(rows, i):
        re, im = win[1, 0, rows, :], win[1, 1, rows, :]
        for m in range(2):
            cr, ci = cur[m, 0, rows, :], cur[m, 1, rows, :]
            put(m, rows, i, re * cr + im * ci, re * ci - im * cr)

    by_rows(behind)
    left_mul(e_c)
    right_mul(e_h, cur)

    def leave(rows, i):
        re, im = win[0, 0, rows, :], win[0, 1, rows, :]
        for m in range(2):
            cr, ci = cur[m, 0, rows, :], cur[m, 1, rows, :]
            esend[m, 0, rows, :] = (re * cr + im * ci).astype(BF)
            esend[m, 1, rows, :] = (re * ci - im * cr).astype(BF)

    by_rows(leave)
    q_pair, q_y, q_z, q_x = 75, 76, 79, 86
    e_copy = remote(esend.at[other], erecv, send.at[q_pair], recv.at[q_pair], (partner, o))
    start(e_copy)
    share(0, probe, cur)
    e_copy.wait_recv()

    def add_pair(rows, i):
        for part in range(2):
            ysend[part, rows, :] = (esend[core, part, rows, :].astype(F32) + erecv[part, rows, :].astype(F32)).astype(BF)

    by_rows(add_pair)
    deep = N // NY
    y_copies = []
    for k in range(1, NY):
        y_to = rem(y + k, NY)
        rows_to = pl.ds(pl.multiple_of(y_to * deep, deep), deep)
        copy = remote(
            ysend.at[:, rows_to, :], yrecv.at[k - 1], send.at[q_y + k - 1], recv.at[q_y + k - 1], (s, y_to * NZ + z)
        )
        start(copy)
        y_copies.append(copy)
    pass_on(0)
    launch(2)
    pass_on(1)
    for copy in y_copies:
        copy.wait_recv()
    rows_me = pl.ds(pl.multiple_of(y * deep, deep), deep)
    totals = []
    for part in range(2):
        total = ysend[part, rows_me, :].astype(F32)
        for k in range(NY - 1):
            total = total + yrecv[k, part].astype(F32)
        totals.append(total)
    for k in range(NZ):
        zsend[k] = jnp.concatenate([total[8 * k : 8 * k + 8] for total in totals], axis=0).astype(BF)
    z_copies = []
    for k in range(1, NZ):
        z_to = rem(z + k, NZ)
        copy = remote(
            zsend.at[z_to], zrecv.at[k - 1], send.at[q_z + k - 1], recv.at[q_z + k - 1], (s, y * NZ + z_to)
        )
        start(copy)
        z_copies.append(copy)
    collect(0)
    pass_on(2)
    launch(3)
    collect(1)
    for copy in z_copies:
        copy.wait_recv()
    total = zsend[z].astype(F32)
    for k in range(NZ - 1):
        total = total + zrecv[k].astype(F32)
    xall[0] = total.astype(BF)
    x_copies = []
    for k in range(1, NS):
        copy = remote(xall.at[0], xall.at[k], send.at[q_x + k - 1], recv.at[q_x + k - 1], (rem(s + k, NS), o))
        start(copy)
        x_copies.append(copy)
    pass_on(3)
    finish(0)
    collect(2)
    for copy in x_copies:
        copy.wait_recv()
    pick = one_hot((N, 128), lambda a, b: a == b + 32 * s)
    factor = 1.0 / math.sqrt(256.0)
    shares = [dot(xall[k], pick) for k in range(NS)]
    mine = (shares[0] + shares[2] + (shares[4] + shares[6])) * factor
    theirs = (shares[1] + shares[3] + (shares[5] + shares[7])) * factor
    for part in range(2):
        pout_ref[core, part] = mine[8 * part : 8 * part + 8, :32]
        pout_ref[other, part] = theirs[8 * part : 8 * part + 8, :32]
    finish(1)
    collect(3)
    finish(2)
    finish(3)
    for copy in gone:
        copy.wait()
    for copy in sends:
        copy.wait_send()

    @pl.when(core == 1)
    def _():
        offer_copy.wait_send()


def hand_on(grad_hbm, probe_hbm, grad_out, probe_out, held, probe_held, sem):
    moves = [(grad_hbm.at[a], held.at[a], grad_out.at[a]) for a in range(4)] + [(probe_hbm, probe_held, probe_out)]
    inward = [pltpu.make_async_copy(source, kept, sem.at[i]) for i, (source, kept, _) in enumerate(moves)]
    outward = [pltpu.make_async_copy(kept, target, sem.at[5 + i]) for i, (_, kept, target) in enumerate(moves)]
    for copy in inward:
        copy.start()
    for copy, after in zip(inward, outward):
        copy.wait()
        after.start()
    for copy in outward:
        copy.wait()


def body(object_slices, probe, measured, positions, counts):
    vmem = pltpu.VMEM
    square = lambda *lead: (*lead, N, N)
    any_spec = pl.BlockSpec(memory_space=pl.ANY)
    results = pl.pallas_call(
        main_kernel,
        out_shape=(
            jax.ShapeDtypeStruct(square(2, 2), F32),
            jax.ShapeDtypeStruct((2, 2, 8, 32), F32),
        ),
        in_specs=[pl.BlockSpec(memory_space=pltpu.SMEM)] + [any_spec] * 5,
        out_specs=(any_spec, pl.BlockSpec(memory_space=vmem)),
        scratch_shapes=[
            pltpu.SMEM((2, 2), jnp.int32),
            vmem((1, 128), jnp.int32),
            vmem((2 * NS, 1, 128), jnp.int32),
            pltpu.SMEM((2 * NS, 1, 128), jnp.int32),
            *[vmem(square(NS, 2), F32)] * 2,
            vmem(square(2, 2), F32),
            vmem(square(2 * NX), BF),
            vmem(square(4), BF),
            *[vmem((2 * N, 2 * N), BF)] * 4,
            vmem(square(2, 2), BF),
            vmem(square(2, 2), BF),
            vmem(square(2, 2), BF),
            *[vmem(square(), BF)] * 3,
            vmem(square(2), BF),
            vmem(square(), BF),
            vmem(square(2, 2), F32),
            vmem((2 * N, 2 * N), BF),
            vmem((2 * N, 2 * N), BF),
            vmem(square(2, 2), F32),
            vmem(square(2, 2), F32),
            vmem(square(2, 2), F32),
            vmem(square(2, 2), BF),
            vmem(square(2, NS), BF),
            vmem(square(2), F32),
            vmem(square(2, 2), F32),
            vmem(square(2), BF),
            vmem(square(2), BF),
            *[vmem(square(2, 2), BF)] * 4,
            vmem(square(2, 2), BF),
            vmem(square(2), BF),
            vmem(square(2), BF),
            vmem((NY - 1, 2, N // NY, N), BF),
            vmem((NZ, 16, N), BF),
            vmem((NZ - 1, 16, N), BF),
            vmem((NS, 16, N), BF),
            pltpu.SemaphoreType.DMA((10 + 2 * NS,)),
            pltpu.SemaphoreType.DMA((115,)),
            pltpu.SemaphoreType.DMA((115,)),
        ],
        compiler_params=pltpu.CompilerParams(
            collective_id=0, has_side_effects=True, vmem_limit_bytes=60 * 1024 * 1024
        ),
        name="gradient",
    )(counts, positions[0, 0], object_slices, probe, measured[0, 0], tables())
    grad, probe_grad = pl.pallas_call(
        hand_on,
        out_shape=(jax.ShapeDtypeStruct(square(4), F32), jax.ShapeDtypeStruct((2, 2, 8, 32), F32)),
        in_specs=[any_spec] * 2,
        out_specs=(any_spec, any_spec),
        scratch_shapes=[vmem(square(4), F32), vmem((2, 2, 8, 32), F32), pltpu.SemaphoreType.DMA((10,))],
        name="results",
    )(results[0].reshape(square(4)), results[1])
    return grad.reshape(square(2, 2)), probe_grad


def solution(mesh):
    return jax.shard_map(
        body,
        mesh=mesh,
        in_specs=(
            P(None, None, "obj", None),
            P(),
            P("scan", "obj", None, None, None),
            P("scan", "obj", None, None),
            P("scan", "obj"),
        ),
        out_specs=(P(None, None, "obj", "scan"), P(None, None, "obj", "scan")),
        check_vma=False,
    )
```

```python
import functools
import math

import jax
import jax.numpy as jnp
import numpy as np
from jax import lax
from jax.experimental import pallas as pl
from jax.experimental.pallas import tpu as pltpu
from jax.sharding import PartitionSpec as P

MESH = pl.DeviceIdType.MESH
BF = jnp.bfloat16
F32 = jnp.float32
N = 256
NS, NX, NO, NY, NZ = 8, 4, 32, 4, 8


def rem(a, b):
    return lax.rem(a, jnp.int32(b))


def tables():
    index = np.arange(N)
    angle = (np.outer(index, index) % N) * (2.0 * np.pi / N)
    rounded = lambda a: a.astype(np.float32).astype(BF)
    f_re, f_im = rounded(np.cos(angle) / 16.0), rounded(-np.sin(angle) / 16.0)
    fwd = f_re.astype(np.float64) + 1j * f_im.astype(np.float64)
    freq = np.where(index < N // 2, index, index - N)
    phase = np.exp(-2j * np.pi * ((freq * freq) % (4 * N)) / (4 * N))
    prop = np.conj(fwd) @ (phase[:, None] * fwd)
    return np.stack([f_re, f_im, rounded(prop.real), rounded(prop.imag)])


def remote(src, dst, send, recv, device):
    return pltpu.make_async_remote_copy(
        src_ref=src, dst_ref=dst, send_sem=send, recv_sem=recv, device_id=device, device_id_type=MESH
    )


def main_kernel(
    count_ref, pos_hbm, tile_hbm, probe_hbm, meas_hbm, table_hbm, out_hbm, pout_ref,
    pos_ref, row, rows_in, tab, tile_0, tile_1, probe, meas, tabs, e_f, e_i, e_h, e_c, hsend, hrecv, local, offer, offered, rising, risen, pattern, win, v, u, arr, far, cur,
    gsend, wins, acc, done, tsend, trecv, bsend, brecv, csend, crecv, esend, erecv, ysend, yrecv, zsend, zrecv, xall,
    dma, send, recv,
):
    s, o = lax.axis_index("scan"), lax.axis_index("obj")
    x, core = lax.div(s, jnp.int32(2)), rem(s, 2)
    y, z = lax.div(o, jnp.int32(NZ)), rem(o, NZ)
    other = 1 - core
    partner = 2 * x + other
    right = [2 * rem(x + 1, NX) + c for c in range(2)]
    left = [2 * rem(x + 3, NX) + c for c in range(2)]
    right_me, left_me = 2 * rem(x + 1, NX) + core, 2 * rem(x + 3, NX) + core
    x_left, x_right, x_far = rem(x + 3, NX), rem(x + 1, NX), rem(x + 2, NX)
    far_at = [2 * rem(x + 2, NX) + c for c in range(2)]
    up, down = rem(o + 1, NO), rem(o + NO - 1, NO)
    tile = (tile_0, tile_1)
    sends, gone = [], []

    barrier = pltpu.get_barrier_semaphore()
    peers = [(rem(s + k, NS), o) for k in range(1, NS)]
    peers += [(s, up), (partner, up)] + [(rem(s + k, NS), down) for k in range(NS)]
    peers += [(s, rem(y + k, NY) * NZ + z) for k in range(1, NY)]
    peers += [(s, y * NZ + rem(z + k, NZ)) for k in range(1, NZ)]
    for peer in peers:
        pl.semaphore_signal(barrier, inc=1, device_id=peer, device_id_type=MESH)

    given = pltpu.make_async_copy(pos_hbm, pos_ref, dma.at[4 + 2 * NS])
    given.start()
    loads = [
        pltpu.make_async_copy(table_hbm, tabs, dma.at[0]),
        pltpu.make_async_copy(probe_hbm, probe, dma.at[1]),
        pltpu.make_async_copy(meas_hbm, meas.at[pl.ds(2 * x, 2)], dma.at[2]),
    ]
    for layer in range(2):
        for b in range(NS):
            block = tile_hbm.at[layer, :, :, pl.ds(b * N, N)]
            loads.append(pltpu.make_async_copy(block, tile[layer].at[b], dma.at[3 + NS * layer + b]))
    for load in loads:
        load.start()

    lane = lax.broadcasted_iota(jnp.int32, (1, 128), 1)
    given.wait()
    line = jnp.zeros((1, 128), jnp.int32)
    for j, value in enumerate((pos_ref[0, 0], pos_ref[0, 1], pos_ref[1, 0], pos_ref[1, 1], count_ref[0, 0])):
        line = jnp.where(lane == j, value, line)
    row[...] = line
    rows_in[s] = line

    def one_hot(shape, rule):
        a, b = lax.broadcasted_iota(jnp.int32, shape, 0), lax.broadcasted_iota(jnp.int32, shape, 1)
        return jnp.where(rule(a, b), 1.0, 0.0).astype(BF)

    def dot(a, b):
        return jnp.dot(a, b, preferred_element_type=F32)

    def col_block(col):
        k = jnp.int32(0)
        for edge in range(1, NS - 1):
            k = k + jnp.where(col >= edge * N, 1, 0)
        return k

    def picks(offset):
        return [one_hot((N, N), lambda a, b: a + h * N == b + offset) for h in range(2)]

    def columns(layer, part, k, pick):
        first, second = tile[layer][k, part].astype(BF), tile[layer][k + 1, part].astype(BF)
        return (dot(first, pick[0]) + dot(second, pick[1])).astype(BF)


    pl.semaphore_wait(barrier, len(peers))

    def start(copy):
        copy.start()
        sends.append(copy)

    def meas_copy(q, slot, n, peer):
        ref = meas.at[pl.ds(slot, n)]
        return remote(ref, ref, send.at[q], recv.at[q], (peer, o))

    def place_copy(k, base, owner):
        peer = (rem(s + k, NS), up if base else o)
        return remote(row, rows_in.at[base + owner], send.at[109 + base + k], recv.at[109 + base + k], peer)

    every = [(k, base) for base in (0, NS) for k in range(NS) if base or k]
    for k, base in every:
        start(place_copy(k, base, s))
    for q, k, peer in ((1, 0, right_me), (2, 1, left_me), (6, 1, right_me), (7, 0, left_me)):
        start(remote(meas_hbm.at[pl.ds(k, 1)], meas.at[pl.ds(2 * x + k, 1)], send.at[q], recv.at[q], (peer, o)))
    loads[0].wait()
    for e_ref, re, im, sign in ((e_f, 0, 1, 1), (e_i, 0, 1, -1), (e_h, 2, 3, 1), (e_c, 2, 3, -1)):
        e_ref[0:N, 0:N] = tabs[re]
        e_ref[N:, N:] = tabs[re]
        e_ref[0:N, N:] = -tabs[im] if sign > 0 else tabs[im]
        e_ref[N:, 0:N] = tabs[im] if sign > 0 else -tabs[im]

    for k, base in every:
        place_copy(k, base, rem(s + NS - k, NS)).wait_recv()
    fetch = pltpu.make_async_copy(rows_in, tab, dma.at[3 + 2 * NS])
    fetch.start()
    fetch.wait()

    def assigned(base, n):
        begin, found = jnp.int32(0), [jnp.int32(0)] * 4
        for t in range(NS):
            count = tab[base + t, 0, 4]
            for k in range(2):
                hit = (k < count) & (begin + k == n)
                values = (jnp.int32(t % 2), jnp.int32(2 * (t // 2) + k), tab[base + t, 0, 2 * k], tab[base + t, 0, 2 * k + 1])
                for j, value in enumerate(values):
                    found[j] = jnp.where(hit, value, found[j])
            begin = begin + count
        return found

    _, _, _, col_out = assigned(NS * other, x + NX * core)
    k_out = col_block(col_out)
    pick_out = picks(col_out - k_out * N)
    halo_to = jnp.where(core == 0, down, up)

    def halo_copy(layer, part):
        q = 127 + 2 * layer + part
        return remote(hsend.at[layer, part], hrecv.at[layer, part], send.at[q], recv.at[q], (s, halo_to))

    for layer in range(2):
        for b in range(NS):
            loads[3 + NS * layer + b].wait()
        for part in range(2):
            hsend[layer, part] = columns(layer, part, k_out, pick_out)
            start(halo_copy(layer, part))
    meas_copy(1, 2 * x_left, 1, right_me).wait_recv()
    start(meas_copy(3, 2 * x_left, 1, right_me))
    meas_copy(2, 2 * x_right + 1, 1, left_me).wait_recv()
    start(meas_copy(5, 2 * x_right + 1, 1, left_me))
    half_mine, slot_mine, row0, col0 = assigned(NS * core, x + NX * core)
    k_own = col_block(col0)
    pick_own = picks(col0 - k_own * N)
    for layer in range(2):
        for part in range(2):
            local[layer, part] = columns(layer, part, k_own, pick_own)
    places = [assigned(NS * (d % 2), d // 2 + NX * (d % 2))[2:] for d in range(NS)]
    _, slot_a, _, _ = assigned(0, x)
    _, slot_b, _, _ = assigned(0, x + NX)
    rows_own = one_hot((N, N), lambda a, b: b + N * core == a + row0)
    rows_halo = one_hot((N, N), lambda a, b: b + N * other == a + row0)
    turn = jnp.where(col0 == 7 * N, 0, col0 - k_own * N)
    turn_rows = one_hot((N, N), lambda a, b: (b + row0 == a) | (b + row0 == a + N))
    turn_cols = one_hot((N, N), lambda a, b: (a + turn == b) | (a + turn == b + N))
    loads[1].wait()

    def window(layer):
        for part in range(2):
            halo_copy(layer, part).wait_recv()
            win[layer, part] = dot(rows_own, local[layer, part]) + dot(rows_halo, hrecv[layer, part])

    step = 32

    def by_rows(body):
        def run(i, carry):
            body(pl.ds(pl.multiple_of(i * step, step), step), i)
            return carry

        lax.fori_loop(0, N // step, run, 0)

    def put(m, rows, i, re, im):
        v[pl.ds(pl.multiple_of(i * step, step), step), m * N : (m + 1) * N] = re.astype(BF)
        v[pl.ds(pl.multiple_of(N + i * step, step), step), m * N : (m + 1) * N] = im.astype(BF)

    def left_mul(matrix):
        for m in range(2):
            product = dot(matrix[...], v[:, m * N : (m + 1) * N])
            u[m * N : (m + 1) * N, 0:N] = product[0:N].astype(BF)
            u[m * N : (m + 1) * N, N:] = product[N:].astype(BF)

    def right_mul(matrix, result):
        for part in range(2):
            product = dot(u[...], matrix[:, part * N : (part + 1) * N])
            result[0, part] = product[0:N]
            result[1, part] = product[N:]

    for q, slot, peer in ((3, 2 * x_far, right_me), (5, 2 * x_far + 1, left_me), (6, 2 * x_left + 1, right_me), (7, 2 * x_right, left_me)):
        meas_copy(q, slot, 1, peer).wait_recv()
    loads[2].wait()
    rising[...] = meas[slot_b]
    start(remote(rising, risen.at[core], send.at[125], recv.at[125 + core], (2 * x + 1, up)))
    offer[...] = meas[slot_a]
    offer_copy = remote(offer, offered, send.at[0], recv.at[0], (2 * x, o))

    @pl.when(core == 1)
    def _():
        offer_copy.start()

    window(0)

    def enter(rows, i):
        re, im = win[0, 0, rows, :], win[0, 1, rows, :]
        for m in range(2):
            pr, pi = probe[m, 0, rows, :], probe[m, 1, rows, :]
            put(m, rows, i, pr * re - pi * im, pr * im + pi * re)

    by_rows(enter)
    left_mul(e_h)
    right_mul(e_c, arr)
    window(1)

    def second(rows, i):
        re, im = win[1, 0, rows, :], win[1, 1, rows, :]
        for m in range(2):
            pr, pi = arr[m, 0, rows, :], arr[m, 1, rows, :]
            put(m, rows, i, pr * re - pi * im, pr * im + pi * re)

    by_rows(second)
    left_mul(e_f)
    right_mul(e_i, far)

    @pl.when(core == 0)
    def _():
        offer_copy.wait_recv()
        pattern[...] = jnp.where(half_mine == 0, offer[...], offered[...])

    @pl.when(core == 1)
    def _():
        for c in range(2):
            remote(rising, risen.at[c], send.at[125], recv.at[125 + c], (s, up)).wait_recv()
        pattern[...] = jnp.where(half_mine == 0, risen[0], risen[1])

    def misfit(rows, i):
        parts = [(far[m, 0, rows, :], far[m, 1, rows, :]) for m in range(2)]
        total = parts[0][0] ** 2 + parts[0][1] ** 2 + (parts[1][0] ** 2 + parts[1][1] ** 2)
        gap = total - pattern[rows, :].astype(F32)
        for m in range(2):
            put(m, rows, i, gap * parts[m][0], gap * parts[m][1])

    by_rows(misfit)
    left_mul(e_i)
    right_mul(e_f, cur)

    chunks = [(1, 0, 128), (1, 128, 128), (0, 0, 96), (0, 96, 96), (0, 192, 64)]

    def span(j, part=None):
        _, first, size = chunks[j]
        return pl.ds(first, size) if part is None else pl.ds(first + part * size // 2, size // 2)

    def near(j, c, side):
        layer, q = chunks[j][0], 11 + 16 * j + (2 if side else 4)
        peer = (right if side else left)[c]
        return remote(
            gsend.at[layer, c, span(j)], wins.at[layer, s, span(j)], send.at[q + c], recv.at[q + core], (peer, o)
        )

    def near_in(j, c, side):
        layer, q = chunks[j][0], 11 + 16 * j + (2 if side else 4)
        slot = wins.at[layer, (left if side else right)[c], span(j)]
        return remote(slot, slot, send.at[q + c], recv.at[q + c], (partner, o))

    def relay(j, c, side, incoming=False):
        q = 11 + 16 * j + (6 if side else 8) + c
        owner = far_at[c] if incoming else (left if side else right)[c]
        piece = wins.at[chunks[j][0], owner, span(j, 0 if side else 1)]
        return remote(piece, piece, send.at[q], recv.at[q], (right_me if side else left_me, o))

    def pair(j, incoming=False):
        layer, q = chunks[j][0], 11 + 16 * j
        slot = wins.at[layer, partner if incoming else s, span(j)]
        return remote(gsend.at[layer, other, span(j)], slot, send.at[q], recv.at[q], (partner, o))

    def share(layer, first, adjoint):
        for part in range(2):
            if part == 0:
                term = lambda m: first[m, 0] * adjoint[m, 0] + first[m, 1] * adjoint[m, 1]
            else:
                term = lambda m: first[m, 0] * adjoint[m, 1] - first[m, 1] * adjoint[m, 0]
            grad = (term(0) + term(1)).astype(BF)
            gsend[layer, part] = dot(dot(turn_rows, grad).astype(BF), turn_cols).astype(BF)
        wins[layer, s] = gsend[layer, core]

    def launch(j):
        for c in range(2):
            start(near(j, c, 1))
            start(near(j, c, 0))
        start(pair(j))

    def pass_on(j):
        for c in range(2):
            for side in (1, 0):
                near_in(j, c, side).wait_recv()
                start(relay(j, c, side))

    lane = lax.broadcasted_iota(jnp.int32, (1, N), 1)
    cols = [
        [jnp.where((lane + (2 * x + b) * N >= c0) & (lane + (2 * x + b) * N < c0 + N), 1.0, 0.0) for b in range(2)]
        for _, c0 in places
    ]

    def gather(j):
        layer, first, size = chunks[j]
        chunk = 16

        def run(i, carry):
            at = pl.multiple_of(first + i * chunk, chunk)
            rows = pl.ds(at, chunk)
            line = lax.broadcasted_iota(jnp.int32, (chunk, N), 0) + at
            sums = [[jnp.zeros((chunk, N), F32) for _ in range(3)] for _ in range(2)]
            for n in range(NS):
                term = wins[layer, n, rows, :].astype(F32)
                above = line >= places[n][0]
                for b in range(2):
                    masked = term * cols[n][b]
                    low, high = (2, 0) if n % 2 else (0, 1)
                    sums[b][low] = sums[b][low] + jnp.where(above, masked, 0.0)
                    sums[b][high] = sums[b][high] + jnp.where(above, 0.0, masked)
            mine = core == 0
            acc[layer, rows, :] = jnp.where(mine, sums[0][0], sums[1][0])
            tsend[layer, rows, :] = jnp.where(mine, sums[1][0], sums[0][0]).astype(BF)
            for b in range(2):
                bsend[layer, b, rows, :] = sums[b][1].astype(BF)
                csend[layer, b, rows, :] = sums[b][2].astype(BF)
            return carry

        lax.fori_loop(0, size // chunk, run, 0)

    def top_copy(j):
        layer, q = chunks[j][0], 21 + 16 * j
        return remote(tsend.at[layer, span(j)], trecv.at[layer, span(j)], send.at[q], recv.at[q], (partner, o))

    def edge(j, upward):
        q = 22 + 16 * j + (0 if upward else 2)
        return (bsend, brecv, q, up) if upward else (csend, crecv, q, down)

    def edge_copy(j, b, upward):
        layer, (source, target, q, to) = chunks[j][0], edge(j, upward)
        return remote(
            source.at[layer, b, span(j)], target.at[layer, core, span(j)], send.at[q + b], recv.at[q + core], (2 * x + b, to)
        )

    def edge_in(j, c, upward):
        layer, (source, target, q, to) = chunks[j][0], edge(j, upward)
        return remote(source.at[layer, c, span(j)], target.at[layer, c, span(j)], send.at[q + c], recv.at[q + c], (s, to))

    def collect(j):
        pair(j, True).wait_recv()
        for c in range(2):
            for side in (1, 0):
                relay(j, c, side, True).wait_recv()
        gather(j)
        for b in range(2):
            start(edge_copy(j, b, True))
            start(edge_copy(j, b, False))
        start(top_copy(j))

    def finish(j):
        layer = chunks[j][0]
        top_copy(j).wait_recv()
        for c in range(2):
            edge_in(j, c, True).wait_recv()
            edge_in(j, c, False).wait_recv()
        for i in range(2):
            rows = span(j, i)
            rims = [brecv[layer, c, rows, :].astype(F32) + crecv[layer, c, rows, :].astype(F32) for c in (core, other)]
            done[layer, core, rows, :] = acc[layer, rows, :] + rims[0]
            done[layer, other, rows, :] = trecv[layer, rows, :].astype(F32) + rims[1]
        leaving = pltpu.make_async_copy(
            done.at[layer, :, span(j)], out_hbm.at[layer, :, span(j)], dma.at[6 + 2 * NS + j]
        )
        leaving.start()
        gone.append(leaving)

    share(1, arr, cur)
    launch(0)
    launch(1)

    def behind(rows, i):
        re, im = win[1, 0, rows, :], win[1, 1, rows, :]
        for m in range(2):
            cr, ci = cur[m, 0, rows, :], cur[m, 1, rows, :]
            put(m, rows, i, re * cr + im * ci, re * ci - im * cr)

    by_rows(behind)
    left_mul(e_c)
    right_mul(e_h, cur)

    def leave(rows, i):
        re, im = win[0, 0, rows, :], win[0, 1, rows, :]
        for m in range(2):
            cr, ci = cur[m, 0, rows, :], cur[m, 1, rows, :]
            esend[m, 0, rows, :] = (re * cr + im * ci).astype(BF)
            esend[m, 1, rows, :] = (re * ci - im * cr).astype(BF)

    by_rows(leave)
    q_pair, q_y, q_z, q_x = 91, 92, 95, 102
    e_copy = remote(esend.at[other], erecv, send.at[q_pair], recv.at[q_pair], (partner, o))
    start(e_copy)
    share(0, probe, cur)
    e_copy.wait_recv()

    def add_pair(rows, i):
        for part in range(2):
            ysend[part, rows, :] = (esend[core, part, rows, :].astype(F32) + erecv[part, rows, :].astype(F32)).astype(BF)

    by_rows(add_pair)
    deep = N // NY
    y_copies = []
    for k in range(1, NY):
        y_to = rem(y + k, NY)
        rows_to = pl.ds(pl.multiple_of(y_to * deep, deep), deep)
        copy = remote(
            ysend.at[:, rows_to, :], yrecv.at[k - 1], send.at[q_y + k - 1], recv.at[q_y + k - 1], (s, y_to * NZ + z)
        )
        start(copy)
        y_copies.append(copy)
    pass_on(0)
    launch(2)
    pass_on(1)
    launch(3)
    for copy in y_copies:
        copy.wait_recv()
    rows_me = pl.ds(pl.multiple_of(y * deep, deep), deep)
    totals = []
    for part in range(2):
        total = ysend[part, rows_me, :].astype(F32)
        for k in range(NY - 1):
            total = total + yrecv[k, part].astype(F32)
        totals.append(total)
    for k in range(NZ):
        zsend[k] = jnp.concatenate([total[8 * k : 8 * k + 8] for total in totals], axis=0).astype(BF)
    z_copies = []
    for k in range(1, NZ):
        z_to = rem(z + k, NZ)
        copy = remote(
            zsend.at[z_to], zrecv.at[k - 1], send.at[q_z + k - 1], recv.at[q_z + k - 1], (s, y * NZ + z_to)
        )
        start(copy)
        z_copies.append(copy)
    collect(0)
    pass_on(2)
    launch(4)
    collect(1)
    pass_on(3)
    for copy in z_copies:
        copy.wait_recv()
    total = zsend[z].astype(F32)
    for k in range(NZ - 1):
        total = total + zrecv[k].astype(F32)
    xall[0] = total.astype(BF)
    x_copies = []
    for k in range(1, NS):
        copy = remote(xall.at[0], xall.at[k], send.at[q_x + k - 1], recv.at[q_x + k - 1], (rem(s + k, NS), o))
        start(copy)
        x_copies.append(copy)
    collect(2)
    pass_on(4)
    finish(0)
    finish(1)
    collect(3)
    for copy in x_copies:
        copy.wait_recv()
    pick = one_hot((N, 128), lambda a, b: a == b + 32 * s)
    factor = 1.0 / math.sqrt(256.0)
    shares = [dot(xall[k], pick) for k in range(NS)]
    mine = (shares[0] + shares[2] + (shares[4] + shares[6])) * factor
    theirs = (shares[1] + shares[3] + (shares[5] + shares[7])) * factor
    for part in range(2):
        pout_ref[core, part] = mine[8 * part : 8 * part + 8, :32]
        pout_ref[other, part] = theirs[8 * part : 8 * part + 8, :32]
    collect(4)
    finish(2)
    finish(3)
    finish(4)
    for copy in gone:
        copy.wait()
    for copy in sends:
        copy.wait_send()

    @pl.when(core == 1)
    def _():
        offer_copy.wait_send()


def hand_on(grad_hbm, probe_hbm, grad_out, probe_out, held, probe_held, sem):
    moves = [(grad_hbm.at[a], held.at[a], grad_out.at[a]) for a in range(4)] + [(probe_hbm, probe_held, probe_out)]
    inward = [pltpu.make_async_copy(source, kept, sem.at[i]) for i, (source, kept, _) in enumerate(moves)]
    outward = [pltpu.make_async_copy(kept, target, sem.at[5 + i]) for i, (_, kept, target) in enumerate(moves)]
    for copy in inward:
        copy.start()
    for copy, after in zip(inward, outward):
        copy.wait()
        after.start()
    for copy in outward:
        copy.wait()


def body(object_slices, probe, measured, positions, counts):
    vmem = pltpu.VMEM
    square = lambda *lead: (*lead, N, N)
    any_spec = pl.BlockSpec(memory_space=pl.ANY)
    results = pl.pallas_call(
        main_kernel,
        out_shape=(
            jax.ShapeDtypeStruct(square(2, 2), F32),
            jax.ShapeDtypeStruct((2, 2, 8, 32), F32),
        ),
        in_specs=[pl.BlockSpec(memory_space=pltpu.SMEM)] + [any_spec] * 5,
        out_specs=(any_spec, pl.BlockSpec(memory_space=vmem)),
        scratch_shapes=[
            pltpu.SMEM((2, 2), jnp.int32),
            vmem((1, 128), jnp.int32),
            vmem((2 * NS, 1, 128), jnp.int32),
            pltpu.SMEM((2 * NS, 1, 128), jnp.int32),
            *[vmem(square(NS, 2), F32)] * 2,
            vmem(square(2, 2), F32),
            vmem(square(2 * NX), BF),
            vmem(square(4), BF),
            *[vmem((2 * N, 2 * N), BF)] * 4,
            vmem(square(2, 2), BF),
            vmem(square(2, 2), BF),
            vmem(square(2, 2), BF),
            *[vmem(square(), BF)] * 3,
            vmem(square(2), BF),
            vmem(square(), BF),
            vmem(square(2, 2), F32),
            vmem((2 * N, 2 * N), BF),
            vmem((2 * N, 2 * N), BF),
            vmem(square(2, 2), F32),
            vmem(square(2, 2), F32),
            vmem(square(2, 2), F32),
            vmem(square(2, 2), BF),
            vmem(square(2, NS), BF),
            vmem(square(2), F32),
            vmem(square(2, 2), F32),
            vmem(square(2), BF),
            vmem(square(2), BF),
            *[vmem(square(2, 2), BF)] * 4,
            vmem(square(2, 2), BF),
            vmem(square(2), BF),
            vmem(square(2), BF),
            vmem((NY - 1, 2, N // NY, N), BF),
            vmem((NZ, 16, N), BF),
            vmem((NZ - 1, 16, N), BF),
            vmem((NS, 16, N), BF),
            pltpu.SemaphoreType.DMA((11 + 2 * NS,)),
            pltpu.SemaphoreType.DMA((131,)),
            pltpu.SemaphoreType.DMA((131,)),
        ],
        compiler_params=pltpu.CompilerParams(
            collective_id=0, has_side_effects=True, vmem_limit_bytes=60 * 1024 * 1024
        ),
        name="gradient",
    )(counts, positions[0, 0], object_slices, probe, measured[0, 0], tables())
    grad, probe_grad = pl.pallas_call(
        hand_on,
        out_shape=(jax.ShapeDtypeStruct(square(4), F32), jax.ShapeDtypeStruct((2, 2, 8, 32), F32)),
        in_specs=[any_spec] * 2,
        out_specs=(any_spec, any_spec),
        scratch_shapes=[vmem(square(4), F32), vmem((2, 2, 8, 32), F32), pltpu.SemaphoreType.DMA((10,))],
        name="results",
    )(results[0].reshape(square(4)), results[1])
    return grad.reshape(square(2, 2)), probe_grad


def solution(mesh):
    return jax.shard_map(
        body,
        mesh=mesh,
        in_specs=(
            P(None, None, "obj", None),
            P(),
            P("scan", "obj", None, None, None),
            P("scan", "obj", None, None),
            P("scan", "obj"),
        ),
        out_specs=(P(None, None, "obj", "scan"), P(None, None, "obj", "scan")),
        check_vma=False,
    )
```

```python
import functools
import math

import jax
import jax.numpy as jnp
import numpy as np
from jax import lax
from jax.experimental import pallas as pl
from jax.experimental.pallas import tpu as pltpu
from jax.sharding import PartitionSpec as P

MESH = pl.DeviceIdType.MESH
BF = jnp.bfloat16
F32 = jnp.float32
N = 256
NS, NX, NO, NY, NZ = 8, 4, 32, 4, 8


def rem(a, b):
    return lax.rem(a, jnp.int32(b))


def tables():
    index = np.arange(N)
    angle = (np.outer(index, index) % N) * (2.0 * np.pi / N)
    rounded = lambda a: a.astype(np.float32).astype(BF)
    f_re, f_im = rounded(np.cos(angle) / 16.0), rounded(-np.sin(angle) / 16.0)
    fwd = f_re.astype(np.float64) + 1j * f_im.astype(np.float64)
    freq = np.where(index < N // 2, index, index - N)
    phase = np.exp(-2j * np.pi * ((freq * freq) % (4 * N)) / (4 * N))
    prop = np.conj(fwd) @ (phase[:, None] * fwd)
    return np.stack([f_re, f_im, rounded(prop.real), rounded(prop.imag)])


def remote(src, dst, send, recv, device):
    return pltpu.make_async_remote_copy(
        src_ref=src, dst_ref=dst, send_sem=send, recv_sem=recv, device_id=device, device_id_type=MESH
    )


def main_kernel(
    count_ref, pos_hbm, tile_hbm, probe_hbm, meas_hbm, table_hbm, out_hbm, pout_ref,
    pos_ref, row, rows_in, tab, tile_0, tile_1, probe, meas, tabs, e_f, e_i, e_h, e_c, hsend, hrecv, local, offer, offered, rising, risen, pattern, win, v, u, arr, far, cur,
    gsend, wins, acc, done, tsend, trecv, bsend, brecv, csend, crecv, esend, erecv, ysend, yrecv, zsend, zrecv, xall,
    dma, send, recv,
):
    s, o = lax.axis_index("scan"), lax.axis_index("obj")
    x, core = lax.div(s, jnp.int32(2)), rem(s, 2)
    y, z = lax.div(o, jnp.int32(NZ)), rem(o, NZ)
    other = 1 - core
    partner = 2 * x + other
    right = [2 * rem(x + 1, NX) + c for c in range(2)]
    left = [2 * rem(x + 3, NX) + c for c in range(2)]
    right_me, left_me = 2 * rem(x + 1, NX) + core, 2 * rem(x + 3, NX) + core
    x_left, x_right, x_far = rem(x + 3, NX), rem(x + 1, NX), rem(x + 2, NX)
    far_at = [2 * rem(x + 2, NX) + c for c in range(2)]
    up, down = rem(o + 1, NO), rem(o + NO - 1, NO)
    tile = (tile_0, tile_1)
    sends, gone = [], []

    barrier = pltpu.get_barrier_semaphore()
    peers = [(s, y * NZ + rem(z + k, NZ)) for k in (4, 3, 5, 2, 6, 1, 7)]
    peers += [(rem(s + k, NS), down) for k in (4, 5, 3, 2, 6, 1, 7, 0)] + [(s, up), (partner, up)]
    peers += [(rem(s + k, NS), o) for k in (4, 5, 3, 2, 6, 1, 7)]
    peers += [(s, rem(y + k, NY) * NZ + z) for k in (2, 1, 3)]
    for peer in peers:
        pl.semaphore_signal(barrier, inc=1, device_id=peer, device_id_type=MESH)

    given = pltpu.make_async_copy(pos_hbm, pos_ref, dma.at[4 + 2 * NS])
    given.start()
    loads = [
        pltpu.make_async_copy(table_hbm, tabs, dma.at[0]),
        pltpu.make_async_copy(probe_hbm, probe, dma.at[1]),
        pltpu.make_async_copy(meas_hbm, meas.at[pl.ds(2 * x, 2)], dma.at[2]),
    ]
    for layer in range(2):
        for b in range(NS):
            block = tile_hbm.at[layer, :, :, pl.ds(b * N, N)]
            loads.append(pltpu.make_async_copy(block, tile[layer].at[b], dma.at[3 + NS * layer + b]))
    for load in loads:
        load.start()

    lane = lax.broadcasted_iota(jnp.int32, (1, 128), 1)
    given.wait()
    line = jnp.zeros((1, 128), jnp.int32)
    for j, value in enumerate((pos_ref[0, 0], pos_ref[0, 1], pos_ref[1, 0], pos_ref[1, 1], count_ref[0, 0])):
        line = jnp.where(lane == j, value, line)
    row[...] = line
    rows_in[s] = line

    def one_hot(shape, rule):
        a, b = lax.broadcasted_iota(jnp.int32, shape, 0), lax.broadcasted_iota(jnp.int32, shape, 1)
        return jnp.where(rule(a, b), 1.0, 0.0).astype(BF)

    def dot(a, b):
        return jnp.dot(a, b, preferred_element_type=F32)

    def col_block(col):
        k = jnp.int32(0)
        for edge in range(1, NS - 1):
            k = k + jnp.where(col >= edge * N, 1, 0)
        return k

    def picks(offset):
        return [one_hot((N, N), lambda a, b: a + h * N == b + offset) for h in range(2)]

    def columns(layer, part, k, pick):
        first, second = tile[layer][k, part].astype(BF), tile[layer][k + 1, part].astype(BF)
        return (dot(first, pick[0]) + dot(second, pick[1])).astype(BF)


    pl.semaphore_wait(barrier, len(peers))

    def start(copy):
        copy.start()
        sends.append(copy)

    def meas_copy(q, slot, n, peer):
        ref = meas.at[pl.ds(slot, n)]
        return remote(ref, ref, send.at[q], recv.at[q], (peer, o))

    def place_copy(k, base, owner):
        peer = (rem(s + k, NS), up if base else o)
        return remote(row, rows_in.at[base + owner], send.at[109 + base + k], recv.at[109 + base + k], peer)

    every = [(k, base) for base in (0, NS) for k in range(NS) if base or k]
    for k, base in every:
        start(place_copy(k, base, s))
    for q, k, peer in ((1, 0, right_me), (2, 1, left_me), (6, 1, right_me), (7, 0, left_me)):
        start(remote(meas_hbm.at[pl.ds(k, 1)], meas.at[pl.ds(2 * x + k, 1)], send.at[q], recv.at[q], (peer, o)))
    loads[0].wait()
    for e_ref, re, im, sign in ((e_f, 0, 1, 1), (e_i, 0, 1, -1), (e_h, 2, 3, 1), (e_c, 2, 3, -1)):
        e_ref[0:N, 0:N] = tabs[re]
        e_ref[N:, N:] = tabs[re]
        e_ref[0:N, N:] = -tabs[im] if sign > 0 else tabs[im]
        e_ref[N:, 0:N] = tabs[im] if sign > 0 else -tabs[im]

    for k, base in every:
        place_copy(k, base, rem(s + NS - k, NS)).wait_recv()
    fetch = pltpu.make_async_copy(rows_in, tab, dma.at[3 + 2 * NS])
    fetch.start()
    fetch.wait()

    def assigned(base, n):
        begin, found = jnp.int32(0), [jnp.int32(0)] * 4
        for t in range(NS):
            count = tab[base + t, 0, 4]
            for k in range(2):
                hit = (k < count) & (begin + k == n)
                values = (jnp.int32(t % 2), jnp.int32(2 * (t // 2) + k), tab[base + t, 0, 2 * k], tab[base + t, 0, 2 * k + 1])
                for j, value in enumerate(values):
                    found[j] = jnp.where(hit, value, found[j])
            begin = begin + count
        return found

    _, _, _, col_out = assigned(NS * other, x + NX * core)
    k_out = col_block(col_out)
    pick_out = picks(col_out - k_out * N)
    halo_to = jnp.where(core == 0, down, up)

    def halo_copy(layer, part):
        q = 127 + 2 * layer + part
        return remote(hsend.at[layer, part], hrecv.at[layer, part], send.at[q], recv.at[q], (s, halo_to))

    for layer in range(2):
        for b in range(NS):
            loads[3 + NS * layer + b].wait()
        for part in range(2):
            hsend[layer, part] = columns(layer, part, k_out, pick_out)
            start(halo_copy(layer, part))
    meas_copy(1, 2 * x_left, 1, right_me).wait_recv()
    start(meas_copy(3, 2 * x_left, 1, right_me))
    meas_copy(2, 2 * x_right + 1, 1, left_me).wait_recv()
    start(meas_copy(5, 2 * x_right + 1, 1, left_me))
    half_mine, slot_mine, row0, col0 = assigned(NS * core, x + NX * core)
    k_own = col_block(col0)
    pick_own = picks(col0 - k_own * N)
    for layer in range(2):
        for part in range(2):
            local[layer, part] = columns(layer, part, k_own, pick_own)
    places = [assigned(NS * (d % 2), d // 2 + NX * (d % 2))[2:] for d in range(NS)]
    _, slot_a, _, _ = assigned(0, x)
    _, slot_b, _, _ = assigned(0, x + NX)
    rows_own = one_hot((N, N), lambda a, b: b + N * core == a + row0)
    rows_halo = one_hot((N, N), lambda a, b: b + N * other == a + row0)
    turn = jnp.where(col0 == 7 * N, 0, col0 - k_own * N)
    turn_rows = one_hot((N, N), lambda a, b: (b + row0 == a) | (b + row0 == a + N))
    turn_cols = one_hot((N, N), lambda a, b: (a + turn == b) | (a + turn == b + N))
    loads[1].wait()

    def window(layer):
        for part in range(2):
            halo_copy(layer, part).wait_recv()
            win[layer, part] = dot(rows_own, local[layer, part]) + dot(rows_halo, hrecv[layer, part])

    step = 32

    def by_rows(body):
        def run(i, carry):
            body(pl.ds(pl.multiple_of(i * step, step), step), i)
            return carry

        lax.fori_loop(0, N // step, run, 0)

    def put(m, rows, i, re, im):
        v[pl.ds(pl.multiple_of(i * step, step), step), m * N : (m + 1) * N] = re.astype(BF)
        v[pl.ds(pl.multiple_of(N + i * step, step), step), m * N : (m + 1) * N] = im.astype(BF)

    def left_mul(matrix):
        for m in range(2):
            product = dot(matrix[...], v[:, m * N : (m + 1) * N])
            u[m * N : (m + 1) * N, 0:N] = product[0:N].astype(BF)
            u[m * N : (m + 1) * N, N:] = product[N:].astype(BF)

    def right_mul(matrix, result):
        for part in range(2):
            product = dot(u[...], matrix[:, part * N : (part + 1) * N])
            result[0, part] = product[0:N]
            result[1, part] = product[N:]

    for q, slot, peer in ((3, 2 * x_far, right_me), (5, 2 * x_far + 1, left_me), (6, 2 * x_left + 1, right_me), (7, 2 * x_right, left_me)):
        meas_copy(q, slot, 1, peer).wait_recv()
    loads[2].wait()
    rising[...] = meas[slot_b]
    start(remote(rising, risen.at[core], send.at[125], recv.at[125 + core], (2 * x + 1, up)))
    offer[...] = meas[slot_a]
    offer_copy = remote(offer, offered, send.at[0], recv.at[0], (2 * x, o))

    @pl.when(core == 1)
    def _():
        offer_copy.start()

    window(0)

    def enter(rows, i):
        re, im = win[0, 0, rows, :], win[0, 1, rows, :]
        for m in range(2):
            pr, pi = probe[m, 0, rows, :], probe[m, 1, rows, :]
            put(m, rows, i, pr * re - pi * im, pr * im + pi * re)

    by_rows(enter)
    left_mul(e_h)
    right_mul(e_c, arr)
    window(1)

    def second(rows, i):
        re, im = win[1, 0, rows, :], win[1, 1, rows, :]
        for m in range(2):
            pr, pi = arr[m, 0, rows, :], arr[m, 1, rows, :]
            put(m, rows, i, pr * re - pi * im, pr * im + pi * re)

    by_rows(second)
    left_mul(e_f)
    right_mul(e_i, far)

    @pl.when(core == 0)
    def _():
        offer_copy.wait_recv()
        pattern[...] = jnp.where(half_mine == 0, offer[...], offered[...])

    @pl.when(core == 1)
    def _():
        for c in range(2):
            remote(rising, risen.at[c], send.at[125], recv.at[125 + c], (s, up)).wait_recv()
        pattern[...] = jnp.where(half_mine == 0, risen[0], risen[1])

    def misfit(rows, i):
        parts = [(far[m, 0, rows, :], far[m, 1, rows, :]) for m in range(2)]
        total = parts[0][0] ** 2 + parts[0][1] ** 2 + (parts[1][0] ** 2 + parts[1][1] ** 2)
        gap = total - pattern[rows, :].astype(F32)
        for m in range(2):
            put(m, rows, i, gap * parts[m][0], gap * parts[m][1])

    by_rows(misfit)
    left_mul(e_i)
    right_mul(e_f, cur)

    chunks = [(1, 0, 128), (1, 128, 128), (0, 0, 128), (0, 128, 64), (0, 192, 64)]

    def span(j, part=None):
        _, first, size = chunks[j]
        return pl.ds(first, size) if part is None else pl.ds(first + part * size // 2, size // 2)

    def near(j, c, side):
        layer, q = chunks[j][0], 11 + 16 * j + (2 if side else 4)
        peer = (right if side else left)[c]
        return remote(
            gsend.at[layer, c, span(j)], wins.at[layer, s, span(j)], send.at[q + c], recv.at[q + core], (peer, o)
        )

    def near_in(j, c, side):
        layer, q = chunks[j][0], 11 + 16 * j + (2 if side else 4)
        slot = wins.at[layer, (left if side else right)[c], span(j)]
        return remote(slot, slot, send.at[q + c], recv.at[q + c], (partner, o))

    def relay(j, c, side, incoming=False):
        q = 11 + 16 * j + (6 if side else 8) + c
        owner = far_at[c] if incoming else (left if side else right)[c]
        piece = wins.at[chunks[j][0], owner, span(j, 0 if side else 1)]
        return remote(piece, piece, send.at[q], recv.at[q], (right_me if side else left_me, o))

    def pair(j, incoming=False):
        layer, q = chunks[j][0], 11 + 16 * j
        slot = wins.at[layer, partner if incoming else s, span(j)]
        return remote(gsend.at[layer, other, span(j)], slot, send.at[q], recv.at[q], (partner, o))

    def share(layer, first, adjoint, ready=None):
        for part in range(2):
            if part == 0:
                term = lambda m: first[m, 0] * adjoint[m, 0] + first[m, 1] * adjoint[m, 1]
            else:
                term = lambda m: first[m, 0] * adjoint[m, 1] - first[m, 1] * adjoint[m, 0]
            grad = (term(0) + term(1)).astype(BF)
            gsend[layer, part] = dot(dot(turn_rows, grad).astype(BF), turn_cols).astype(BF)
            if ready is not None:
                start(near(ready, part, 1))
                start(near(ready, part, 0))
        wins[layer, s] = gsend[layer, core]

    def launch(j):
        for c in range(2):
            start(near(j, c, 1))
            start(near(j, c, 0))
        start(pair(j))

    def pass_on(j):
        for c in range(2):
            for side in (1, 0):
                near_in(j, c, side).wait_recv()
                start(relay(j, c, side))

    lane = lax.broadcasted_iota(jnp.int32, (1, N), 1)
    cols = [
        [jnp.where((lane + (2 * x + b) * N >= c0) & (lane + (2 * x + b) * N < c0 + N), 1.0, 0.0) for b in range(2)]
        for _, c0 in places
    ]

    def gather(j):
        layer, first, size = chunks[j]
        chunk = 16

        def run(i, carry):
            at = pl.multiple_of(first + i * chunk, chunk)
            rows = pl.ds(at, chunk)
            line = lax.broadcasted_iota(jnp.int32, (chunk, N), 0) + at
            sums = [[jnp.zeros((chunk, N), F32) for _ in range(3)] for _ in range(2)]
            for n in range(NS):
                term = wins[layer, n, rows, :].astype(F32)
                above = line >= places[n][0]
                for b in range(2):
                    masked = term * cols[n][b]
                    low, high = (2, 0) if n % 2 else (0, 1)
                    sums[b][low] = sums[b][low] + jnp.where(above, masked, 0.0)
                    sums[b][high] = sums[b][high] + jnp.where(above, 0.0, masked)
            mine = core == 0
            acc[layer, rows, :] = jnp.where(mine, sums[0][0], sums[1][0])
            tsend[layer, rows, :] = jnp.where(mine, sums[1][0], sums[0][0]).astype(BF)
            for b in range(2):
                bsend[layer, b, rows, :] = sums[b][1].astype(BF)
                csend[layer, b, rows, :] = sums[b][2].astype(BF)
            return carry

        lax.fori_loop(0, size // chunk, run, 0)

    def top_copy(j):
        layer, q = chunks[j][0], 21 + 16 * j
        return remote(tsend.at[layer, span(j)], trecv.at[layer, span(j)], send.at[q], recv.at[q], (partner, o))

    def edge(j, upward):
        q = 22 + 16 * j + (0 if upward else 2)
        return (bsend, brecv, q, up) if upward else (csend, crecv, q, down)

    def edge_copy(j, b, upward):
        layer, (source, target, q, to) = chunks[j][0], edge(j, upward)
        return remote(
            source.at[layer, b, span(j)], target.at[layer, core, span(j)], send.at[q + b], recv.at[q + core], (2 * x + b, to)
        )

    def edge_in(j, c, upward):
        layer, (source, target, q, to) = chunks[j][0], edge(j, upward)
        return remote(source.at[layer, c, span(j)], target.at[layer, c, span(j)], send.at[q + c], recv.at[q + c], (s, to))

    def collect(j):
        pair(j, True).wait_recv()
        for c in range(2):
            for side in (1, 0):
                relay(j, c, side, True).wait_recv()
        gather(j)
        for b in range(2):
            start(edge_copy(j, b, True))
            start(edge_copy(j, b, False))
        start(top_copy(j))

    def finish(j):
        layer = chunks[j][0]
        top_copy(j).wait_recv()
        for c in range(2):
            edge_in(j, c, True).wait_recv()
            edge_in(j, c, False).wait_recv()
        for i in range(2):
            rows = span(j, i)
            rims = [brecv[layer, c, rows, :].astype(F32) + crecv[layer, c, rows, :].astype(F32) for c in (core, other)]
            done[layer, core, rows, :] = acc[layer, rows, :] + rims[0]
            done[layer, other, rows, :] = trecv[layer, rows, :].astype(F32) + rims[1]
        leaving = pltpu.make_async_copy(
            done.at[layer, :, span(j)], out_hbm.at[layer, :, span(j)], dma.at[6 + 2 * NS + j]
        )
        leaving.start()
        gone.append(leaving)

    share(1, arr, cur, ready=0)
    start(pair(0))
    launch(1)

    def behind(rows, i):
        re, im = win[1, 0, rows, :], win[1, 1, rows, :]
        for m in range(2):
            cr, ci = cur[m, 0, rows, :], cur[m, 1, rows, :]
            put(m, rows, i, re * cr + im * ci, re * ci - im * cr)

    by_rows(behind)
    left_mul(e_c)
    right_mul(e_h, cur)

    def leave(rows, i):
        re, im = win[0, 0, rows, :], win[0, 1, rows, :]
        for m in range(2):
            cr, ci = cur[m, 0, rows, :], cur[m, 1, rows, :]
            esend[m, 0, rows, :] = (re * cr + im * ci).astype(BF)
            esend[m, 1, rows, :] = (re * ci - im * cr).astype(BF)

    by_rows(leave)
    q_pair, q_y, q_z, q_x = 91, 92, 95, 102
    e_copy = remote(esend.at[other], erecv, send.at[q_pair], recv.at[q_pair], (partner, o))
    start(e_copy)
    share(0, probe, cur)
    e_copy.wait_recv()

    def add_pair(rows, i):
        for part in range(2):
            ysend[part, rows, :] = (esend[core, part, rows, :].astype(F32) + erecv[part, rows, :].astype(F32)).astype(BF)

    by_rows(add_pair)
    deep = N // NY
    y_copies = []
    for k in range(1, NY):
        y_to = rem(y + k, NY)
        rows_to = pl.ds(pl.multiple_of(y_to * deep, deep), deep)
        copy = remote(
            ysend.at[:, rows_to, :], yrecv.at[k - 1], send.at[q_y + k - 1], recv.at[q_y + k - 1], (s, y_to * NZ + z)
        )
        start(copy)
        y_copies.append(copy)
    pass_on(0)
    launch(2)
    pass_on(1)
    launch(3)
    for copy in y_copies:
        copy.wait_recv()
    rows_me = pl.ds(pl.multiple_of(y * deep, deep), deep)
    totals = []
    for part in range(2):
        total = ysend[part, rows_me, :].astype(F32)
        for k in range(NY - 1):
            total = total + yrecv[k, part].astype(F32)
        totals.append(total)
    for k in range(NZ):
        zsend[k] = jnp.concatenate([total[8 * k : 8 * k + 8] for total in totals], axis=0).astype(BF)
    z_copies = []
    for k in range(1, NZ):
        z_to = rem(z + k, NZ)
        copy = remote(
            zsend.at[z_to], zrecv.at[k - 1], send.at[q_z + k - 1], recv.at[q_z + k - 1], (s, y * NZ + z_to)
        )
        start(copy)
        z_copies.append(copy)
    collect(0)
    pass_on(2)
    launch(4)
    collect(1)
    pass_on(3)
    for copy in z_copies:
        copy.wait_recv()
    total = zsend[z].astype(F32)
    for k in range(NZ - 1):
        total = total + zrecv[k].astype(F32)
    xall[0] = total.astype(BF)
    x_copies = []
    for k in range(1, NS):
        copy = remote(xall.at[0], xall.at[k], send.at[q_x + k - 1], recv.at[q_x + k - 1], (rem(s + k, NS), o))
        start(copy)
        x_copies.append(copy)
    collect(2)
    pass_on(4)
    collect(3)
    collect(4)
    for copy in x_copies:
        copy.wait_recv()
    pick = one_hot((N, 128), lambda a, b: a == b + 32 * s)
    factor = 1.0 / math.sqrt(256.0)
    shares = [dot(xall[k], pick) for k in range(NS)]
    mine = (shares[0] + shares[2] + (shares[4] + shares[6])) * factor
    theirs = (shares[1] + shares[3] + (shares[5] + shares[7])) * factor
    for part in range(2):
        pout_ref[core, part] = mine[8 * part : 8 * part + 8, :32]
        pout_ref[other, part] = theirs[8 * part : 8 * part + 8, :32]
    for j in range(len(chunks)):
        finish(j)
    for copy in gone:
        copy.wait()
    for copy in sends:
        copy.wait_send()

    @pl.when(core == 1)
    def _():
        offer_copy.wait_send()


def hand_on(grad_ref, probe_ref, grad_out, probe_out, sem):
    copies = [
        pltpu.make_async_copy(grad_ref, grad_out, sem.at[0]),
        pltpu.make_async_copy(probe_ref, probe_out, sem.at[1]),
    ]
    for copy in copies:
        copy.start()
    for copy in copies:
        copy.wait()


def body(object_slices, probe, measured, positions, counts):
    vmem = pltpu.VMEM
    square = lambda *lead: (*lead, N, N)
    any_spec = pl.BlockSpec(memory_space=pl.ANY)
    given = [
        pltpu.with_memory_space_constraint(value, pltpu.HBM)
        for value in (positions[0, 0], object_slices, probe, measured[0, 0], jnp.asarray(tables()))
    ]
    results = pl.pallas_call(
        main_kernel,
        out_shape=(
            jax.ShapeDtypeStruct(square(2, 2), F32),
            jax.ShapeDtypeStruct((2, 2, 8, 32), F32),
        ),
        in_specs=[pl.BlockSpec(memory_space=pltpu.SMEM)] + [any_spec] * 5,
        out_specs=(any_spec, pl.BlockSpec(memory_space=vmem)),
        scratch_shapes=[
            pltpu.SMEM((2, 2), jnp.int32),
            vmem((1, 128), jnp.int32),
            vmem((2 * NS, 1, 128), jnp.int32),
            pltpu.SMEM((2 * NS, 1, 128), jnp.int32),
            *[vmem(square(NS, 2), F32)] * 2,
            vmem(square(2, 2), F32),
            vmem(square(2 * NX), BF),
            vmem(square(4), BF),
            *[vmem((2 * N, 2 * N), BF)] * 4,
            vmem(square(2, 2), BF),
            vmem(square(2, 2), BF),
            vmem(square(2, 2), BF),
            *[vmem(square(), BF)] * 3,
            vmem(square(2), BF),
            vmem(square(), BF),
            vmem(square(2, 2), F32),
            vmem((2 * N, 2 * N), BF),
            vmem((2 * N, 2 * N), BF),
            vmem(square(2, 2), F32),
            vmem(square(2, 2), F32),
            vmem(square(2, 2), F32),
            vmem(square(2, 2), BF),
            vmem(square(2, NS), BF),
            vmem(square(2), F32),
            vmem(square(2, 2), F32),
            vmem(square(2), BF),
            vmem(square(2), BF),
            *[vmem(square(2, 2), BF)] * 4,
            vmem(square(2, 2), BF),
            vmem(square(2), BF),
            vmem(square(2), BF),
            vmem((NY - 1, 2, N // NY, N), BF),
            vmem((NZ, 16, N), BF),
            vmem((NZ - 1, 16, N), BF),
            vmem((NS, 16, N), BF),
            pltpu.SemaphoreType.DMA((11 + 2 * NS,)),
            pltpu.SemaphoreType.DMA((131,)),
            pltpu.SemaphoreType.DMA((131,)),
        ],
        compiler_params=pltpu.CompilerParams(
            collective_id=0, has_side_effects=True, vmem_limit_bytes=44 * 1024 * 1024
        ),
        name="gradient",
    )(counts, *given)
    return pl.pallas_call(
        hand_on,
        out_shape=tuple(jax.ShapeDtypeStruct(r.shape, F32) for r in results),
        in_specs=[any_spec] * 2,
        out_specs=(any_spec, any_spec),
        scratch_shapes=[pltpu.SemaphoreType.DMA((2,))],
        compiler_params=pltpu.CompilerParams(vmem_limit_bytes=8 * 1024 * 1024),
        name="results",
    )(*results)


def solution(mesh):
    return jax.shard_map(
        body,
        mesh=mesh,
        in_specs=(
            P(None, None, "obj", None),
            P(),
            P("scan", "obj", None, None, None),
            P("scan", "obj", None, None),
            P("scan", "obj"),
        ),
        out_specs=(P(None, None, "obj", "scan"), P(None, None, "obj", "scan")),
        check_vma=False,
    )
```

```python
import functools
import math

import jax
import jax.numpy as jnp
import numpy as np
from jax import lax
from jax.experimental import pallas as pl
from jax.experimental.pallas import tpu as pltpu
from jax.sharding import PartitionSpec as P

MESH = pl.DeviceIdType.MESH
BF = jnp.bfloat16
F32 = jnp.float32
N = 256
NS, NX, NO, NY, NZ = 8, 4, 32, 4, 8


def rem(a, b):
    return lax.rem(a, jnp.int32(b))


def tables():
    index = np.arange(N)
    angle = (np.outer(index, index) % N) * (2.0 * np.pi / N)
    rounded = lambda a: a.astype(np.float32).astype(BF)
    f_re, f_im = rounded(np.cos(angle) / 16.0), rounded(-np.sin(angle) / 16.0)
    fwd = f_re.astype(np.float64) + 1j * f_im.astype(np.float64)
    freq = np.where(index < N // 2, index, index - N)
    phase = np.exp(-2j * np.pi * ((freq * freq) % (4 * N)) / (4 * N))
    prop = np.conj(fwd) @ (phase[:, None] * fwd)
    return np.stack([f_re, f_im, rounded(prop.real), rounded(prop.imag)])


def remote(src, dst, send, recv, device):
    return pltpu.make_async_remote_copy(
        src_ref=src, dst_ref=dst, send_sem=send, recv_sem=recv, device_id=device, device_id_type=MESH
    )


def main_kernel(
    count_ref, pos_hbm, tile_hbm, probe_hbm, meas_hbm, table_hbm, out_hbm, pout_ref,
    pos_ref, row, rows_in, tab, tile_0, tile_1, probe, meas, tabs, e_f, e_i, e_h, e_c, hsend, hrecv, local, offer, offered, rising, risen, pattern, win, v, u, arr, far, cur,
    gsend, wins, acc, done, tsend, trecv, bsend, brecv, csend, crecv, esend, erecv, ysend, yrecv, zsend, zrecv, xall,
    dma, send, recv,
):
    s, o = lax.axis_index("scan"), lax.axis_index("obj")
    x, core = lax.div(s, jnp.int32(2)), rem(s, 2)
    y, z = lax.div(o, jnp.int32(NZ)), rem(o, NZ)
    other = 1 - core
    partner = 2 * x + other
    right = [2 * rem(x + 1, NX) + c for c in range(2)]
    left = [2 * rem(x + 3, NX) + c for c in range(2)]
    right_me, left_me = 2 * rem(x + 1, NX) + core, 2 * rem(x + 3, NX) + core
    x_left, x_right, x_far = rem(x + 3, NX), rem(x + 1, NX), rem(x + 2, NX)
    far_at = [2 * rem(x + 2, NX) + c for c in range(2)]
    up, down = rem(o + 1, NO), rem(o + NO - 1, NO)
    tile = (tile_0, tile_1)
    sends, gone = [], []

    barrier = pltpu.get_barrier_semaphore()
    peers = [(s, y * NZ + rem(z + k, NZ)) for k in (4, 3, 5, 2, 6, 1, 7)]
    peers += [(rem(s + k, NS), down) for k in (4, 5, 3, 2, 6, 1, 7, 0)] + [(s, up), (partner, up)]
    peers += [(rem(s + k, NS), o) for k in (4, 5, 3, 2, 6, 1, 7)]
    peers += [(s, rem(y + k, NY) * NZ + z) for k in (2, 1, 3)]
    for peer in peers:
        pl.semaphore_signal(barrier, inc=1, device_id=peer, device_id_type=MESH)

    given = pltpu.make_async_copy(pos_hbm, pos_ref, dma.at[4 + 2 * NS])
    given.start()
    loads = [
        pltpu.make_async_copy(table_hbm, tabs, dma.at[0]),
        pltpu.make_async_copy(probe_hbm, probe, dma.at[1]),
        pltpu.make_async_copy(meas_hbm, meas.at[pl.ds(2 * x, 2)], dma.at[2]),
    ]
    for layer in range(2):
        for b in range(NS):
            block = tile_hbm.at[layer, :, :, pl.ds(b * N, N)]
            loads.append(pltpu.make_async_copy(block, tile[layer].at[b], dma.at[3 + NS * layer + b]))
    for load in loads:
        load.start()

    lane = lax.broadcasted_iota(jnp.int32, (1, 128), 1)
    given.wait()
    line = jnp.zeros((1, 128), jnp.int32)
    for j, value in enumerate((pos_ref[0, 0], pos_ref[0, 1], pos_ref[1, 0], pos_ref[1, 1], count_ref[0, 0])):
        line = jnp.where(lane == j, value, line)
    row[...] = line
    rows_in[s] = line

    def one_hot(shape, rule):
        a, b = lax.broadcasted_iota(jnp.int32, shape, 0), lax.broadcasted_iota(jnp.int32, shape, 1)
        return jnp.where(rule(a, b), 1.0, 0.0).astype(BF)

    def dot(a, b):
        return jnp.dot(a, b, preferred_element_type=F32)

    def col_block(col):
        k = jnp.int32(0)
        for edge in range(1, NS - 1):
            k = k + jnp.where(col >= edge * N, 1, 0)
        return k

    def picks(offset):
        return [one_hot((N, N), lambda a, b: a + h * N == b + offset) for h in range(2)]

    def columns(layer, part, k, pick):
        first, second = tile[layer][k, part].astype(BF), tile[layer][k + 1, part].astype(BF)
        return (dot(first, pick[0]) + dot(second, pick[1])).astype(BF)


    pl.semaphore_wait(barrier, len(peers))

    def start(copy):
        copy.start()
        sends.append(copy)

    def meas_copy(q, slot, n, peer):
        ref = meas.at[pl.ds(slot, n)]
        return remote(ref, ref, send.at[q], recv.at[q], (peer, o))

    def place_copy(k, base, owner):
        peer = (rem(s + k, NS), up if base else o)
        return remote(row, rows_in.at[base + owner], send.at[125 + base + k], recv.at[125 + base + k], peer)

    every = [(k, base) for base in (0, NS) for k in range(NS) if base or k]
    for k, base in every:
        start(place_copy(k, base, s))
    for q, k, peer in ((1, 0, right_me), (2, 1, left_me), (6, 1, right_me), (7, 0, left_me)):
        start(remote(meas_hbm.at[pl.ds(k, 1)], meas.at[pl.ds(2 * x + k, 1)], send.at[q], recv.at[q], (peer, o)))
    loads[0].wait()
    for e_ref, re, im, sign in ((e_f, 0, 1, 1), (e_i, 0, 1, -1), (e_h, 2, 3, 1), (e_c, 2, 3, -1)):
        e_ref[0:N, 0:N] = tabs[re]
        e_ref[N:, N:] = tabs[re]
        e_ref[0:N, N:] = -tabs[im] if sign > 0 else tabs[im]
        e_ref[N:, 0:N] = tabs[im] if sign > 0 else -tabs[im]

    for k, base in every:
        place_copy(k, base, rem(s + NS - k, NS)).wait_recv()
    fetch = pltpu.make_async_copy(rows_in, tab, dma.at[3 + 2 * NS])
    fetch.start()
    fetch.wait()

    def assigned(base, n):
        begin, found = jnp.int32(0), [jnp.int32(0)] * 4
        for t in range(NS):
            count = tab[base + t, 0, 4]
            for k in range(2):
                hit = (k < count) & (begin + k == n)
                values = (jnp.int32(t % 2), jnp.int32(2 * (t // 2) + k), tab[base + t, 0, 2 * k], tab[base + t, 0, 2 * k + 1])
                for j, value in enumerate(values):
                    found[j] = jnp.where(hit, value, found[j])
            begin = begin + count
        return found

    _, _, _, col_out = assigned(NS * other, x + NX * core)
    k_out = col_block(col_out)
    pick_out = picks(col_out - k_out * N)
    halo_to = jnp.where(core == 0, down, up)

    def halo_copy(layer, part):
        q = 143 + 2 * layer + part
        return remote(hsend.at[layer, part], hrecv.at[layer, part], send.at[q], recv.at[q], (s, halo_to))

    for layer in range(2):
        for b in range(NS):
            loads[3 + NS * layer + b].wait()
        for part in range(2):
            hsend[layer, part] = columns(layer, part, k_out, pick_out)
            start(halo_copy(layer, part))
    meas_copy(1, 2 * x_left, 1, right_me).wait_recv()
    start(meas_copy(3, 2 * x_left, 1, right_me))
    meas_copy(2, 2 * x_right + 1, 1, left_me).wait_recv()
    start(meas_copy(5, 2 * x_right + 1, 1, left_me))
    half_mine, slot_mine, row0, col0 = assigned(NS * core, x + NX * core)
    k_own = col_block(col0)
    pick_own = picks(col0 - k_own * N)
    for layer in range(2):
        for part in range(2):
            local[layer, part] = columns(layer, part, k_own, pick_own)
    places = [assigned(NS * (d % 2), d // 2 + NX * (d % 2))[2:] for d in range(NS)]
    _, slot_a, _, _ = assigned(0, x)
    _, slot_b, _, _ = assigned(0, x + NX)
    rows_own = one_hot((N, N), lambda a, b: b + N * core == a + row0)
    rows_halo = one_hot((N, N), lambda a, b: b + N * other == a + row0)
    turn = jnp.where(col0 == 7 * N, 0, col0 - k_own * N)
    turn_rows = one_hot((N, N), lambda a, b: (b + row0 == a) | (b + row0 == a + N))
    turn_cols = one_hot((N, N), lambda a, b: (a + turn == b) | (a + turn == b + N))
    loads[1].wait()

    def window(layer):
        for part in range(2):
            halo_copy(layer, part).wait_recv()
            win[layer, part] = dot(rows_own, local[layer, part]) + dot(rows_halo, hrecv[layer, part])

    step = 32

    def by_rows(body):
        def run(i, carry):
            body(pl.ds(pl.multiple_of(i * step, step), step), i)
            return carry

        lax.fori_loop(0, N // step, run, 0)

    def put(m, rows, i, re, im):
        v[pl.ds(pl.multiple_of(i * step, step), step), m * N : (m + 1) * N] = re.astype(BF)
        v[pl.ds(pl.multiple_of(N + i * step, step), step), m * N : (m + 1) * N] = im.astype(BF)

    def left_mul(matrix):
        for m in range(2):
            product = dot(matrix[...], v[:, m * N : (m + 1) * N])
            u[m * N : (m + 1) * N, 0:N] = product[0:N].astype(BF)
            u[m * N : (m + 1) * N, N:] = product[N:].astype(BF)

    def right_mul(matrix, result):
        for part in range(2):
            product = dot(u[...], matrix[:, part * N : (part + 1) * N])
            result[0, part] = product[0:N]
            result[1, part] = product[N:]

    for q, slot, peer in ((3, 2 * x_far, right_me), (5, 2 * x_far + 1, left_me), (6, 2 * x_left + 1, right_me), (7, 2 * x_right, left_me)):
        meas_copy(q, slot, 1, peer).wait_recv()
    loads[2].wait()
    rising[...] = meas[slot_b]
    start(remote(rising, risen.at[core], send.at[141], recv.at[141 + core], (2 * x + 1, up)))
    offer[...] = meas[slot_a]
    offer_copy = remote(offer, offered, send.at[0], recv.at[0], (2 * x, o))

    @pl.when(core == 1)
    def _():
        offer_copy.start()

    window(0)

    def enter(rows, i):
        re, im = win[0, 0, rows, :], win[0, 1, rows, :]
        for m in range(2):
            pr, pi = probe[m, 0, rows, :], probe[m, 1, rows, :]
            put(m, rows, i, pr * re - pi * im, pr * im + pi * re)

    by_rows(enter)
    left_mul(e_h)
    right_mul(e_c, arr)
    window(1)

    def second(rows, i):
        re, im = win[1, 0, rows, :], win[1, 1, rows, :]
        for m in range(2):
            pr, pi = arr[m, 0, rows, :], arr[m, 1, rows, :]
            put(m, rows, i, pr * re - pi * im, pr * im + pi * re)

    by_rows(second)
    left_mul(e_f)
    right_mul(e_i, far)

    @pl.when(core == 0)
    def _():
        offer_copy.wait_recv()
        pattern[...] = jnp.where(half_mine == 0, offer[...], offered[...])

    @pl.when(core == 1)
    def _():
        for c in range(2):
            remote(rising, risen.at[c], send.at[141], recv.at[141 + c], (s, up)).wait_recv()
        pattern[...] = jnp.where(half_mine == 0, risen[0], risen[1])

    def misfit(rows, i):
        parts = [(far[m, 0, rows, :], far[m, 1, rows, :]) for m in range(2)]
        total = parts[0][0] ** 2 + parts[0][1] ** 2 + (parts[1][0] ** 2 + parts[1][1] ** 2)
        gap = total - pattern[rows, :].astype(F32)
        for m in range(2):
            put(m, rows, i, gap * parts[m][0], gap * parts[m][1])

    by_rows(misfit)
    left_mul(e_i)
    right_mul(e_f, cur)

    chunks = [(1, 0, 128), (1, 128, 128), (0, 0, 96), (0, 96, 96), (0, 192, 32), (0, 224, 32)]

    def span(j, part=None):
        _, first, size = chunks[j]
        return pl.ds(first, size) if part is None else pl.ds(first + part * size // 2, size // 2)

    def near(j, c, side):
        layer, q = chunks[j][0], 11 + 16 * j + (2 if side else 4)
        peer = (right if side else left)[c]
        return remote(
            gsend.at[layer, c, span(j)], wins.at[layer, s, span(j)], send.at[q + c], recv.at[q + core], (peer, o)
        )

    def near_in(j, c, side):
        layer, q = chunks[j][0], 11 + 16 * j + (2 if side else 4)
        slot = wins.at[layer, (left if side else right)[c], span(j)]
        return remote(slot, slot, send.at[q + c], recv.at[q + c], (partner, o))

    def relay(j, c, side, incoming=False):
        q = 11 + 16 * j + (6 if side else 8) + c
        owner = far_at[c] if incoming else (left if side else right)[c]
        piece = wins.at[chunks[j][0], owner, span(j, 0 if side else 1)]
        return remote(piece, piece, send.at[q], recv.at[q], (right_me if side else left_me, o))

    def pair(j, incoming=False):
        layer, q = chunks[j][0], 11 + 16 * j
        slot = wins.at[layer, partner if incoming else s, span(j)]
        return remote(gsend.at[layer, other, span(j)], slot, send.at[q], recv.at[q], (partner, o))

    def share(layer, first, adjoint, ready=None):
        for part in range(2):
            if part == 0:
                term = lambda m: first[m, 0] * adjoint[m, 0] + first[m, 1] * adjoint[m, 1]
            else:
                term = lambda m: first[m, 0] * adjoint[m, 1] - first[m, 1] * adjoint[m, 0]
            grad = (term(0) + term(1)).astype(BF)
            gsend[layer, part] = dot(dot(turn_rows, grad).astype(BF), turn_cols).astype(BF)
            if ready is not None:
                start(near(ready, part, 1))
                start(near(ready, part, 0))
        wins[layer, s] = gsend[layer, core]

    def launch(j):
        for c in range(2):
            start(near(j, c, 1))
            start(near(j, c, 0))
        start(pair(j))

    def pass_on(j):
        for c in range(2):
            for side in (1, 0):
                near_in(j, c, side).wait_recv()
                start(relay(j, c, side))

    lane = lax.broadcasted_iota(jnp.int32, (1, N), 1)
    cols = [
        [jnp.where((lane + (2 * x + b) * N >= c0) & (lane + (2 * x + b) * N < c0 + N), 1.0, 0.0) for b in range(2)]
        for _, c0 in places
    ]

    def gather(j):
        layer, first, size = chunks[j]
        chunk = 16

        def run(i, carry):
            at = pl.multiple_of(first + i * chunk, chunk)
            rows = pl.ds(at, chunk)
            line = lax.broadcasted_iota(jnp.int32, (chunk, N), 0) + at
            sums = [[jnp.zeros((chunk, N), F32) for _ in range(3)] for _ in range(2)]
            for n in range(NS):
                term = wins[layer, n, rows, :].astype(F32)
                above = line >= places[n][0]
                for b in range(2):
                    masked = term * cols[n][b]
                    low, high = (2, 0) if n % 2 else (0, 1)
                    sums[b][low] = sums[b][low] + jnp.where(above, masked, 0.0)
                    sums[b][high] = sums[b][high] + jnp.where(above, 0.0, masked)
            mine = core == 0
            acc[layer, rows, :] = jnp.where(mine, sums[0][0], sums[1][0])
            tsend[layer, rows, :] = jnp.where(mine, sums[1][0], sums[0][0]).astype(BF)
            for b in range(2):
                bsend[layer, b, rows, :] = sums[b][1].astype(BF)
                csend[layer, b, rows, :] = sums[b][2].astype(BF)
            return carry

        lax.fori_loop(0, size // chunk, run, 0)

    def top_copy(j):
        layer, q = chunks[j][0], 21 + 16 * j
        return remote(tsend.at[layer, span(j)], trecv.at[layer, span(j)], send.at[q], recv.at[q], (partner, o))

    def edge(j, upward):
        q = 22 + 16 * j + (0 if upward else 2)
        return (bsend, brecv, q, up) if upward else (csend, crecv, q, down)

    def edge_copy(j, b, upward):
        layer, (source, target, q, to) = chunks[j][0], edge(j, upward)
        return remote(
            source.at[layer, b, span(j)], target.at[layer, core, span(j)], send.at[q + b], recv.at[q + core], (2 * x + b, to)
        )

    def edge_in(j, c, upward):
        layer, (source, target, q, to) = chunks[j][0], edge(j, upward)
        return remote(source.at[layer, c, span(j)], target.at[layer, c, span(j)], send.at[q + c], recv.at[q + c], (s, to))

    def collect(j):
        pair(j, True).wait_recv()
        for c in range(2):
            for side in (1, 0):
                relay(j, c, side, True).wait_recv()
        gather(j)
        for b in range(2):
            start(edge_copy(j, b, True))
            start(edge_copy(j, b, False))
        start(top_copy(j))

    def finish(j):
        layer = chunks[j][0]
        top_copy(j).wait_recv()
        for c in range(2):
            edge_in(j, c, True).wait_recv()
            edge_in(j, c, False).wait_recv()
        for i in range(2):
            rows = span(j, i)
            rims = [brecv[layer, c, rows, :].astype(F32) + crecv[layer, c, rows, :].astype(F32) for c in (core, other)]
            done[layer, core, rows, :] = acc[layer, rows, :] + rims[0]
            done[layer, other, rows, :] = trecv[layer, rows, :].astype(F32) + rims[1]
        leaving = pltpu.make_async_copy(
            done.at[layer, :, span(j)], out_hbm.at[layer, :, span(j)], dma.at[6 + 2 * NS + j]
        )
        leaving.start()
        gone.append(leaving)

    share(1, arr, cur, ready=0)
    start(pair(0))
    launch(1)

    def behind(rows, i):
        re, im = win[1, 0, rows, :], win[1, 1, rows, :]
        for m in range(2):
            cr, ci = cur[m, 0, rows, :], cur[m, 1, rows, :]
            put(m, rows, i, re * cr + im * ci, re * ci - im * cr)

    by_rows(behind)
    left_mul(e_c)
    right_mul(e_h, cur)

    def leave(rows, i):
        re, im = win[0, 0, rows, :], win[0, 1, rows, :]
        for m in range(2):
            cr, ci = cur[m, 0, rows, :], cur[m, 1, rows, :]
            esend[m, 0, rows, :] = (re * cr + im * ci).astype(BF)
            esend[m, 1, rows, :] = (re * ci - im * cr).astype(BF)

    by_rows(leave)
    q_pair, q_y, q_z, q_x = 107, 108, 111, 118
    e_copy = remote(esend.at[other], erecv, send.at[q_pair], recv.at[q_pair], (partner, o))
    start(e_copy)
    share(0, probe, cur)
    e_copy.wait_recv()

    def add_pair(rows, i):
        for part in range(2):
            ysend[part, rows, :] = (esend[core, part, rows, :].astype(F32) + erecv[part, rows, :].astype(F32)).astype(BF)

    by_rows(add_pair)
    deep = N // NY
    y_copies = []
    for k in range(1, NY):
        y_to = rem(y + k, NY)
        rows_to = pl.ds(pl.multiple_of(y_to * deep, deep), deep)
        copy = remote(
            ysend.at[:, rows_to, :], yrecv.at[k - 1], send.at[q_y + k - 1], recv.at[q_y + k - 1], (s, y_to * NZ + z)
        )
        start(copy)
        y_copies.append(copy)
    pass_on(0)
    launch(2)
    pass_on(1)
    launch(3)
    for copy in y_copies:
        copy.wait_recv()
    rows_me = pl.ds(pl.multiple_of(y * deep, deep), deep)
    totals = []
    for part in range(2):
        total = ysend[part, rows_me, :].astype(F32)
        for k in range(NY - 1):
            total = total + yrecv[k, part].astype(F32)
        totals.append(total)
    for k in range(NZ):
        zsend[k] = jnp.concatenate([total[8 * k : 8 * k + 8] for total in totals], axis=0).astype(BF)
    z_copies = []
    for k in range(1, NZ):
        z_to = rem(z + k, NZ)
        copy = remote(
            zsend.at[z_to], zrecv.at[k - 1], send.at[q_z + k - 1], recv.at[q_z + k - 1], (s, y * NZ + z_to)
        )
        start(copy)
        z_copies.append(copy)
    collect(0)
    pass_on(2)
    launch(4)
    collect(1)
    pass_on(3)
    launch(5)
    for copy in z_copies:
        copy.wait_recv()
    total = zsend[z].astype(F32)
    for k in range(NZ - 1):
        total = total + zrecv[k].astype(F32)
    xall[0] = total.astype(BF)
    x_copies = []
    for k in range(1, NS):
        copy = remote(xall.at[0], xall.at[k], send.at[q_x + k - 1], recv.at[q_x + k - 1], (rem(s + k, NS), o))
        start(copy)
        x_copies.append(copy)
    collect(2)
    pass_on(4)
    collect(3)
    pass_on(5)
    collect(4)
    collect(5)
    for copy in x_copies:
        copy.wait_recv()
    pick = one_hot((N, 128), lambda a, b: a == b + 32 * s)
    factor = 1.0 / math.sqrt(256.0)
    shares = [dot(xall[k], pick) for k in range(NS)]
    mine = (shares[0] + shares[2] + (shares[4] + shares[6])) * factor
    theirs = (shares[1] + shares[3] + (shares[5] + shares[7])) * factor
    for part in range(2):
        pout_ref[core, part] = mine[8 * part : 8 * part + 8, :32]
        pout_ref[other, part] = theirs[8 * part : 8 * part + 8, :32]
    for j in range(len(chunks)):
        finish(j)
    for copy in gone:
        copy.wait()
    for copy in sends:
        copy.wait_send()

    @pl.when(core == 1)
    def _():
        offer_copy.wait_send()


def hand_on(grad_ref, probe_ref, grad_out, probe_out, sem):
    copies = [
        pltpu.make_async_copy(grad_ref, grad_out, sem.at[0]),
        pltpu.make_async_copy(probe_ref, probe_out, sem.at[1]),
    ]
    for copy in copies:
        copy.start()
    for copy in copies:
        copy.wait()


def body(object_slices, probe, measured, positions, counts):
    vmem = pltpu.VMEM
    square = lambda *lead: (*lead, N, N)
    any_spec = pl.BlockSpec(memory_space=pl.ANY)
    given = [
        pltpu.with_memory_space_constraint(value, pltpu.HBM)
        for value in (positions[0, 0], object_slices, probe, measured[0, 0], jnp.asarray(tables()))
    ]
    results = pl.pallas_call(
        main_kernel,
        out_shape=(
            jax.ShapeDtypeStruct(square(2, 2), F32),
            jax.ShapeDtypeStruct((2, 2, 8, 32), F32),
        ),
        in_specs=[pl.BlockSpec(memory_space=pltpu.SMEM)] + [any_spec] * 5,
        out_specs=(any_spec, pl.BlockSpec(memory_space=vmem)),
        scratch_shapes=[
            pltpu.SMEM((2, 2), jnp.int32),
            vmem((1, 128), jnp.int32),
            vmem((2 * NS, 1, 128), jnp.int32),
            pltpu.SMEM((2 * NS, 1, 128), jnp.int32),
            *[vmem(square(NS, 2), F32)] * 2,
            vmem(square(2, 2), F32),
            vmem(square(2 * NX), BF),
            vmem(square(4), BF),
            *[vmem((2 * N, 2 * N), BF)] * 4,
            vmem(square(2, 2), BF),
            vmem(square(2, 2), BF),
            vmem(square(2, 2), BF),
            *[vmem(square(), BF)] * 3,
            vmem(square(2), BF),
            vmem(square(), BF),
            vmem(square(2, 2), F32),
            vmem((2 * N, 2 * N), BF),
            vmem((2 * N, 2 * N), BF),
            vmem(square(2, 2), F32),
            vmem(square(2, 2), F32),
            vmem(square(2, 2), F32),
            vmem(square(2, 2), BF),
            vmem(square(2, NS), BF),
            vmem(square(2), F32),
            vmem(square(2, 2), F32),
            vmem(square(2), BF),
            vmem(square(2), BF),
            *[vmem(square(2, 2), BF)] * 4,
            vmem(square(2, 2), BF),
            vmem(square(2), BF),
            vmem(square(2), BF),
            vmem((NY - 1, 2, N // NY, N), BF),
            vmem((NZ, 16, N), BF),
            vmem((NZ - 1, 16, N), BF),
            vmem((NS, 16, N), BF),
            pltpu.SemaphoreType.DMA((12 + 2 * NS,)),
            pltpu.SemaphoreType.DMA((147,)),
            pltpu.SemaphoreType.DMA((147,)),
        ],
        compiler_params=pltpu.CompilerParams(
            collective_id=0, has_side_effects=True, vmem_limit_bytes=44 * 1024 * 1024
        ),
        name="gradient",
    )(counts, *given)
    return pl.pallas_call(
        hand_on,
        out_shape=tuple(jax.ShapeDtypeStruct(r.shape, F32) for r in results),
        in_specs=[any_spec] * 2,
        out_specs=(any_spec, any_spec),
        scratch_shapes=[pltpu.SemaphoreType.DMA((2,))],
        compiler_params=pltpu.CompilerParams(vmem_limit_bytes=8 * 1024 * 1024),
        name="results",
    )(*results)


def solution(mesh):
    return jax.shard_map(
        body,
        mesh=mesh,
        in_specs=(
            P(None, None, "obj", None),
            P(),
            P("scan", "obj", None, None, None),
            P("scan", "obj", None, None),
            P("scan", "obj"),
        ),
        out_specs=(P(None, None, "obj", "scan"), P(None, None, "obj", "scan")),
        check_vma=False,
    )
```

```python
import functools
import math

import jax
import jax.numpy as jnp
import numpy as np
from jax import lax
from jax.experimental import pallas as pl
from jax.experimental.pallas import tpu as pltpu
from jax.sharding import PartitionSpec as P

MESH = pl.DeviceIdType.MESH
BF = jnp.bfloat16
F32 = jnp.float32
N = 256
NS, NX, NO, NY, NZ = 8, 4, 32, 4, 8


def rem(a, b):
    return lax.rem(a, jnp.int32(b))


def tables():
    index = np.arange(N)
    angle = (np.outer(index, index) % N) * (2.0 * np.pi / N)
    rounded = lambda a: a.astype(np.float32).astype(BF)
    f_re, f_im = rounded(np.cos(angle) / 16.0), rounded(-np.sin(angle) / 16.0)
    fwd = f_re.astype(np.float64) + 1j * f_im.astype(np.float64)
    freq = np.where(index < N // 2, index, index - N)
    phase = np.exp(-2j * np.pi * ((freq * freq) % (4 * N)) / (4 * N))
    prop = np.conj(fwd) @ (phase[:, None] * fwd)
    return np.stack([f_re, f_im, rounded(prop.real), rounded(prop.imag)])


def remote(src, dst, send, recv, device):
    return pltpu.make_async_remote_copy(
        src_ref=src, dst_ref=dst, send_sem=send, recv_sem=recv, device_id=device, device_id_type=MESH
    )


def main_kernel(
    count_ref, pos_hbm, tile_hbm, probe_hbm, meas_hbm, table_hbm, out_hbm, pout_ref,
    pos_ref, row, rows_in, tab, tile_0, tile_1, probe, meas, tabs, e_f, e_i, e_h, e_c, hsend, hrecv, local, offer, offered, rising, risen, pattern, win, v, u, arr, far, cur,
    gsend, wins, acc, done, tsend, trecv, bsend, brecv, csend, crecv, esend, erecv, ysend, yrecv, zsend, zrecv, xall,
    dma, send, recv,
):
    s, o = lax.axis_index("scan"), lax.axis_index("obj")
    x, core = lax.div(s, jnp.int32(2)), rem(s, 2)
    y, z = lax.div(o, jnp.int32(NZ)), rem(o, NZ)
    other = 1 - core
    partner = 2 * x + other
    right = [2 * rem(x + 1, NX) + c for c in range(2)]
    left = [2 * rem(x + 3, NX) + c for c in range(2)]
    right_me, left_me = 2 * rem(x + 1, NX) + core, 2 * rem(x + 3, NX) + core
    x_left, x_right, x_far = rem(x + 3, NX), rem(x + 1, NX), rem(x + 2, NX)
    far_at = [2 * rem(x + 2, NX) + c for c in range(2)]
    up, down = rem(o + 1, NO), rem(o + NO - 1, NO)
    tile = (tile_0, tile_1)
    sends, gone, made = {}, [], []

    def remote_at(src, dst, place, recv_sem, device):
        copy = remote(src, dst, send.at[place], recv_sem, device)
        made.append((copy, place))
        return copy

    barrier = pltpu.get_barrier_semaphore()
    peers = [(s, y * NZ + rem(z + k, NZ)) for k in (4, 3, 5, 2, 6, 1, 7)]
    peers += [(rem(s + k, NS), down) for k in (4, 5, 3, 2, 6, 1, 7, 0)] + [(s, up), (partner, up)]
    peers += [(rem(s + k, NS), o) for k in (4, 5, 3, 2, 6, 1, 7)]
    peers += [(s, rem(y + k, NY) * NZ + z) for k in (2, 1, 3)]
    for peer in peers:
        pl.semaphore_signal(barrier, inc=1, device_id=peer, device_id_type=MESH)

    given = pltpu.make_async_copy(pos_hbm, pos_ref, dma.at[4 + 2 * NS])
    given.start()
    loads = [
        pltpu.make_async_copy(table_hbm, tabs, dma.at[0]),
        pltpu.make_async_copy(probe_hbm, probe, dma.at[1]),
        pltpu.make_async_copy(meas_hbm, meas.at[pl.ds(2 * x, 2)], dma.at[2]),
    ]
    for layer in range(2):
        for b in range(NS):
            block = tile_hbm.at[layer, :, :, pl.ds(b * N, N)]
            loads.append(pltpu.make_async_copy(block, tile[layer].at[b], dma.at[3 + NS * layer + b]))
    for load in loads:
        load.start()

    lane = lax.broadcasted_iota(jnp.int32, (1, 128), 1)
    given.wait()
    line = jnp.zeros((1, 128), jnp.int32)
    for j, value in enumerate((pos_ref[0, 0], pos_ref[0, 1], pos_ref[1, 0], pos_ref[1, 1], count_ref[0, 0])):
        line = jnp.where(lane == j, value, line)
    row[...] = line
    rows_in[s] = line

    def one_hot(shape, rule):
        a, b = lax.broadcasted_iota(jnp.int32, shape, 0), lax.broadcasted_iota(jnp.int32, shape, 1)
        return jnp.where(rule(a, b), 1.0, 0.0).astype(BF)

    def dot(a, b):
        return jnp.dot(a, b, preferred_element_type=F32)

    def col_block(col):
        k = jnp.int32(0)
        for edge in range(1, NS - 1):
            k = k + jnp.where(col >= edge * N, 1, 0)
        return k

    def picks(offset):
        return [one_hot((N, N), lambda a, b: a + h * N == b + offset) for h in range(2)]

    def columns(layer, part, k, pick):
        first, second = tile[layer][k, part].astype(BF), tile[layer][k + 1, part].astype(BF)
        return (dot(first, pick[0]) + dot(second, pick[1])).astype(BF)


    pl.semaphore_wait(barrier, len(peers))

    def start(copy):
        place = next(i for c, i in made if c is copy)
        if place in sends:
            sends[place].wait_send()
        copy.start()
        sends[place] = copy

    def meas_copy(q, slot, n, peer):
        ref = meas.at[pl.ds(slot, n)]
        return remote_at(ref, ref, q, recv.at[q], (peer, o))

    def place_copy(k, base, owner):
        peer = (rem(s + k, NS), up if base else o)
        return remote_at(row, rows_in.at[base + owner], 35 + base + k, recv.at[95 + base + k], peer)

    every = [(k, base) for base in (0, NS) for k in range(NS) if base or k]
    for k, base in every:
        start(place_copy(k, base, s))
    for q, k, peer in ((1, 0, right_me), (2, 1, left_me), (6, 1, right_me), (7, 0, left_me)):
        start(remote_at(meas_hbm.at[pl.ds(k, 1)], meas.at[pl.ds(2 * x + k, 1)], q, recv.at[q], (peer, o)))
    loads[0].wait()
    for e_ref, re, im, sign in ((e_f, 0, 1, 1), (e_i, 0, 1, -1), (e_h, 2, 3, 1), (e_c, 2, 3, -1)):
        e_ref[0:N, 0:N] = tabs[re]
        e_ref[N:, N:] = tabs[re]
        e_ref[0:N, N:] = -tabs[im] if sign > 0 else tabs[im]
        e_ref[N:, 0:N] = tabs[im] if sign > 0 else -tabs[im]

    for k, base in every:
        place_copy(k, base, rem(s + NS - k, NS)).wait_recv()
    fetch = pltpu.make_async_copy(rows_in, tab, dma.at[3 + 2 * NS])
    fetch.start()
    fetch.wait()

    def assigned(base, n):
        begin, found = jnp.int32(0), [jnp.int32(0)] * 4
        for t in range(NS):
            count = tab[base + t, 0, 4]
            for k in range(2):
                hit = (k < count) & (begin + k == n)
                values = (jnp.int32(t % 2), jnp.int32(2 * (t // 2) + k), tab[base + t, 0, 2 * k], tab[base + t, 0, 2 * k + 1])
                for j, value in enumerate(values):
                    found[j] = jnp.where(hit, value, found[j])
            begin = begin + count
        return found

    _, _, _, col_out = assigned(NS * other, x + NX * core)
    k_out = col_block(col_out)
    pick_out = picks(col_out - k_out * N)
    halo_to = jnp.where(core == 0, down, up)

    def halo_copy(layer, part):
        q = 2 * layer + part
        return remote_at(hsend.at[layer, part], hrecv.at[layer, part], 51 + q, recv.at[113 + q], (s, halo_to))

    for layer in range(2):
        for b in range(NS):
            loads[3 + NS * layer + b].wait()
        for part in range(2):
            hsend[layer, part] = columns(layer, part, k_out, pick_out)
            start(halo_copy(layer, part))
    meas_copy(1, 2 * x_left, 1, right_me).wait_recv()
    start(meas_copy(3, 2 * x_left, 1, right_me))
    meas_copy(2, 2 * x_right + 1, 1, left_me).wait_recv()
    start(meas_copy(5, 2 * x_right + 1, 1, left_me))
    half_mine, slot_mine, row0, col0 = assigned(NS * core, x + NX * core)
    k_own = col_block(col0)
    pick_own = picks(col0 - k_own * N)
    for layer in range(2):
        for part in range(2):
            local[layer, part] = columns(layer, part, k_own, pick_own)
    places = [assigned(NS * (d % 2), d // 2 + NX * (d % 2))[2:] for d in range(NS)]
    _, slot_a, _, _ = assigned(0, x)
    _, slot_b, _, _ = assigned(0, x + NX)
    rows_own = one_hot((N, N), lambda a, b: b + N * core == a + row0)
    rows_halo = one_hot((N, N), lambda a, b: b + N * other == a + row0)
    turn = jnp.where(col0 == 7 * N, 0, col0 - k_own * N)
    turn_rows = one_hot((N, N), lambda a, b: (b + row0 == a) | (b + row0 == a + N))
    turn_cols = one_hot((N, N), lambda a, b: (a + turn == b) | (a + turn == b + N))
    loads[1].wait()

    def window(layer):
        for part in range(2):
            halo_copy(layer, part).wait_recv()
            win[layer, part] = dot(rows_own, local[layer, part]) + dot(rows_halo, hrecv[layer, part])

    step = 32

    def by_rows(body):
        def run(i, carry):
            body(pl.ds(pl.multiple_of(i * step, step), step), i)
            return carry

        lax.fori_loop(0, N // step, run, 0)

    def put(m, rows, i, re, im):
        v[pl.ds(pl.multiple_of(i * step, step), step), m * N : (m + 1) * N] = re.astype(BF)
        v[pl.ds(pl.multiple_of(N + i * step, step), step), m * N : (m + 1) * N] = im.astype(BF)

    def left_mul(matrix):
        for m in range(2):
            product = dot(matrix[...], v[:, m * N : (m + 1) * N])
            u[m * N : (m + 1) * N, 0:N] = product[0:N].astype(BF)
            u[m * N : (m + 1) * N, N:] = product[N:].astype(BF)

    def right_mul(matrix, result):
        for part in range(2):
            product = dot(u[...], matrix[:, part * N : (part + 1) * N])
            result[0, part] = product[0:N]
            result[1, part] = product[N:]

    for q, slot, peer in ((3, 2 * x_far, right_me), (5, 2 * x_far + 1, left_me), (6, 2 * x_left + 1, right_me), (7, 2 * x_right, left_me)):
        meas_copy(q, slot, 1, peer).wait_recv()
    loads[2].wait()
    rising[...] = meas[slot_b]
    start(remote_at(rising, risen.at[core], 55, recv.at[111 + core], (2 * x + 1, up)))
    offer[...] = meas[slot_a]
    offer_copy = remote_at(offer, offered, 0, recv.at[0], (2 * x, o))

    @pl.when(core == 1)
    def _():
        offer_copy.start()

    window(0)

    def enter(rows, i):
        re, im = win[0, 0, rows, :], win[0, 1, rows, :]
        for m in range(2):
            pr, pi = probe[m, 0, rows, :], probe[m, 1, rows, :]
            put(m, rows, i, pr * re - pi * im, pr * im + pi * re)

    by_rows(enter)
    left_mul(e_h)
    right_mul(e_c, arr)
    window(1)

    def second(rows, i):
        re, im = win[1, 0, rows, :], win[1, 1, rows, :]
        for m in range(2):
            pr, pi = arr[m, 0, rows, :], arr[m, 1, rows, :]
            put(m, rows, i, pr * re - pi * im, pr * im + pi * re)

    by_rows(second)
    left_mul(e_f)
    right_mul(e_i, far)

    @pl.when(core == 0)
    def _():
        offer_copy.wait_recv()
        pattern[...] = jnp.where(half_mine == 0, offer[...], offered[...])

    @pl.when(core == 1)
    def _():
        for c in range(2):
            remote_at(rising, risen.at[c], 55, recv.at[111 + c], (s, up)).wait_recv()
        pattern[...] = jnp.where(half_mine == 0, risen[0], risen[1])

    def misfit(rows, i):
        parts = [(far[m, 0, rows, :], far[m, 1, rows, :]) for m in range(2)]
        total = parts[0][0] ** 2 + parts[0][1] ** 2 + (parts[1][0] ** 2 + parts[1][1] ** 2)
        gap = total - pattern[rows, :].astype(F32)
        for m in range(2):
            put(m, rows, i, gap * parts[m][0], gap * parts[m][1])

    by_rows(misfit)
    left_mul(e_i)
    right_mul(e_f, cur)

    chunks = [(1, 0, 128), (1, 128, 128), (0, 0, 128), (0, 128, 64), (0, 192, 64)]

    def span(j, part=None):
        _, first, size = chunks[j]
        return pl.ds(first, size) if part is None else pl.ds(first + part * size // 2, size // 2)

    def near(j, c, side):
        layer, q, sq = chunks[j][0], 8 + 14 * j + (1 if side else 3), 8 + 14 * (j % 2) + (1 if side else 3)
        peer = (right if side else left)[c]
        return remote_at(
            gsend.at[layer, c, span(j)], wins.at[layer, s, span(j)], sq + c, recv.at[q + core], (peer, o)
        )

    def near_in(j, c, side):
        layer, q, sq = chunks[j][0], 8 + 14 * j + (1 if side else 3), 8 + 14 * (j % 2) + (1 if side else 3)
        slot = wins.at[layer, (left if side else right)[c], span(j)]
        return remote_at(slot, slot, sq + c, recv.at[q + c], (partner, o))

    def relay(j, c, side, incoming=False):
        q, sq = 8 + 14 * j + (5 if side else 7) + c, 8 + 14 * (j % 2) + (5 if side else 7) + c
        owner = far_at[c] if incoming else (left if side else right)[c]
        piece = wins.at[chunks[j][0], owner, span(j, 0 if side else 1)]
        return remote_at(piece, piece, sq, recv.at[q], (right_me if side else left_me, o))

    def pair(j, incoming=False):
        layer, q, sq = chunks[j][0], 8 + 14 * j, 8 + 14 * (j % 2)
        slot = wins.at[layer, partner if incoming else s, span(j)]
        return remote_at(gsend.at[layer, other, span(j)], slot, sq, recv.at[q], (partner, o))

    def share(layer, first, adjoint, ready=None):
        for part in range(2):
            if part == 0:
                term = lambda m: first[m, 0] * adjoint[m, 0] + first[m, 1] * adjoint[m, 1]
            else:
                term = lambda m: first[m, 0] * adjoint[m, 1] - first[m, 1] * adjoint[m, 0]
            grad = (term(0) + term(1)).astype(BF)
            gsend[layer, part] = dot(dot(turn_rows, grad).astype(BF), turn_cols).astype(BF)
            if ready is not None:
                start(near(ready, part, 1))
                start(near(ready, part, 0))
        wins[layer, s] = gsend[layer, core]

    def launch(j):
        for c in range(2):
            start(near(j, c, 1))
            start(near(j, c, 0))
        start(pair(j))

    def pass_on(j):
        for c in range(2):
            for side in (1, 0):
                near_in(j, c, side).wait_recv()
                start(relay(j, c, side))

    lane = lax.broadcasted_iota(jnp.int32, (1, N), 1)
    cols = [
        [jnp.where((lane + (2 * x + b) * N >= c0) & (lane + (2 * x + b) * N < c0 + N), 1.0, 0.0) for b in range(2)]
        for _, c0 in places
    ]

    def gather(j):
        layer, first, size = chunks[j]
        chunk = 16

        def run(i, carry):
            at = pl.multiple_of(first + i * chunk, chunk)
            rows = pl.ds(at, chunk)
            line = lax.broadcasted_iota(jnp.int32, (chunk, N), 0) + at
            sums = [[jnp.zeros((chunk, N), F32) for _ in range(3)] for _ in range(2)]
            for n in range(NS):
                term = wins[layer, n, rows, :].astype(F32)
                above = line >= places[n][0]
                for b in range(2):
                    masked = term * cols[n][b]
                    low, high = (2, 0) if n % 2 else (0, 1)
                    sums[b][low] = sums[b][low] + jnp.where(above, masked, 0.0)
                    sums[b][high] = sums[b][high] + jnp.where(above, 0.0, masked)
            mine = core == 0
            acc[layer, rows, :] = jnp.where(mine, sums[0][0], sums[1][0])
            tsend[layer, rows, :] = jnp.where(mine, sums[1][0], sums[0][0]).astype(BF)
            for b in range(2):
                bsend[layer, b, rows, :] = sums[b][1].astype(BF)
                csend[layer, b, rows, :] = sums[b][2].astype(BF)
            return carry

        lax.fori_loop(0, size // chunk, run, 0)

    def top_copy(j):
        layer, q, sq = chunks[j][0], 17 + 14 * j, 17 + 14 * (j % 2)
        return remote_at(tsend.at[layer, span(j)], trecv.at[layer, span(j)], sq, recv.at[q], (partner, o))

    def edge(j, upward):
        more = 18 + (0 if upward else 2)
        q, sq = more + 14 * j, more + 14 * (j % 2)
        return (bsend, brecv, q, sq, up) if upward else (csend, crecv, q, sq, down)

    def edge_copy(j, b, upward):
        layer, (source, target, q, sq, to) = chunks[j][0], edge(j, upward)
        return remote_at(
            source.at[layer, b, span(j)], target.at[layer, core, span(j)], sq + b, recv.at[q + core], (2 * x + b, to)
        )

    def edge_in(j, c, upward):
        layer, (source, target, q, sq, to) = chunks[j][0], edge(j, upward)
        return remote_at(source.at[layer, c, span(j)], target.at[layer, c, span(j)], sq + c, recv.at[q + c], (s, to))

    def collect(j):
        pair(j, True).wait_recv()
        for c in range(2):
            for side in (1, 0):
                relay(j, c, side, True).wait_recv()
        gather(j)
        for b in range(2):
            start(edge_copy(j, b, True))
            start(edge_copy(j, b, False))
        start(top_copy(j))

    def finish(j):
        layer = chunks[j][0]
        top_copy(j).wait_recv()
        for c in range(2):
            edge_in(j, c, True).wait_recv()
            edge_in(j, c, False).wait_recv()
        for i in range(2):
            rows = span(j, i)
            rims = [brecv[layer, c, rows, :].astype(F32) + crecv[layer, c, rows, :].astype(F32) for c in (core, other)]
            done[layer, core, rows, :] = acc[layer, rows, :] + rims[0]
            done[layer, other, rows, :] = trecv[layer, rows, :].astype(F32) + rims[1]
        leaving = pltpu.make_async_copy(
            done.at[layer, :, span(j)], out_hbm.at[layer, :, span(j)], dma.at[6 + 2 * NS + j]
        )
        leaving.start()
        gone.append(leaving)

    share(1, arr, cur, ready=0)
    start(pair(0))
    launch(1)

    def behind(rows, i):
        re, im = win[1, 0, rows, :], win[1, 1, rows, :]
        for m in range(2):
            cr, ci = cur[m, 0, rows, :], cur[m, 1, rows, :]
            put(m, rows, i, re * cr + im * ci, re * ci - im * cr)

    by_rows(behind)
    left_mul(e_c)
    right_mul(e_h, cur)

    def leave(rows, i):
        re, im = win[0, 0, rows, :], win[0, 1, rows, :]
        for m in range(2):
            cr, ci = cur[m, 0, rows, :], cur[m, 1, rows, :]
            esend[m, 0, rows, :] = (re * cr + im * ci).astype(BF)
            esend[m, 1, rows, :] = (re * ci - im * cr).astype(BF)

    by_rows(leave)
    q_pair, q_y, q_z, q_x = 78, 79, 82, 89
    e_copy = remote_at(esend.at[other], erecv, q_pair - 42, recv.at[q_pair], (partner, o))
    start(e_copy)
    share(0, probe, cur)
    e_copy.wait_recv()

    def add_pair(rows, i):
        for part in range(2):
            ysend[part, rows, :] = (esend[core, part, rows, :].astype(F32) + erecv[part, rows, :].astype(F32)).astype(BF)

    by_rows(add_pair)
    deep = N // NY
    y_copies = []
    for k in range(1, NY):
        y_to = rem(y + k, NY)
        rows_to = pl.ds(pl.multiple_of(y_to * deep, deep), deep)
        copy = remote_at(
            ysend.at[:, rows_to, :], yrecv.at[k - 1], q_y + k - 43, recv.at[q_y + k - 1], (s, y_to * NZ + z)
        )
        start(copy)
        y_copies.append(copy)
    pass_on(0)
    launch(2)
    pass_on(1)
    launch(3)
    for copy in y_copies:
        copy.wait_recv()
    rows_me = pl.ds(pl.multiple_of(y * deep, deep), deep)
    totals = []
    for part in range(2):
        total = ysend[part, rows_me, :].astype(F32)
        for k in range(NY - 1):
            total = total + yrecv[k, part].astype(F32)
        totals.append(total)
    for k in range(NZ):
        zsend[k] = jnp.concatenate([total[8 * k : 8 * k + 8] for total in totals], axis=0).astype(BF)
    z_copies = []
    for k in range(1, NZ):
        z_to = rem(z + k, NZ)
        copy = remote_at(
            zsend.at[z_to], zrecv.at[k - 1], q_z + k - 43, recv.at[q_z + k - 1], (s, y * NZ + z_to)
        )
        start(copy)
        z_copies.append(copy)
    collect(0)
    pass_on(2)
    launch(4)
    collect(1)
    pass_on(3)
    for copy in z_copies:
        copy.wait_recv()
    total = zsend[z].astype(F32)
    for k in range(NZ - 1):
        total = total + zrecv[k].astype(F32)
    xall[0] = total.astype(BF)
    x_copies = []
    for k in range(1, NS):
        copy = remote_at(xall.at[0], xall.at[k], q_x + k - 43, recv.at[q_x + k - 1], (rem(s + k, NS), o))
        start(copy)
        x_copies.append(copy)
    collect(2)
    pass_on(4)
    collect(3)
    collect(4)
    for copy in x_copies:
        copy.wait_recv()
    pick = one_hot((N, 128), lambda a, b: a == b + 32 * s)
    factor = 1.0 / math.sqrt(256.0)
    shares = [dot(xall[k], pick) for k in range(NS)]
    mine = (shares[0] + shares[2] + (shares[4] + shares[6])) * factor
    theirs = (shares[1] + shares[3] + (shares[5] + shares[7])) * factor
    for part in range(2):
        pout_ref[core, part] = mine[8 * part : 8 * part + 8, :32]
        pout_ref[other, part] = theirs[8 * part : 8 * part + 8, :32]
    for j in range(len(chunks)):
        finish(j)
    for copy in gone:
        copy.wait()
    for copy in sends.values():
        copy.wait_send()

    @pl.when(core == 1)
    def _():
        offer_copy.wait_send()


def hand_on(grad_ref, probe_ref, grad_out, probe_out, sem):
    copies = [
        pltpu.make_async_copy(grad_ref, grad_out, sem.at[0]),
        pltpu.make_async_copy(probe_ref, probe_out, sem.at[1]),
    ]
    for copy in copies:
        copy.start()
    for copy in copies:
        copy.wait()


def body(object_slices, probe, measured, positions, counts):
    vmem = pltpu.VMEM
    square = lambda *lead: (*lead, N, N)
    any_spec = pl.BlockSpec(memory_space=pl.ANY)
    given = [
        pltpu.with_memory_space_constraint(value, pltpu.HBM)
        for value in (positions[0, 0], object_slices, probe, measured[0, 0], jnp.asarray(tables()))
    ]
    results = pl.pallas_call(
        main_kernel,
        out_shape=(
            jax.ShapeDtypeStruct(square(2, 2), F32),
            jax.ShapeDtypeStruct((2, 2, 8, 32), F32),
        ),
        in_specs=[pl.BlockSpec(memory_space=pltpu.SMEM)] + [any_spec] * 5,
        out_specs=(any_spec, pl.BlockSpec(memory_space=vmem)),
        scratch_shapes=[
            pltpu.SMEM((2, 2), jnp.int32),
            vmem((1, 128), jnp.int32),
            vmem((2 * NS, 1, 128), jnp.int32),
            pltpu.SMEM((2 * NS, 1, 128), jnp.int32),
            *[vmem(square(NS, 2), F32)] * 2,
            vmem(square(2, 2), F32),
            vmem(square(2 * NX), BF),
            vmem(square(4), BF),
            *[vmem((2 * N, 2 * N), BF)] * 4,
            vmem(square(2, 2), BF),
            vmem(square(2, 2), BF),
            vmem(square(2, 2), BF),
            *[vmem(square(), BF)] * 3,
            vmem(square(2), BF),
            vmem(square(), BF),
            vmem(square(2, 2), F32),
            vmem((2 * N, 2 * N), BF),
            vmem((2 * N, 2 * N), BF),
            vmem(square(2, 2), F32),
            vmem(square(2, 2), F32),
            vmem(square(2, 2), F32),
            vmem(square(2, 2), BF),
            vmem(square(2, NS), BF),
            vmem(square(2), F32),
            vmem(square(2, 2), F32),
            vmem(square(2), BF),
            vmem(square(2), BF),
            *[vmem(square(2, 2), BF)] * 4,
            vmem(square(2, 2), BF),
            vmem(square(2), BF),
            vmem(square(2), BF),
            vmem((NY - 1, 2, N // NY, N), BF),
            vmem((NZ, 16, N), BF),
            vmem((NZ - 1, 16, N), BF),
            vmem((NS, 16, N), BF),
            pltpu.SemaphoreType.DMA((11 + 2 * NS,)),
            pltpu.SemaphoreType.DMA((56,)),
            pltpu.SemaphoreType.DMA((117,)),
        ],
        compiler_params=pltpu.CompilerParams(
            collective_id=0, has_side_effects=True, vmem_limit_bytes=44 * 1024 * 1024
        ),
        name="gradient",
    )(counts, *given)
    return pl.pallas_call(
        hand_on,
        out_shape=tuple(jax.ShapeDtypeStruct(r.shape, F32) for r in results),
        in_specs=[any_spec] * 2,
        out_specs=(any_spec, any_spec),
        scratch_shapes=[pltpu.SemaphoreType.DMA((2,))],
        compiler_params=pltpu.CompilerParams(vmem_limit_bytes=8 * 1024 * 1024),
        name="results",
    )(*results)


def solution(mesh):
    return jax.shard_map(
        body,
        mesh=mesh,
        in_specs=(
            P(None, None, "obj", None),
            P(),
            P("scan", "obj", None, None, None),
            P("scan", "obj", None, None),
            P("scan", "obj"),
        ),
        out_specs=(P(None, None, "obj", "scan"), P(None, None, "obj", "scan")),
        check_vma=False,
    )
```

```python
import functools
import math

import jax
import jax.numpy as jnp
import numpy as np
from jax import lax
from jax.experimental import pallas as pl
from jax.experimental.pallas import tpu as pltpu
from jax.sharding import PartitionSpec as P

MESH = pl.DeviceIdType.MESH
BF = jnp.bfloat16
F32 = jnp.float32
N = 256
NS, NX, NO, NY, NZ = 8, 4, 32, 4, 8


def rem(a, b):
    return lax.rem(a, jnp.int32(b))


def tables():
    index = np.arange(N)
    angle = (np.outer(index, index) % N) * (2.0 * np.pi / N)
    rounded = lambda a: a.astype(np.float32).astype(BF)
    f_re, f_im = rounded(np.cos(angle) / 16.0), rounded(-np.sin(angle) / 16.0)
    fwd = f_re.astype(np.float64) + 1j * f_im.astype(np.float64)
    freq = np.where(index < N // 2, index, index - N)
    phase = np.exp(-2j * np.pi * ((freq * freq) % (4 * N)) / (4 * N))
    prop = np.conj(fwd) @ (phase[:, None] * fwd)
    return np.stack([f_re, f_im, rounded(prop.real), rounded(prop.imag)])


def remote(src, dst, send, recv, device):
    return pltpu.make_async_remote_copy(
        src_ref=src, dst_ref=dst, send_sem=send, recv_sem=recv, device_id=device, device_id_type=MESH
    )


def main_kernel(
    count_ref, pos_hbm, tile_hbm, probe_hbm, meas_hbm, table_hbm, out_hbm, pout_ref,
    pos_ref, row, rows_in, tab, tile_0, tile_1, probe, meas, tabs, e_f, e_i, e_h, e_c, hsend, hrecv, local, offer, offered, rising, risen, pattern, win, v, u, arr, far, cur,
    gsend, wins, acc, done, tsend, trecv, bsend, brecv, csend, crecv, esend, erecv, ysend, yrecv, zsend, zrecv, xall,
    dma, send, recv,
):
    s, o = lax.axis_index("scan"), lax.axis_index("obj")
    x, core = lax.div(s, jnp.int32(2)), rem(s, 2)
    y, z = lax.div(o, jnp.int32(NZ)), rem(o, NZ)
    other = 1 - core
    partner = 2 * x + other
    right = [2 * rem(x + 1, NX) + c for c in range(2)]
    left = [2 * rem(x + 3, NX) + c for c in range(2)]
    right_me, left_me = 2 * rem(x + 1, NX) + core, 2 * rem(x + 3, NX) + core
    x_left, x_right, x_far = rem(x + 3, NX), rem(x + 1, NX), rem(x + 2, NX)
    far_at = [2 * rem(x + 2, NX) + c for c in range(2)]
    up, down = rem(o + 1, NO), rem(o + NO - 1, NO)
    tile = (tile_0, tile_1)
    sends, gone, made = {}, [], []

    def remote_at(src, dst, place, recv_sem, device):
        copy = remote(src, dst, send.at[place], recv_sem, device)
        made.append((copy, place))
        return copy

    barrier = pltpu.get_barrier_semaphore()
    peers = [(s, y * NZ + rem(z + k, NZ)) for k in (4, 3, 5, 2, 6, 1, 7)]
    peers += [(rem(s + k, NS), down) for k in (4, 5, 3, 2, 6, 1, 7, 0)] + [(s, up), (partner, up)]
    peers += [(rem(s + k, NS), o) for k in (4, 5, 3, 2, 6, 1, 7)]
    peers += [(s, rem(y + k, NY) * NZ + z) for k in (2, 1, 3)]
    for peer in peers:
        pl.semaphore_signal(barrier, inc=1, device_id=peer, device_id_type=MESH)

    given = pltpu.make_async_copy(pos_hbm, pos_ref, dma.at[4 + 2 * NS])
    given.start()
    loads = [
        pltpu.make_async_copy(table_hbm, tabs, dma.at[0]),
        pltpu.make_async_copy(probe_hbm, probe, dma.at[1]),
        pltpu.make_async_copy(meas_hbm, meas.at[pl.ds(2 * x, 2)], dma.at[2]),
    ]
    for layer in range(2):
        for b in range(NS):
            block = tile_hbm.at[layer, :, :, pl.ds(b * N, N)]
            loads.append(pltpu.make_async_copy(block, tile[layer].at[b], dma.at[3 + NS * layer + b]))
    for load in loads:
        load.start()

    lane = lax.broadcasted_iota(jnp.int32, (1, 128), 1)
    given.wait()
    line = jnp.zeros((1, 128), jnp.int32)
    for j, value in enumerate((pos_ref[0, 0], pos_ref[0, 1], pos_ref[1, 0], pos_ref[1, 1], count_ref[0, 0])):
        line = jnp.where(lane == j, value, line)
    row[...] = line
    rows_in[s] = line

    def one_hot(shape, rule):
        a, b = lax.broadcasted_iota(jnp.int32, shape, 0), lax.broadcasted_iota(jnp.int32, shape, 1)
        return jnp.where(rule(a, b), 1.0, 0.0).astype(BF)

    def dot(a, b):
        return jnp.dot(a, b, preferred_element_type=F32)

    def col_block(col):
        k = jnp.int32(0)
        for edge in range(1, NS - 1):
            k = k + jnp.where(col >= edge * N, 1, 0)
        return k

    def picks(offset):
        return [one_hot((N, N), lambda a, b: a + h * N == b + offset) for h in range(2)]

    def columns(layer, part, k, pick):
        first, second = tile[layer][k, part].astype(BF), tile[layer][k + 1, part].astype(BF)
        return (dot(first, pick[0]) + dot(second, pick[1])).astype(BF)


    pl.semaphore_wait(barrier, len(peers))

    def start(copy):
        place = next(i for c, i in made if c is copy)
        if place in sends:
            sends[place].wait_send()
        copy.start()
        sends[place] = copy

    def meas_copy(q, slot, n, peer):
        ref = meas.at[pl.ds(slot, n)]
        return remote_at(ref, ref, q, recv.at[q], (peer, o))

    def place_copy(k, base, owner):
        peer = (rem(s + k, NS), up if base else o)
        return remote_at(row, rows_in.at[base + owner], 35 + base + k, recv.at[82 + base // NS], peer)

    every = [(k, base) for base in (0, NS) for k in range(NS) if base or k]
    for k, base in every:
        start(place_copy(k, base, s))
    for q, k, peer in ((1, 0, right_me), (2, 1, left_me), (6, 1, right_me), (7, 0, left_me)):
        start(remote_at(meas_hbm.at[pl.ds(k, 1)], meas.at[pl.ds(2 * x + k, 1)], q, recv.at[q], (peer, o)))
    loads[0].wait()
    for e_ref, re, im, sign in ((e_f, 0, 1, 1), (e_i, 0, 1, -1), (e_h, 2, 3, 1), (e_c, 2, 3, -1)):
        e_ref[0:N, 0:N] = tabs[re]
        e_ref[N:, N:] = tabs[re]
        e_ref[0:N, N:] = -tabs[im] if sign > 0 else tabs[im]
        e_ref[N:, 0:N] = tabs[im] if sign > 0 else -tabs[im]

    def await_all(ref, place):
        remote_at(ref, ref, 0, recv.at[place], (partner, o)).wait_recv()

    await_all(rows_in.at[pl.ds(0, NS - 1)], 82)
    await_all(rows_in.at[pl.ds(NS, NS)], 83)
    fetch = pltpu.make_async_copy(rows_in, tab, dma.at[3 + 2 * NS])
    fetch.start()
    fetch.wait()

    def assigned(base, n):
        begin, found = jnp.int32(0), [jnp.int32(0)] * 4
        for t in range(NS):
            count = tab[base + t, 0, 4]
            for k in range(2):
                hit = (k < count) & (begin + k == n)
                values = (jnp.int32(t % 2), jnp.int32(2 * (t // 2) + k), tab[base + t, 0, 2 * k], tab[base + t, 0, 2 * k + 1])
                for j, value in enumerate(values):
                    found[j] = jnp.where(hit, value, found[j])
            begin = begin + count
        return found

    _, _, _, col_out = assigned(NS * other, x + NX * core)
    k_out = col_block(col_out)
    pick_out = picks(col_out - k_out * N)
    halo_to = jnp.where(core == 0, down, up)

    def halo_copy(layer, part):
        q = 2 * layer + part
        return remote_at(hsend.at[layer, part], hrecv.at[layer, part], 51 + q, recv.at[86 + q], (s, halo_to))

    for layer in range(2):
        for b in range(NS):
            loads[3 + NS * layer + b].wait()
        for part in range(2):
            hsend[layer, part] = columns(layer, part, k_out, pick_out)
            start(halo_copy(layer, part))
    meas_copy(1, 2 * x_left, 1, right_me).wait_recv()
    start(meas_copy(3, 2 * x_left, 1, right_me))
    meas_copy(2, 2 * x_right + 1, 1, left_me).wait_recv()
    start(meas_copy(5, 2 * x_right + 1, 1, left_me))
    half_mine, slot_mine, row0, col0 = assigned(NS * core, x + NX * core)
    k_own = col_block(col0)
    pick_own = picks(col0 - k_own * N)
    for layer in range(2):
        for part in range(2):
            local[layer, part] = columns(layer, part, k_own, pick_own)
    places = [assigned(NS * (d % 2), d // 2 + NX * (d % 2))[2:] for d in range(NS)]
    _, slot_a, _, _ = assigned(0, x)
    _, slot_b, _, _ = assigned(0, x + NX)
    rows_own = one_hot((N, N), lambda a, b: b + N * core == a + row0)
    rows_halo = one_hot((N, N), lambda a, b: b + N * other == a + row0)
    turn = jnp.where(col0 == 7 * N, 0, col0 - k_own * N)
    turn_rows = one_hot((N, N), lambda a, b: (b + row0 == a) | (b + row0 == a + N))
    turn_cols = one_hot((N, N), lambda a, b: (a + turn == b) | (a + turn == b + N))
    loads[1].wait()

    def window(layer):
        for part in range(2):
            halo_copy(layer, part).wait_recv()
            win[layer, part] = dot(rows_own, local[layer, part]) + dot(rows_halo, hrecv[layer, part])

    step = 32

    def by_rows(body):
        def run(i, carry):
            body(pl.ds(pl.multiple_of(i * step, step), step), i)
            return carry

        lax.fori_loop(0, N // step, run, 0)

    def put(m, rows, i, re, im):
        v[pl.ds(pl.multiple_of(i * step, step), step), m * N : (m + 1) * N] = re.astype(BF)
        v[pl.ds(pl.multiple_of(N + i * step, step), step), m * N : (m + 1) * N] = im.astype(BF)

    def left_mul(matrix):
        for m in range(2):
            product = dot(matrix[...], v[:, m * N : (m + 1) * N])
            u[m * N : (m + 1) * N, 0:N] = product[0:N].astype(BF)
            u[m * N : (m + 1) * N, N:] = product[N:].astype(BF)

    def right_mul(matrix, result):
        for part in range(2):
            product = dot(u[...], matrix[:, part * N : (part + 1) * N])
            result[0, part] = product[0:N]
            result[1, part] = product[N:]

    for q, slot, peer in ((3, 2 * x_far, right_me), (5, 2 * x_far + 1, left_me), (6, 2 * x_left + 1, right_me), (7, 2 * x_right, left_me)):
        meas_copy(q, slot, 1, peer).wait_recv()
    loads[2].wait()
    rising[...] = meas[slot_b]
    start(remote_at(rising, risen.at[core], 55, recv.at[84 + core], (2 * x + 1, up)))
    offer[...] = meas[slot_a]
    offer_copy = remote_at(offer, offered, 0, recv.at[0], (2 * x, o))

    @pl.when(core == 1)
    def _():
        offer_copy.start()

    window(0)

    def enter(rows, i):
        re, im = win[0, 0, rows, :], win[0, 1, rows, :]
        for m in range(2):
            pr, pi = probe[m, 0, rows, :], probe[m, 1, rows, :]
            put(m, rows, i, pr * re - pi * im, pr * im + pi * re)

    by_rows(enter)
    left_mul(e_h)
    right_mul(e_c, arr)
    window(1)

    def second(rows, i):
        re, im = win[1, 0, rows, :], win[1, 1, rows, :]
        for m in range(2):
            pr, pi = arr[m, 0, rows, :], arr[m, 1, rows, :]
            put(m, rows, i, pr * re - pi * im, pr * im + pi * re)

    by_rows(second)
    left_mul(e_f)
    right_mul(e_i, far)

    @pl.when(core == 0)
    def _():
        offer_copy.wait_recv()
        pattern[...] = jnp.where(half_mine == 0, offer[...], offered[...])

    @pl.when(core == 1)
    def _():
        for c in range(2):
            remote_at(rising, risen.at[c], 55, recv.at[84 + c], (s, up)).wait_recv()
        pattern[...] = jnp.where(half_mine == 0, risen[0], risen[1])

    def misfit(rows, i):
        parts = [(far[m, 0, rows, :], far[m, 1, rows, :]) for m in range(2)]
        total = parts[0][0] ** 2 + parts[0][1] ** 2 + (parts[1][0] ** 2 + parts[1][1] ** 2)
        gap = total - pattern[rows, :].astype(F32)
        for m in range(2):
            put(m, rows, i, gap * parts[m][0], gap * parts[m][1])

    by_rows(misfit)
    left_mul(e_i)
    right_mul(e_f, cur)

    chunks = [(1, 0, 128), (1, 128, 128), (0, 0, 128), (0, 128, 64), (0, 192, 64)]

    def span(j, part=None):
        _, first, size = chunks[j]
        return pl.ds(first, size) if part is None else pl.ds(first + part * size // 2, size // 2)

    def near(j, c, side):
        layer, q, sq = chunks[j][0], 8 + 14 * j + (1 if side else 3), 8 + 14 * (j % 2) + (1 if side else 3)
        peer = (right if side else left)[c]
        return remote_at(
            gsend.at[layer, c, span(j)], wins.at[layer, s, span(j)], sq + c, recv.at[q + core], (peer, o)
        )

    def near_in(j, c, side):
        layer, q, sq = chunks[j][0], 8 + 14 * j + (1 if side else 3), 8 + 14 * (j % 2) + (1 if side else 3)
        slot = wins.at[layer, (left if side else right)[c], span(j)]
        return remote_at(slot, slot, sq + c, recv.at[q + c], (partner, o))

    def relay(j, c, side, incoming=False):
        q, sq = 8 + 14 * j + (5 if side else 7) + c, 8 + 14 * (j % 2) + (5 if side else 7) + c
        owner = far_at[c] if incoming else (left if side else right)[c]
        piece = wins.at[chunks[j][0], owner, span(j, 0 if side else 1)]
        return remote_at(piece, piece, sq, recv.at[q], (right_me if side else left_me, o))

    def pair(j, incoming=False):
        layer, q, sq = chunks[j][0], 8 + 14 * j, 8 + 14 * (j % 2)
        slot = wins.at[layer, partner if incoming else s, span(j)]
        return remote_at(gsend.at[layer, other, span(j)], slot, sq, recv.at[q], (partner, o))

    def share(layer, first, adjoint, ready=None):
        for part in range(2):
            if part == 0:
                term = lambda m: first[m, 0] * adjoint[m, 0] + first[m, 1] * adjoint[m, 1]
            else:
                term = lambda m: first[m, 0] * adjoint[m, 1] - first[m, 1] * adjoint[m, 0]
            grad = (term(0) + term(1)).astype(BF)
            gsend[layer, part] = dot(dot(turn_rows, grad).astype(BF), turn_cols).astype(BF)
            if ready is not None:
                start(near(ready, part, 1))
                start(near(ready, part, 0))
        wins[layer, s] = gsend[layer, core]

    def launch(j):
        for c in range(2):
            start(near(j, c, 1))
            start(near(j, c, 0))
        start(pair(j))

    def pass_on(j):
        for c in range(2):
            for side in (1, 0):
                near_in(j, c, side).wait_recv()
                start(relay(j, c, side))

    lane = lax.broadcasted_iota(jnp.int32, (1, N), 1)
    cols = [
        [jnp.where((lane + (2 * x + b) * N >= c0) & (lane + (2 * x + b) * N < c0 + N), 1.0, 0.0) for b in range(2)]
        for _, c0 in places
    ]

    def gather(j):
        layer, first, size = chunks[j]
        chunk = 16

        def run(i, carry):
            at = pl.multiple_of(first + i * chunk, chunk)
            rows = pl.ds(at, chunk)
            line = lax.broadcasted_iota(jnp.int32, (chunk, N), 0) + at
            sums = [[jnp.zeros((chunk, N), F32) for _ in range(3)] for _ in range(2)]
            for n in range(NS):
                term = wins[layer, n, rows, :].astype(F32)
                above = line >= places[n][0]
                for b in range(2):
                    masked = term * cols[n][b]
                    low, high = (2, 0) if n % 2 else (0, 1)
                    sums[b][low] = sums[b][low] + jnp.where(above, masked, 0.0)
                    sums[b][high] = sums[b][high] + jnp.where(above, 0.0, masked)
            mine = core == 0
            acc[layer, rows, :] = jnp.where(mine, sums[0][0], sums[1][0])
            tsend[layer, rows, :] = jnp.where(mine, sums[1][0], sums[0][0]).astype(BF)
            for b in range(2):
                bsend[layer, b, rows, :] = sums[b][1].astype(BF)
                csend[layer, b, rows, :] = sums[b][2].astype(BF)
            return carry

        lax.fori_loop(0, size // chunk, run, 0)

    def top_copy(j):
        layer, q, sq = chunks[j][0], 17 + 14 * j, 17 + 14 * (j % 2)
        return remote_at(tsend.at[layer, span(j)], trecv.at[layer, span(j)], sq, recv.at[q], (partner, o))

    def edge(j, upward):
        more = 18 + (0 if upward else 2)
        q, sq = more + 14 * j, more + 14 * (j % 2)
        return (bsend, brecv, q, sq, up) if upward else (csend, crecv, q, sq, down)

    def edge_copy(j, b, upward):
        layer, (source, target, q, sq, to) = chunks[j][0], edge(j, upward)
        return remote_at(
            source.at[layer, b, span(j)], target.at[layer, core, span(j)], sq + b, recv.at[q + core], (2 * x + b, to)
        )

    def edge_in(j, c, upward):
        layer, (source, target, q, sq, to) = chunks[j][0], edge(j, upward)
        return remote_at(source.at[layer, c, span(j)], target.at[layer, c, span(j)], sq + c, recv.at[q + c], (s, to))

    def collect(j):
        pair(j, True).wait_recv()
        for c in range(2):
            for side in (1, 0):
                relay(j, c, side, True).wait_recv()
        gather(j)
        for b in range(2):
            start(edge_copy(j, b, True))
            start(edge_copy(j, b, False))
        start(top_copy(j))

    def finish(j):
        layer = chunks[j][0]
        top_copy(j).wait_recv()
        for c in range(2):
            edge_in(j, c, True).wait_recv()
            edge_in(j, c, False).wait_recv()
        for i in range(2):
            rows = span(j, i)
            rims = [brecv[layer, c, rows, :].astype(F32) + crecv[layer, c, rows, :].astype(F32) for c in (core, other)]
            done[layer, core, rows, :] = acc[layer, rows, :] + rims[0]
            done[layer, other, rows, :] = trecv[layer, rows, :].astype(F32) + rims[1]
        leaving = pltpu.make_async_copy(
            done.at[layer, :, span(j)], out_hbm.at[layer, :, span(j)], dma.at[6 + 2 * NS + j]
        )
        leaving.start()
        gone.append(leaving)

    share(1, arr, cur, ready=0)
    start(pair(0))
    launch(1)

    def behind(rows, i):
        re, im = win[1, 0, rows, :], win[1, 1, rows, :]
        for m in range(2):
            cr, ci = cur[m, 0, rows, :], cur[m, 1, rows, :]
            put(m, rows, i, re * cr + im * ci, re * ci - im * cr)

    by_rows(behind)
    left_mul(e_c)
    right_mul(e_h, cur)

    def leave(rows, i):
        re, im = win[0, 0, rows, :], win[0, 1, rows, :]
        for m in range(2):
            cr, ci = cur[m, 0, rows, :], cur[m, 1, rows, :]
            esend[m, 0, rows, :] = (re * cr + im * ci).astype(BF)
            esend[m, 1, rows, :] = (re * ci - im * cr).astype(BF)

    by_rows(leave)
    q_pair, q_y, q_z, q_x = 78, 79, 82, 89
    e_copy = remote_at(esend.at[other], erecv, q_pair - 42, recv.at[q_pair], (partner, o))
    start(e_copy)
    share(0, probe, cur)
    e_copy.wait_recv()

    def add_pair(rows, i):
        for part in range(2):
            ysend[part, rows, :] = (esend[core, part, rows, :].astype(F32) + erecv[part, rows, :].astype(F32)).astype(BF)

    by_rows(add_pair)
    deep = N // NY
    for k in range(1, NY):
        y_to = rem(y + k, NY)
        rows_to = pl.ds(pl.multiple_of(y_to * deep, deep), deep)
        copy = remote_at(
            ysend.at[:, rows_to, :], yrecv.at[k - 1], q_y + k - 43, recv.at[79], (s, y_to * NZ + z)
        )
        start(copy)
    pass_on(0)
    launch(2)
    pass_on(1)
    launch(3)
    await_all(yrecv, 79)
    rows_me = pl.ds(pl.multiple_of(y * deep, deep), deep)
    totals = []
    for part in range(2):
        total = ysend[part, rows_me, :].astype(F32)
        for k in range(NY - 1):
            total = total + yrecv[k, part].astype(F32)
        totals.append(total)
    for k in range(NZ):
        zsend[k] = jnp.concatenate([total[8 * k : 8 * k + 8] for total in totals], axis=0).astype(BF)
    for k in range(1, NZ):
        z_to = rem(z + k, NZ)
        copy = remote_at(
            zsend.at[z_to], zrecv.at[k - 1], q_z + k - 43, recv.at[80], (s, y * NZ + z_to)
        )
        start(copy)
    collect(0)
    pass_on(2)
    launch(4)
    collect(1)
    pass_on(3)
    await_all(zrecv, 80)
    total = zsend[z].astype(F32)
    for k in range(NZ - 1):
        total = total + zrecv[k].astype(F32)
    xall[0] = total.astype(BF)
    for k in range(1, NS):
        copy = remote_at(xall.at[0], xall.at[k], q_x + k - 43, recv.at[81], (rem(s + k, NS), o))
        start(copy)
    collect(2)
    pass_on(4)
    collect(3)
    collect(4)
    await_all(xall.at[pl.ds(1, NS - 1)], 81)
    pick = one_hot((N, 128), lambda a, b: a == b + 32 * s)
    factor = 1.0 / math.sqrt(256.0)
    shares = [dot(xall[k], pick) for k in range(NS)]
    mine = (shares[0] + shares[2] + (shares[4] + shares[6])) * factor
    theirs = (shares[1] + shares[3] + (shares[5] + shares[7])) * factor
    for part in range(2):
        pout_ref[core, part] = mine[8 * part : 8 * part + 8, :32]
        pout_ref[other, part] = theirs[8 * part : 8 * part + 8, :32]
    for j in range(len(chunks)):
        finish(j)
    for copy in gone:
        copy.wait()
    for copy in sends.values():
        copy.wait_send()

    @pl.when(core == 1)
    def _():
        offer_copy.wait_send()


def hand_on(grad_ref, probe_ref, grad_out, probe_out, sem):
    copies = [
        pltpu.make_async_copy(grad_ref, grad_out, sem.at[0]),
        pltpu.make_async_copy(probe_ref, probe_out, sem.at[1]),
    ]
    for copy in copies:
        copy.start()
    for copy in copies:
        copy.wait()


def body(object_slices, probe, measured, positions, counts):
    vmem = pltpu.VMEM
    square = lambda *lead: (*lead, N, N)
    any_spec = pl.BlockSpec(memory_space=pl.ANY)
    given = [
        pltpu.with_memory_space_constraint(value, pltpu.HBM)
        for value in (positions[0, 0], object_slices, probe, measured[0, 0], jnp.asarray(tables()))
    ]
    results = pl.pallas_call(
        main_kernel,
        out_shape=(
            jax.ShapeDtypeStruct(square(2, 2), F32),
            jax.ShapeDtypeStruct((2, 2, 8, 32), F32),
        ),
        in_specs=[pl.BlockSpec(memory_space=pltpu.SMEM)] + [any_spec] * 5,
        out_specs=(any_spec, pl.BlockSpec(memory_space=vmem)),
        scratch_shapes=[
            pltpu.SMEM((2, 2), jnp.int32),
            vmem((1, 128), jnp.int32),
            vmem((2 * NS, 1, 128), jnp.int32),
            pltpu.SMEM((2 * NS, 1, 128), jnp.int32),
            *[vmem(square(NS, 2), F32)] * 2,
            vmem(square(2, 2), F32),
            vmem(square(2 * NX), BF),
            vmem(square(4), BF),
            *[vmem((2 * N, 2 * N), BF)] * 4,
            vmem(square(2, 2), BF),
            vmem(square(2, 2), BF),
            vmem(square(2, 2), BF),
            *[vmem(square(), BF)] * 3,
            vmem(square(2), BF),
            vmem(square(), BF),
            vmem(square(2, 2), F32),
            vmem((2 * N, 2 * N), BF),
            vmem((2 * N, 2 * N), BF),
            vmem(square(2, 2), F32),
            vmem(square(2, 2), F32),
            vmem(square(2, 2), F32),
            vmem(square(2, 2), BF),
            vmem(square(2, NS), BF),
            vmem(square(2), F32),
            vmem(square(2, 2), F32),
            vmem(square(2), BF),
            vmem(square(2), BF),
            *[vmem(square(2, 2), BF)] * 4,
            vmem(square(2, 2), BF),
            vmem(square(2), BF),
            vmem(square(2), BF),
            vmem((NY - 1, 2, N // NY, N), BF),
            vmem((NZ, 16, N), BF),
            vmem((NZ - 1, 16, N), BF),
            vmem((NS, 16, N), BF),
            pltpu.SemaphoreType.DMA((11 + 2 * NS,)),
            pltpu.SemaphoreType.DMA((56,)),
            pltpu.SemaphoreType.DMA((90,)),
        ],
        compiler_params=pltpu.CompilerParams(
            collective_id=0, has_side_effects=True, vmem_limit_bytes=44 * 1024 * 1024
        ),
        name="gradient",
    )(counts, *given)
    return pl.pallas_call(
        hand_on,
        out_shape=tuple(jax.ShapeDtypeStruct(r.shape, F32) for r in results),
        in_specs=[any_spec] * 2,
        out_specs=(any_spec, any_spec),
        scratch_shapes=[pltpu.SemaphoreType.DMA((2,))],
        compiler_params=pltpu.CompilerParams(vmem_limit_bytes=8 * 1024 * 1024),
        name="results",
    )(*results)


def solution(mesh):
    return jax.shard_map(
        body,
        mesh=mesh,
        in_specs=(
            P(None, None, "obj", None),
            P(),
            P("scan", "obj", None, None, None),
            P("scan", "obj", None, None),
            P("scan", "obj"),
        ),
        out_specs=(P(None, None, "obj", "scan"), P(None, None, "obj", "scan")),
        check_vma=False,
    )
```
